32 devices in a mesh: src: 4 (over y, x), rec: 4 (over z), freq: 2 (over core).
Axes of the slice: x: 2, y: 2, z: 4, core: 2. Of those that a mesh axis runs over, the one named last changes fastest.
Arguments:
- wave: bfloat16 [2, 4, 256, 2048], P(None, 'freq', 'src', 'rec'), may hold values from -6 to 6
- tap_table: float32 [2, 64, 4, 33], P(None, None, 'freq'), may hold values from -0.75 to 0.75
- src_index: int32 [3, 256], P(None, 'src'), may hold values from 0 to 63
- rec_index: int32 [3, 2048], P(None, 'rec'), may hold values from 0 to 63
- offset_bin: int32 [256, 2048], P('src', 'rec'), may hold values from 0 to 63
- bin_weight: float32 [3, 64], replicated, may hold values from 0.5 to 2
Outputs:
- final_wave: bfloat16 [2, 4, 256, 2048], P(None, 'freq', 'src', 'rec')
- image: float32 [256, 2048], P(('src', 'freq'), 'rec')
The draws below stay inside these ranges and needn't reach their ends.
All inputs are finite; a program needn't handle non-finite values.
Results may differ from the reference program's by a relative error of at most 0.012.
Values may be sent and summed in bfloat16 or wider, within the bound.
No kernel may reach another device: no remote copies, remote signals or barrier semaphores. Data moves between devices by JAX's collectives and lax.ppermute only.
A program may use at most 64 MiB of HBM per device.

```python
import math
import jax
import jax.numpy as jnp
from jax import lax

S_DEV = 64
R_DEV = 512
F_DEV = 2
TAPS = 33
NTAB = 64
NBIN = 64
DEPTHS = 3
NS = 256
NR = 2048
NF = 4
N_FREQ = 2


def place_ends(drawn, rng, low, largest):
    place = [jax.random.randint(jax.random.fold_in(rng, axis), (), 0, length) for axis, length in enumerate(drawn.shape)]
    main_axis = drawn.shape.index(max(drawn.shape))
    beside = place[:main_axis] + [(place[main_axis] + 1) % drawn.shape[main_axis]] + place[main_axis + 1:]
    return drawn.at[tuple(place)].set(low).at[tuple(beside)].set(largest)


def steps_of(own_key, dims, shards, least, top_value):
    loudness, own = 1.0, jax.random.fold_in(own_key, 6)
    for dim, shards_of in shards:
        steps = jnp.exp(jax.random.uniform(jax.random.fold_in(own, dim), (shards_of,), jnp.float32, least / len(shards), top_value / len(shards)))
        loudness = loudness * jnp.repeat(steps, dims[dim] // shards_of).reshape([-1 if axis == dim else 1 for axis in range(len(dims))])
    return loudness


def gaussian(key, extent, spread, limit, shards=(), kind=jnp.bfloat16):
    level = steps_of(key, extent, shards, -0.22, 0.18) if shards else 1.0
    entries = jax.random.normal(key, extent, jnp.float32) * spread * level
    return jnp.minimum(jnp.maximum(entries, -limit), limit).astype(kind)


def setup_inputs(seed: int = 0) -> dict:
    streams_of = jax.random.split(jax.random.key(seed), 7)
    return {
        "wave": gaussian(streams_of[0], (2, NF, NS, NR), 1.0, 6.0, ((1, 2), (2, 4), (3, 4))),
        "tap_table": gaussian(streams_of[1], (2, NTAB, NF, TAPS), (2 * TAPS) ** -0.5, 0.75, ((2, 2),), jnp.float32),
        "src_index": place_ends(jax.random.randint(streams_of[2], (DEPTHS, NS), 0, NTAB), jax.random.fold_in(streams_of[2], 1), 0, NTAB - 1).astype(jnp.int32),
        "rec_index": place_ends(jax.random.randint(streams_of[3], (DEPTHS, NR), 0, NTAB), jax.random.fold_in(streams_of[3], 1), 0, NTAB - 1).astype(jnp.int32),
        "offset_bin": place_ends(jax.random.randint(streams_of[4], (NS, NR), 0, NBIN), jax.random.fold_in(streams_of[4], 1), 0, NBIN - 1).astype(jnp.int32),
        "bin_weight": jnp.clip(jnp.exp(jax.random.uniform(streams_of[5], (DEPTHS, NBIN), jnp.float32, math.log(0.5), math.log(2.0))), 0.5, 2.0),
    }


def banded(tap_rows, block_size):
    leading = tap_rows.shape[:-2]
    tap_count = tap_rows.shape[-1]
    block_count = tap_rows.shape[-2] // block_size
    grouped = tap_rows.reshape(leading + (block_count, block_size, tap_count))
    padded = jnp.pad(grouped, [(0, 0)] * (len(leading) + 2) + [(0, block_size)])
    flattened = padded.reshape(leading + (block_count, block_size * (tap_count + block_size)))
    flattened = flattened[..., :block_size * (block_size + tap_count - 1)]
    return flattened.reshape(leading + (block_count, block_size, block_size + tap_count - 1))

def operator_pair(tap_rows, block_size):
    matrices = banded(tap_rows, block_size)
    real_part = jnp.concatenate([matrices[0], -matrices[1]], axis=-1)
    imag_part = jnp.concatenate([matrices[1], matrices[0]], axis=-1)
    return (real_part, imag_part)

def receiver_pass(padded, operators, block_size):
    block_count = operators[0].shape[1]
    extra = (block_count + 1) * block_size - padded.shape[3]
    widened = jnp.pad(padded, ((0, 0), (0, 0), (0, 0), (0, extra)))
    grouped = widened.reshape(padded.shape[:3] + (block_count + 1, block_size))
    windows = jnp.concatenate([grouped[..., :block_count, :], grouped[..., 1:, :TAPS - 1]], axis=-1)
    stacked = jnp.concatenate([windows[0], windows[1]], axis=-1).astype(jnp.float32)
    real_out = jnp.einsum('fsnj,fncj->fsnc', stacked, operators[0].astype(jnp.float32), precision=lax.Precision.HIGHEST)
    imag_out = jnp.einsum('fsnj,fncj->fsnc', stacked, operators[1].astype(jnp.float32), precision=lax.Precision.HIGHEST)
    result = jnp.stack([real_out, imag_out]).reshape(padded.shape[:3] + (block_count * block_size,))
    return result.astype(jnp.bfloat16)

def source_pass(padded, operators, block_size):
    block_count = operators[0].shape[1]
    extra = (block_count + 1) * block_size - padded.shape[2]
    widened = jnp.pad(padded, ((0, 0), (0, 0), (0, extra), (0, 0)))
    grouped = widened.reshape(padded.shape[:2] + (block_count + 1, block_size, padded.shape[3]))
    windows = jnp.concatenate([grouped[:, :, :block_count], grouped[:, :, 1:, :TAPS - 1]], axis=3)
    stacked = jnp.concatenate([windows[0], windows[1]], axis=2).astype(jnp.float32)
    real_out = jnp.einsum('fnjr,fncj->fncr', stacked, operators[0].astype(jnp.float32), precision=lax.Precision.HIGHEST)
    imag_out = jnp.einsum('fnjr,fncj->fncr', stacked, operators[1].astype(jnp.float32), precision=lax.Precision.HIGHEST)
    result = jnp.stack([real_out, imag_out]).reshape(padded.shape[:2] + (block_count * block_size, padded.shape[3]))
    return result.astype(jnp.bfloat16)

def reference(wave, tap_table, src_index, rec_index, offset_bin, bin_weight):
    half_taps = TAPS // 2
    block_rec = min(128, R_DEV)
    block_src = min(128, S_DEV)
    table_bf = tap_table.astype(jnp.bfloat16)
    pair_weight = bin_weight[:, offset_bin]

    def one_frequency(inputs):
        wavefield, table_one = inputs
        image_part = jnp.zeros((NS, NR), jnp.float32)
        for depth_step in range(DEPTHS):
            rec_taps = jnp.moveaxis(table_one[:, rec_index[depth_step]], 1, 2)
            src_taps = jnp.moveaxis(table_one[:, src_index[depth_step]], 1, 2)
            padded = jnp.pad(wavefield, ((0, 0), (0, 0), (0, 0), (half_taps, half_taps)))
            swept = receiver_pass(padded, operator_pair(rec_taps, block_rec), block_rec)
            padded = jnp.pad(swept, ((0, 0), (0, 0), (half_taps, half_taps), (0, 0)))
            wavefield = source_pass(padded, operator_pair(src_taps, block_src), block_src)
            image_part = image_part + pair_weight[depth_step] * wavefield[0, 0].astype(jnp.float32)
        return (wavefield, image_part)
    per_wave = jnp.moveaxis(wave, 1, 0)[:, :, None]
    per_table = jnp.moveaxis(table_bf, 2, 0)[:, :, :, None]
    waves_out, images = lax.map(one_frequency, (per_wave, per_table))
    partial_value = lax.optimization_barrier(jnp.sum(images.reshape((N_FREQ, F_DEV, NS, NR)), axis=1)).astype(jnp.bfloat16)
    total = lax.optimization_barrier(jnp.sum(partial_value.astype(jnp.float32), axis=0))
    image = total * (1.0 / math.sqrt(NF * DEPTHS))
    final_wave = jnp.moveaxis(waves_out[:, :, 0], 0, 1)
    return (final_wave, image)
```

```python
import functools
import math

import jax
import jax.numpy as jnp
from jax import lax
from jax.experimental import pallas as pl
from jax.experimental.pallas import tpu as pltpu
from jax.sharding import PartitionSpec as P

TAPS = 33
DEPTHS = 3
HALF = TAPS // 2
HALO = DEPTHS * HALF
LANES = 128
SPAN = 2 * LANES
IDX_ROWS = 16
BF = jnp.bfloat16
F32 = jnp.float32


def pairs_of(axis, odd):
    count, groups = lax.axis_size(axis), lax.axis_size("freq")
    pairs, alone = [], list(range(count))
    for i in range(odd, count - 1, 2):
        alone.remove(i)
        alone.remove(i + 1)
        for g in range(groups):
            pairs += [(i * groups + g, (i + 1) * groups + g), ((i + 1) * groups + g, i * groups + g)]
    for i in alone:
        for g in range(0, groups - 1, 2):
            pairs += [(i * groups + g, i * groups + g + 1), (i * groups + g + 1, i * groups + g)]
    return pairs


def swap(cells, axis, odd):
    return lax.ppermute(cells, (axis, "freq"), pairs_of(axis, odd))


def parity(axis):
    return lax.rem(lax.axis_index(axis), 2)


def has_left(axis):
    return lax.axis_index(axis) > 0


def has_right(axis):
    return lax.axis_index(axis) < lax.axis_size(axis) - 1


def lane_of(shape):
    return lax.broadcasted_iota(jnp.int32, shape, len(shape) - 1)


def shifted(cells, amount):
    amount = amount % LANES
    return pltpu.roll(cells, amount, 1) if amount else cells


def left_right(a_ref, b_ref, axis):
    even = parity(axis) == 0
    a, b = a_ref[...], b_ref[...]
    return jnp.where(even, b, a), jnp.where(even, a, b)


def pack_kernel(x_ref, ridx_ref, sa_ref, sb_ref, ra_ref, rb_ref):
    planes, rows, cols = x_ref.shape
    even = parity("src") == 0
    low = rows - HALO
    at = pl.multiple_of(jnp.where(even, low, 0), 16)
    other = pl.multiple_of(jnp.where(even, 0, low), 16)
    for p in range(planes):
        sa_ref[p * HALO:(p + 1) * HALO, :] = x_ref[p, pl.ds(at, HALO), :]
        sb_ref[p * HALO:(p + 1) * HALO, :] = x_ref[p, pl.ds(other, HALO), :]
    even = parity("rec") == 0
    tail_at = cols - LANES
    for p in range(planes):
        head, tail = x_ref[p, :, 0:LANES], x_ref[p, :, tail_at:cols]
        ra_ref[p * rows:(p + 1) * rows, :] = jnp.where(even, tail, head)
        rb_ref[p * rows:(p + 1) * rows, :] = jnp.where(even, head, tail)
    base = planes * rows
    head = ridx_ref[:, 0:LANES].astype(F32).astype(BF)
    tail = ridx_ref[:, tail_at:cols].astype(F32).astype(BF)
    for ref in (ra_ref, rb_ref):
        ref[base:base + IDX_ROWS, :] = jnp.zeros((IDX_ROWS, LANES), BF)
    ra_ref[base:base + DEPTHS, :] = jnp.where(even, tail, head)
    rb_ref[base:base + DEPTHS, :] = jnp.where(even, head, tail)


def corner_kernel(rows, ra_ref, rb_ref, sidx_ref, ca_ref, cb_ref, edge_ref):
    left, right = left_right(ra_ref, rb_ref, "rec")
    total = (left.shape[0] - IDX_ROWS)
    planes = total // rows
    lane = lane_of((total, LANES))
    left = shifted(left[:total].astype(F32), HALO)
    right = shifted(right[:total].astype(F32), HALO)
    in_left = (lane < HALO) & has_left("rec")
    in_right = (lane >= HALO) & (lane < 2 * HALO) & has_right("rec")
    edge_ref[...] = jnp.where(in_left, left, jnp.where(in_right, right, 0.0)).astype(BF)
    even = parity("src") == 0
    low = rows - HALO
    at = jnp.where(even, low, 0)
    other = jnp.where(even, 0, low)
    for p in range(planes):
        ca_ref[p * HALO:(p + 1) * HALO, :] = edge_ref[pl.ds(pl.multiple_of(p * rows + at, 16), HALO), :]
        cb_ref[p * HALO:(p + 1) * HALO, :] = edge_ref[pl.ds(pl.multiple_of(p * rows + other, 16), HALO), :]
    base = planes * HALO
    idx = sidx_ref[...].astype(F32).astype(BF)
    for ref in (ca_ref, cb_ref):
        ref[base:base + IDX_ROWS, :] = jnp.zeros((IDX_ROWS, LANES), BF)
        ref[base:base + DEPTHS, 0:rows] = idx


def wide_tiles(own, left, right, amount, fill):
    count = len(own)
    lane = lane_of(own[0].shape)
    moved = [shifted(t, amount) for t in own]
    if amount == 0:
        return moved
    tiles = [jnp.where(lane < amount, shifted(left, amount), moved[0])]
    for t in range(1, count):
        tiles.append(jnp.where(lane < amount, moved[t - 1], moved[t]))
    last = jnp.where(lane < 2 * amount, shifted(right, amount), fill)
    tiles.append(jnp.where(lane < amount, moved[count - 1], last))
    return tiles


def bands(idx_row, table, entries):
    onehot = (lax.broadcasted_iota(jnp.int32, (entries, LANES), 0) == idx_row).astype(F32).astype(BF)
    taps = lax.dot_general(onehot, table, (((0,), (0,)), ((), ())), preferred_element_type=F32)
    out = lax.broadcasted_iota(jnp.int32, (LANES, LANES), 0)
    lane = lane_of((LANES, LANES))
    found = []
    for part in range(taps.shape[1] // LANES):
        skewed = pltpu.roll(taps[:, part * LANES:(part + 1) * LANES], 0, 1, stride=1, stride_axis=0)
        first = jnp.where(lane >= out, skewed, 0.0).astype(BF)
        second = jnp.where(lane < out, skewed, 0.0).astype(BF)
        found.append((first, second))
    return found


NT = (((1,), (1,)), ((), ()))
NN = (((1,), (0,)), ((), ()))


def dot(a, b, dims=NN):
    return lax.dot_general(a, b, dims, preferred_element_type=F32)


def step_blocks(cols, z):
    return -(-(cols + 2 * HALF * (DEPTHS - 1 - z)) // LANES)


def receiver_steps(x_ref, outs, w_ref, freqs, cols):
    block = 0
    source = x_ref
    for z in range(DEPTHS):
        for b in range(step_blocks(cols, z)):
            window = pl.ds(b * LANES, SPAN)
            for f in range(freqs):
                got = dot(source[f, :, window], w_ref[block, f, 0], NT)
                got += dot(source[freqs + f, :, window], w_ref[block, f, 1], NT)
                outs(z, f, b, got[:, :LANES].astype(BF))
                outs(z, freqs + f, b, got[:, LANES:].astype(BF))
            block += 1
        source = outs.source(z)


class Store:
    def __init__(self, refs, places):
        self.refs, self.places = refs, places

    def __call__(self, z, plane, b, value):
        for at, start, size in self.places:
            self.refs[z][plane, at:at + size, b * LANES:(b + 1) * LANES] = value[start:start + size]

    def source(self, z):
        return self.refs[z]


def own_kernel(
    x_ref, edge_ref, ra_ref, rb_ref, ridx_ref, table_ref, bins_ref, weight_ref,
    w_ref, a0_ref, a1_ref, a2_ref, pair_ref, wide_ref, widx_ref, wt_ref,
):
    planes, rows, cols = x_ref.shape
    freqs = planes // 2
    tiles = cols // LANES
    entries = table_ref.shape[0]
    wt_ref[...] = jnp.zeros(wt_ref.shape, F32)
    wt_ref[0:DEPTHS, 0:weight_ref.shape[1]] = weight_ref[...]
    for t in range(tiles):
        bins = bins_ref[:, t * LANES:(t + 1) * LANES]
        for z in range(DEPTHS):
            row = jnp.broadcast_to(wt_ref[z:z + 1, :], (rows, LANES))
            pair_ref[z, :, t * LANES:(t + 1) * LANES] = jnp.take_along_axis(row, bins, axis=1)
    lane = lane_of((rows, LANES))
    for p in range(planes):
        edge = edge_ref[p * rows:(p + 1) * rows, :].astype(F32)
        own = [x_ref[p, :, t * LANES:(t + 1) * LANES].astype(F32) for t in range(tiles)]
        moved = [shifted(o, HALO) for o in own]
        before = [edge] + moved
        after = moved + [edge]
        for t in range(tiles + 1):
            wide_ref[p, :, t * LANES:(t + 1) * LANES] = jnp.where(lane < HALO, before[t], after[t]).astype(BF)
        wide_ref[p, :, (tiles + 1) * LANES:] = jnp.zeros((rows, LANES), BF)
    base = planes * rows
    even = parity("rec") == 0
    got_a, got_b = ra_ref[base:base + IDX_ROWS, :], rb_ref[base:base + IDX_ROWS, :]
    left = jnp.where(even, got_b, got_a).astype(F32)[0:8]
    right = jnp.where(even, got_a, got_b).astype(F32)[0:8]
    left = jnp.where(has_left("rec"), left, -1.0)
    right = jnp.where(has_right("rec"), right, -1.0)
    widx_ref[...] = jnp.zeros(widx_ref.shape, F32)
    widx_ref[0:DEPTHS, :] = ridx_ref[...].astype(F32)
    own = [widx_ref[:, t * LANES:(t + 1) * LANES] for t in range(tiles)]
    table = table_ref[...]
    block = 0
    for z in range(DEPTHS):
        index = wide_tiles(own, left, right, HALF * (DEPTHS - 1 - z), -1.0)
        for b in range(step_blocks(cols, z)):
            found = bands(index[b][z:z + 1].astype(jnp.int32), table, entries)
            for f in range(freqs):
                re, im = found[2 * f], found[2 * f + 1]
                for half in range(2):
                    at = pl.ds(half * LANES, LANES)
                    w_ref[block, f, 0, 0:LANES, at] = re[half]
                    w_ref[block, f, 0, LANES:SPAN, at] = im[half]
                    w_ref[block, f, 1, 0:LANES, at] = -im[half]
                    w_ref[block, f, 1, LANES:SPAN, at] = re[half]
            block += 1
    for ref in (a0_ref, a1_ref):
        for p in range(planes):
            ref[p, :, (tiles + 1) * LANES:] = jnp.zeros((rows, LANES), BF)
    store = Store((a0_ref, a1_ref, a2_ref), ((0, 0, rows),))
    receiver_steps(wide_ref, store, w_ref, freqs, cols)


def last_kernel(
    rows, cols, sa_ref, sb_ref, ca_ref, cb_ref, sidx_ref, table_ref, w_ref, o0_ref, o1_ref, o2_ref, pair_ref,
    final_ref, send_ref, keep_ref, wide_ref, a0_ref, a1_ref, a2_ref, sx_ref, part_ref,
):
    planes = o0_ref.shape[0]
    freqs = planes // 2
    tiles = cols // LANES
    entries = table_ref.shape[0]
    even = parity("src") == 0
    lane = lane_of((HALO, LANES))
    for side in range(2):
        there = has_left("src") if side == 0 else has_right("src")
        for p in range(planes):
            at = slice(p * HALO, (p + 1) * HALO)

            def got(a_ref, b_ref, lanes):
                a, b = a_ref[at, lanes], b_ref[at, lanes]
                return jnp.where(even, b, a) if side == 0 else jnp.where(even, a, b)

            edge = got(ca_ref, cb_ref, slice(0, LANES)).astype(F32)
            moved = [
                shifted(got(sa_ref, sb_ref, slice(t * LANES, (t + 1) * LANES)).astype(F32), HALO)
                for t in range(tiles)
            ]
            before, after = [edge] + moved, moved + [edge]
            to = slice(side * HALO, (side + 1) * HALO)
            for t in range(tiles + 1):
                value = jnp.where(lane < HALO, before[t], after[t])
                wide_ref[p, to, t * LANES:(t + 1) * LANES] = jnp.where(there, value, 0.0).astype(BF)
            wide_ref[p, to, (tiles + 1) * LANES:] = jnp.zeros((HALO, LANES), BF)
    full = rows + 2 * HALO
    for ref, own in ((a0_ref, o0_ref), (a1_ref, o1_ref), (a2_ref, o2_ref)):
        width = ref.shape[2]
        for p in range(planes):
            ref[p, HALO:HALO + rows, :] = own[p]
            ref[p, full:, :] = jnp.zeros((ref.shape[1] - full, width), BF)
            if width > (tiles + 1) * LANES:
                for to in (0, HALO + rows):
                    ref[p, to:to + HALO, (tiles + 1) * LANES:] = jnp.zeros((HALO, LANES), BF)
    base = planes * HALO
    got_a, got_b = ca_ref[base:base + IDX_ROWS, :], cb_ref[base:base + IDX_ROWS, :]
    left = jnp.where(even, got_b, got_a).astype(F32)[0:8]
    right = jnp.where(even, got_a, got_b).astype(F32)[0:8]
    left = jnp.where(has_left("src"), left, -1.0)
    right = jnp.where(has_right("src"), right, -1.0)
    sx_ref[...] = jnp.zeros(sx_ref.shape, F32)
    sx_ref[0:DEPTHS, 0:rows] = sidx_ref[...].astype(F32)
    reach = HALO - HALF
    lane8 = lane_of((8, LANES))
    index = jnp.where(
        lane8 < reach,
        shifted(left, reach - rows),
        jnp.where(lane8 < reach + rows, shifted(sx_ref[...], reach), shifted(right, reach + rows)),
    )
    table = table_ref[...]
    ops = []
    for z in range(DEPTHS):
        row = shifted(index, -z * HALF)[z:z + 1].astype(jnp.int32)
        ops.append(bands(row, table, entries))
    sums = []
    for f in range(freqs):
        (s0r, s0r2), (s0i, s0i2) = ops[0][2 * f], ops[0][2 * f + 1]
        s1r, s1i = ops[1][2 * f][0], ops[1][2 * f + 1][0]
        s2r, s2i = ops[2][2 * f][0][:rows], ops[2][2 * f + 1][0][:rows]
        s12r = (dot(s2r, s1r) - dot(s2i, s1i)).astype(BF)
        s12i = (dot(s2r, s1i) + dot(s2i, s1r)).astype(BF)
        lr = jnp.concatenate([s12r, s1r[HALF:HALF + rows]], axis=0)
        li = jnp.concatenate([s12i, s1i[HALF:HALF + rows]], axis=0)
        s0r = jnp.concatenate([s0r, s0r2], axis=1)
        s0i = jnp.concatenate([s0i, s0i2], axis=1)
        pr = (dot(lr, s0r) - dot(li, s0i)).astype(BF)
        pi = (dot(lr, s0i) + dot(li, s0r)).astype(BF)
        sums.append((
            (s0r[reach:reach + rows], s0i[reach:reach + rows]),
            (pr[rows:], pi[rows:]),
            (pr[:rows], pi[:rows]),
        ))
    store = Store((a0_ref, a1_ref, a2_ref), ((0, 0, HALO), (HALO + rows, HALO, HALO)))
    receiver_halo(wide_ref, store, w_ref, freqs, cols, rows)
    lane = lane_of((rows, LANES))
    images = []
    for z in range(DEPTHS - 1):
        ref = (a0_ref, a1_ref)[z]
        width = (tiles + 1) * LANES
        total = None
        for f in range(freqs):
            re, im = sums[f][z]
            term = dot(re, ref[f, :, 0:width]) - dot(im, ref[freqs + f, :, 0:width])
            total = term if total is None else total + term
        back = HALF * (DEPTHS - 1 - z)
        moved = [shifted(total[:, t * LANES:(t + 1) * LANES], -back) for t in range(tiles + 1)]
        images.append([jnp.where(lane < LANES - back, moved[t], moved[t + 1]) for t in range(tiles)])
    real = None
    for f in range(freqs):
        re, im = sums[f][DEPTHS - 1]
        first = dot(jnp.concatenate([re, im], axis=0), a2_ref[f])
        second = dot(jnp.concatenate([-im, re], axis=0), a2_ref[freqs + f])
        both = (first + second).astype(BF)
        final_ref[f] = both[:rows]
        final_ref[freqs + f] = both[rows:]
        term = both[:rows].astype(F32)
        real = term if real is None else real + term
    for t in range(tiles):
        at = slice(t * LANES, (t + 1) * LANES)
        value = pair_ref[DEPTHS - 1, :, at] * real[:, at]
        for z in range(DEPTHS - 1):
            value += pair_ref[z, :, at] * images[z][t]
        part_ref[:, at] = value
    count = lax.axis_size("freq")
    share = rows // count
    me = lax.axis_index("freq")
    keep_ref[...] = part_ref[pl.ds(pl.multiple_of(me * share, 8), share), :]
    for j in range(1, count):
        there = partner(me, j, count)
        send_ref[j - 1] = part_ref[pl.ds(pl.multiple_of(there * share, 8), share), :].astype(BF)


def receiver_halo(x_ref, store, w_ref, freqs, cols, rows):
    block = 0
    for z in range(DEPTHS):
        for b in range(step_blocks(cols, z)):
            window = slice(b * LANES, b * LANES + SPAN)
            for f in range(freqs):
                if z == 0:
                    re, im = x_ref[f, :, window], x_ref[freqs + f, :, window]
                else:
                    ref = store.refs[z - 1]
                    re, im = (
                        jnp.concatenate([ref[p, 0:HALO, window], ref[p, HALO + rows:2 * HALO + rows, window]], axis=0)
                        for p in (f, freqs + f)
                    )
                got = dot(re, w_ref[block, f, 0], NT) + dot(im, w_ref[block, f, 1], NT)
                store(z, f, b, got[:, :LANES].astype(BF))
                store(z, freqs + f, b, got[:, LANES:].astype(BF))
            block += 1


def partner(me, j, count):
    if count & (count - 1) == 0:
        return me ^ j
    return (me + j) % count


def local_call(kernel, outs, scratch=(), flops=0, moved=0, vmem=16):
    return pl.pallas_call(
        kernel,
        out_shape=[jax.ShapeDtypeStruct(s, d) for s, d in outs],
        scratch_shapes=[pltpu.VMEM(s, d) for s, d in scratch],
        compiler_params=pltpu.CompilerParams(vmem_limit_bytes=vmem << 20),
        cost_estimate=pl.CostEstimate(flops=flops, bytes_accessed=moved, transcendentals=0),
    )


def shards(wave, tap_table, src_index, rec_index, offset_bin, bin_weight):
    freqs, rows, cols = wave.shape[1:]
    planes = 2 * freqs
    tiles = cols // LANES
    entries = tap_table.shape[1]
    count = lax.axis_size("freq")
    share = rows // count
    x = wave.reshape(planes, rows, cols)
    table = jnp.transpose(tap_table.astype(BF), (1, 2, 0, 3))
    table = jnp.pad(table, ((0, 0), (0, 0), (0, 0), (0, LANES - TAPS))).reshape(entries, planes * LANES)

    main = (planes * HALO, cols)
    beside = (planes * rows + IDX_ROWS, LANES)
    sa, sb, ra, rb = local_call(pack_kernel, [(main, BF), (main, BF), (beside, BF), (beside, BF)], moved=1 << 20)(
        x, rec_index
    )
    ra, rb = swap(ra, "rec", 0), swap(rb, "rec", 1)
    sa, sb = swap(sa, "src", 0), swap(sb, "src", 1)
    corner = (planes * HALO + IDX_ROWS, LANES)
    ca, cb, edge = local_call(
        functools.partial(corner_kernel, rows),
        [(corner, BF), (corner, BF), ((planes * rows, LANES), BF)],
        moved=1 << 18,
    )(ra, rb, src_index)
    ca, cb = swap(ca, "src", 0), swap(cb, "src", 1)

    blocks = sum(step_blocks(cols, z) for z in range(DEPTHS))
    wide = (tiles + 2) * LANES
    w, o0, o1, o2, pair = local_call(
        own_kernel,
        [
            ((blocks, freqs, 2, SPAN, SPAN), BF),
            ((planes, rows, wide), BF),
            ((planes, rows, wide), BF),
            ((planes, rows, cols), BF),
            ((DEPTHS, rows, cols), F32),
        ],
        [((planes, rows, wide), BF), ((8, cols), F32), ((8, LANES), F32)],
        flops=1 << 31,
        moved=10 << 20,
        vmem=24,
    )(x, edge, ra, rb, rec_index, table, offset_bin, bin_weight)
    deep = -(-(rows + 2 * HALO) // SPAN) * SPAN
    final, send, keep = local_call(
        functools.partial(last_kernel, rows, cols),
        [((planes, rows, cols), BF), ((max(count - 1, 1), share, cols), BF), ((share, cols), F32)],
        [
            ((planes, 2 * HALO, wide), BF),
            ((planes, deep, wide), BF),
            ((planes, deep, wide), BF),
            ((planes, deep, cols), BF),
            ((8, LANES), F32),
            ((rows, cols), F32),
        ],
        flops=1 << 31,
        moved=10 << 20,
        vmem=28,
    )(sa, sb, ca, cb, src_index, table, w, o0, o1, o2, pair)
    total = keep
    for j in range(1, count):
        got = lax.ppermute(send[j - 1], "freq", [(i, partner(i, j, count)) for i in range(count)])
        total = total + got.astype(F32)
    scale = 1.0 / math.sqrt(freqs * count * DEPTHS)
    return final.reshape(wave.shape), total * scale


def solution(mesh):
    placed = (
        P(None, "freq", "src", "rec"),
        P(None, None, "freq", None),
        P(None, "src"),
        P(None, "rec"),
        P("src", "rec"),
        P(),
    )
    return jax.shard_map(
        shards,
        mesh=mesh,
        in_specs=placed,
        out_specs=(P(None, "freq", "src", "rec"), P(("src", "freq"), "rec")),
        check_vma=False,
    )
```

```python
import functools
import math

import jax
import jax.numpy as jnp
from jax import lax
from jax.experimental import pallas as pl
from jax.experimental.pallas import tpu as pltpu
from jax.sharding import PartitionSpec as P

TAPS = 33
DEPTHS = 3
HALF = TAPS // 2
HALO = DEPTHS * HALF
LANES = 128
SPAN = 2 * LANES
IDX_ROWS = 16
BF = jnp.bfloat16
F32 = jnp.float32


def pairs_of(axis, odd):
    count, groups = lax.axis_size(axis), lax.axis_size("freq")
    pairs, alone = [], list(range(count))
    for i in range(odd, count - 1, 2):
        alone.remove(i)
        alone.remove(i + 1)
        for g in range(groups):
            pairs += [(i * groups + g, (i + 1) * groups + g), ((i + 1) * groups + g, i * groups + g)]
    for i in alone:
        for g in range(0, groups - 1, 2):
            pairs += [(i * groups + g, i * groups + g + 1), (i * groups + g + 1, i * groups + g)]
    return pairs


def swap(cells, axis, odd):
    return lax.ppermute(cells, (axis, "freq"), pairs_of(axis, odd))


def parity(axis):
    return lax.rem(lax.axis_index(axis), 2)


def has_left(axis):
    return lax.axis_index(axis) > 0


def has_right(axis):
    return lax.axis_index(axis) < lax.axis_size(axis) - 1


def lane_of(shape):
    return lax.broadcasted_iota(jnp.int32, shape, len(shape) - 1)


def shifted(cells, amount):
    amount = amount % LANES
    return pltpu.roll(cells, amount, 1) if amount else cells


def left_right(a_ref, b_ref, axis):
    even = parity(axis) == 0
    a, b = a_ref[...], b_ref[...]
    return jnp.where(even, b, a), jnp.where(even, a, b)


def pack_kernel(*refs):
    sources, targets = refs[:5], refs[9:14]
    sa_ref, sb_ref, ra_ref, rb_ref = refs[5:9]
    sem = refs[14]
    copies = [pltpu.make_async_copy(s, t, sem.at[i]) for i, (s, t) in enumerate(zip(sources, targets))]
    for copy in copies:
        copy.start()
    x_ref, ridx_ref = targets[:2]
    planes, rows, cols = x_ref.shape
    copies[0].wait()
    even = parity("src") == 0
    low = rows - HALO
    at = pl.multiple_of(jnp.where(even, low, 0), 16)
    other = pl.multiple_of(jnp.where(even, 0, low), 16)
    for p in range(planes):
        sa_ref[p * HALO:(p + 1) * HALO, :] = x_ref[p, pl.ds(at, HALO), :]
        sb_ref[p * HALO:(p + 1) * HALO, :] = x_ref[p, pl.ds(other, HALO), :]
    even = parity("rec") == 0
    tail_at = cols - LANES
    copies[1].wait()
    for p in range(planes):
        head, tail = x_ref[p, :, 0:LANES], x_ref[p, :, tail_at:cols]
        ra_ref[p * rows:(p + 1) * rows, :] = jnp.where(even, tail, head)
        rb_ref[p * rows:(p + 1) * rows, :] = jnp.where(even, head, tail)
    base = planes * rows
    head = ridx_ref[:, 0:LANES].astype(F32).astype(BF)
    tail = ridx_ref[:, tail_at:cols].astype(F32).astype(BF)
    for ref in (ra_ref, rb_ref):
        ref[base:base + IDX_ROWS, :] = jnp.zeros((IDX_ROWS, LANES), BF)
    ra_ref[base:base + DEPTHS, :] = jnp.where(even, tail, head)
    rb_ref[base:base + DEPTHS, :] = jnp.where(even, head, tail)
    for copy in copies[2:]:
        copy.wait()


def corner_kernel(rows, ra_ref, rb_ref, sidx_ref, ca_ref, cb_ref, edge_ref):
    left, right = left_right(ra_ref, rb_ref, "rec")
    total = (left.shape[0] - IDX_ROWS)
    planes = total // rows
    lane = lane_of((total, LANES))
    left = shifted(left[:total].astype(F32), HALO)
    right = shifted(right[:total].astype(F32), HALO)
    in_left = (lane < HALO) & has_left("rec")
    in_right = (lane >= HALO) & (lane < 2 * HALO) & has_right("rec")
    edge_ref[...] = jnp.where(in_left, left, jnp.where(in_right, right, 0.0)).astype(BF)
    even = parity("src") == 0
    low = rows - HALO
    at = jnp.where(even, low, 0)
    other = jnp.where(even, 0, low)
    for p in range(planes):
        ca_ref[p * HALO:(p + 1) * HALO, :] = edge_ref[pl.ds(pl.multiple_of(p * rows + at, 16), HALO), :]
        cb_ref[p * HALO:(p + 1) * HALO, :] = edge_ref[pl.ds(pl.multiple_of(p * rows + other, 16), HALO), :]
    base = planes * HALO
    idx = sidx_ref[...].astype(F32).astype(BF)
    for ref in (ca_ref, cb_ref):
        ref[base:base + IDX_ROWS, :] = jnp.zeros((IDX_ROWS, LANES), BF)
        ref[base:base + DEPTHS, 0:rows] = idx


def wide_tiles(own, left, right, amount, fill):
    count = len(own)
    lane = lane_of(own[0].shape)
    moved = [shifted(t, amount) for t in own]
    if amount == 0:
        return moved
    tiles = [jnp.where(lane < amount, shifted(left, amount), moved[0])]
    for t in range(1, count):
        tiles.append(jnp.where(lane < amount, moved[t - 1], moved[t]))
    last = jnp.where(lane < 2 * amount, shifted(right, amount), fill)
    tiles.append(jnp.where(lane < amount, moved[count - 1], last))
    return tiles


def bands(idx_row, table, entries):
    onehot = (lax.broadcasted_iota(jnp.int32, (entries, LANES), 0) == idx_row).astype(F32).astype(BF)
    taps = lax.dot_general(onehot, table, (((0,), (0,)), ((), ())), preferred_element_type=F32)
    out = lax.broadcasted_iota(jnp.int32, (LANES, LANES), 0)
    lane = lane_of((LANES, LANES))
    found = []
    for part in range(taps.shape[1] // LANES):
        skewed = pltpu.roll(taps[:, part * LANES:(part + 1) * LANES], 0, 1, stride=1, stride_axis=0)
        first = jnp.where(lane >= out, skewed, 0.0).astype(BF)
        second = jnp.where(lane < out, skewed, 0.0).astype(BF)
        found.append((first, second))
    return found


NT = (((1,), (1,)), ((), ()))
NN = (((1,), (0,)), ((), ()))


def dot(a, b, dims=NN):
    return lax.dot_general(a, b, dims, preferred_element_type=F32)


def step_blocks(cols, z):
    return -(-(cols + 2 * HALF * (DEPTHS - 1 - z)) // LANES)


def receiver_steps(x_ref, outs, w_ref, freqs, cols):
    block = 0
    source = x_ref
    for z in range(DEPTHS):
        for b in range(step_blocks(cols, z)):
            window = pl.ds(b * LANES, SPAN)
            for f in range(freqs):
                got = dot(source[f, :, window], w_ref[block, f, 0], NT)
                got += dot(source[freqs + f, :, window], w_ref[block, f, 1], NT)
                outs(z, f, b, got[:, :LANES].astype(BF))
                outs(z, freqs + f, b, got[:, LANES:].astype(BF))
            block += 1
        source = outs.source(z)


class Store:
    def __init__(self, refs, places):
        self.refs, self.places = refs, places

    def __call__(self, z, plane, b, value):
        for at, start, size in self.places:
            self.refs[z][plane, at:at + size, b * LANES:(b + 1) * LANES] = value[start:start + size]

    def source(self, z):
        return self.refs[z]


def own_kernel(
    x_ref, edge_ref, ra_ref, rb_ref, ridx_ref, table_ref, bins_ref, weight_ref,
    w_ref, a0_ref, a1_ref, a2_ref, pair_ref, wide_ref, widx_ref, wt_ref,
):
    planes, rows, cols = x_ref.shape
    freqs = planes // 2
    tiles = cols // LANES
    entries = table_ref.shape[0]
    wt_ref[...] = jnp.zeros(wt_ref.shape, F32)
    wt_ref[0:DEPTHS, 0:weight_ref.shape[1]] = weight_ref[...]
    for t in range(tiles):
        bins = bins_ref[:, t * LANES:(t + 1) * LANES]
        for z in range(DEPTHS):
            row = jnp.broadcast_to(wt_ref[z:z + 1, :], (rows, LANES))
            pair_ref[z, :, t * LANES:(t + 1) * LANES] = jnp.take_along_axis(row, bins, axis=1)
    lane = lane_of((rows, LANES))
    for p in range(planes):
        edge = edge_ref[p * rows:(p + 1) * rows, :].astype(F32)
        own = [x_ref[p, :, t * LANES:(t + 1) * LANES].astype(F32) for t in range(tiles)]
        moved = [shifted(o, HALO) for o in own]
        before = [edge] + moved
        after = moved + [edge]
        for t in range(tiles + 1):
            wide_ref[p, :, t * LANES:(t + 1) * LANES] = jnp.where(lane < HALO, before[t], after[t]).astype(BF)
        wide_ref[p, :, (tiles + 1) * LANES:] = jnp.zeros((rows, LANES), BF)
    base = planes * rows
    even = parity("rec") == 0
    got_a, got_b = ra_ref[base:base + IDX_ROWS, :], rb_ref[base:base + IDX_ROWS, :]
    left = jnp.where(even, got_b, got_a).astype(F32)[0:8]
    right = jnp.where(even, got_a, got_b).astype(F32)[0:8]
    left = jnp.where(has_left("rec"), left, -1.0)
    right = jnp.where(has_right("rec"), right, -1.0)
    widx_ref[...] = jnp.zeros(widx_ref.shape, F32)
    widx_ref[0:DEPTHS, :] = ridx_ref[...].astype(F32)
    own = [widx_ref[:, t * LANES:(t + 1) * LANES] for t in range(tiles)]
    table = table_ref[...]
    block = 0
    for z in range(DEPTHS):
        index = wide_tiles(own, left, right, HALF * (DEPTHS - 1 - z), -1.0)
        for b in range(step_blocks(cols, z)):
            found = bands(index[b][z:z + 1].astype(jnp.int32), table, entries)
            for f in range(freqs):
                re, im = found[2 * f], found[2 * f + 1]
                for half in range(2):
                    at = pl.ds(half * LANES, LANES)
                    w_ref[block, f, 0, 0:LANES, at] = re[half]
                    w_ref[block, f, 0, LANES:SPAN, at] = im[half]
                    w_ref[block, f, 1, 0:LANES, at] = -im[half]
                    w_ref[block, f, 1, LANES:SPAN, at] = re[half]
            block += 1
    for ref in (a0_ref, a1_ref):
        for p in range(planes):
            ref[p, :, (tiles + 1) * LANES:] = jnp.zeros((rows, LANES), BF)
    store = Store((a0_ref, a1_ref, a2_ref), ((0, 0, rows),))
    receiver_steps(wide_ref, store, w_ref, freqs, cols)


def last_kernel(
    rows, cols, sa_ref, sb_ref, ca_ref, cb_ref, sidx_ref, table_ref, w_ref, o0_ref, o1_ref, o2_ref, pair_ref,
    final_ref, send_ref, keep_ref, wide_ref, a0_ref, a1_ref, a2_ref, sx_ref, part_ref,
):
    planes = o0_ref.shape[0]
    freqs = planes // 2
    tiles = cols // LANES
    entries = table_ref.shape[0]
    even = parity("src") == 0
    lane = lane_of((HALO, LANES))
    for side in range(2):
        there = has_left("src") if side == 0 else has_right("src")
        for p in range(planes):
            at = slice(p * HALO, (p + 1) * HALO)

            def got(a_ref, b_ref, lanes):
                a, b = a_ref[at, lanes], b_ref[at, lanes]
                return jnp.where(even, b, a) if side == 0 else jnp.where(even, a, b)

            edge = got(ca_ref, cb_ref, slice(0, LANES)).astype(F32)
            moved = [
                shifted(got(sa_ref, sb_ref, slice(t * LANES, (t + 1) * LANES)).astype(F32), HALO)
                for t in range(tiles)
            ]
            before, after = [edge] + moved, moved + [edge]
            to = slice(side * HALO, (side + 1) * HALO)
            for t in range(tiles + 1):
                value = jnp.where(lane < HALO, before[t], after[t])
                wide_ref[p, to, t * LANES:(t + 1) * LANES] = jnp.where(there, value, 0.0).astype(BF)
            wide_ref[p, to, (tiles + 1) * LANES:] = jnp.zeros((HALO, LANES), BF)
    full = rows + 2 * HALO
    for ref, own in ((a0_ref, o0_ref), (a1_ref, o1_ref), (a2_ref, o2_ref)):
        width = ref.shape[2]
        for p in range(planes):
            ref[p, HALO:HALO + rows, :] = own[p]
            ref[p, full:, :] = jnp.zeros((ref.shape[1] - full, width), BF)
            if width > (tiles + 1) * LANES:
                for to in (0, HALO + rows):
                    ref[p, to:to + HALO, (tiles + 1) * LANES:] = jnp.zeros((HALO, LANES), BF)
    base = planes * HALO
    got_a, got_b = ca_ref[base:base + IDX_ROWS, :], cb_ref[base:base + IDX_ROWS, :]
    left = jnp.where(even, got_b, got_a).astype(F32)[0:8]
    right = jnp.where(even, got_a, got_b).astype(F32)[0:8]
    left = jnp.where(has_left("src"), left, -1.0)
    right = jnp.where(has_right("src"), right, -1.0)
    sx_ref[...] = jnp.zeros(sx_ref.shape, F32)
    sx_ref[0:DEPTHS, 0:rows] = sidx_ref[...].astype(F32)
    reach = HALO - HALF
    lane8 = lane_of((8, LANES))
    index = jnp.where(
        lane8 < reach,
        shifted(left, reach - rows),
        jnp.where(lane8 < reach + rows, shifted(sx_ref[...], reach), shifted(right, reach + rows)),
    )
    table = table_ref[...]
    ops = []
    for z in range(DEPTHS):
        row = shifted(index, -z * HALF)[z:z + 1].astype(jnp.int32)
        ops.append(bands(row, table, entries))
    sums = []
    for f in range(freqs):
        (s0r, s0r2), (s0i, s0i2) = ops[0][2 * f], ops[0][2 * f + 1]
        s1r, s1i = ops[1][2 * f][0], ops[1][2 * f + 1][0]
        s2r, s2i = ops[2][2 * f][0][:rows], ops[2][2 * f + 1][0][:rows]
        s12r = (dot(s2r, s1r) - dot(s2i, s1i)).astype(BF)
        s12i = (dot(s2r, s1i) + dot(s2i, s1r)).astype(BF)
        lr = jnp.concatenate([s12r, s1r[HALF:HALF + rows]], axis=0)
        li = jnp.concatenate([s12i, s1i[HALF:HALF + rows]], axis=0)
        s0r = jnp.concatenate([s0r, s0r2], axis=1)
        s0i = jnp.concatenate([s0i, s0i2], axis=1)
        pr = (dot(lr, s0r) - dot(li, s0i)).astype(BF)
        pi = (dot(lr, s0i) + dot(li, s0r)).astype(BF)
        sums.append((
            (s0r[reach:reach + rows], s0i[reach:reach + rows]),
            (pr[rows:], pi[rows:]),
            (pr[:rows], pi[:rows]),
        ))
    store = Store((a0_ref, a1_ref, a2_ref), ((0, 0, HALO), (HALO + rows, HALO, HALO)))
    receiver_halo(wide_ref, store, w_ref, freqs, cols, rows)
    lane = lane_of((rows, LANES))
    images = []
    for z in range(DEPTHS - 1):
        ref = (a0_ref, a1_ref)[z]
        width = (tiles + 1) * LANES
        total = None
        for f in range(freqs):
            re, im = sums[f][z]
            term = dot(re, ref[f, :, 0:width]) - dot(im, ref[freqs + f, :, 0:width])
            total = term if total is None else total + term
        back = HALF * (DEPTHS - 1 - z)
        moved = [shifted(total[:, t * LANES:(t + 1) * LANES], -back) for t in range(tiles + 1)]
        images.append([jnp.where(lane < LANES - back, moved[t], moved[t + 1]) for t in range(tiles)])
    real = None
    for f in range(freqs):
        re, im = sums[f][DEPTHS - 1]
        first = dot(jnp.concatenate([re, im], axis=0), a2_ref[f])
        second = dot(jnp.concatenate([-im, re], axis=0), a2_ref[freqs + f])
        both = (first + second).astype(BF)
        final_ref[f] = both[:rows]
        final_ref[freqs + f] = both[rows:]
        term = both[:rows].astype(F32)
        real = term if real is None else real + term
    for t in range(tiles):
        at = slice(t * LANES, (t + 1) * LANES)
        value = pair_ref[DEPTHS - 1, :, at] * real[:, at]
        for z in range(DEPTHS - 1):
            value += pair_ref[z, :, at] * images[z][t]
        part_ref[:, at] = value
    count = lax.axis_size("freq")
    share = rows // count
    me = lax.axis_index("freq")
    keep_ref[...] = part_ref[pl.ds(pl.multiple_of(me * share, 8), share), :]
    for j in range(1, count):
        there = partner(me, j, count)
        send_ref[j - 1] = part_ref[pl.ds(pl.multiple_of(there * share, 8), share), :].astype(BF)


def receiver_halo(x_ref, store, w_ref, freqs, cols, rows):
    block = 0
    for z in range(DEPTHS):
        for b in range(step_blocks(cols, z)):
            window = slice(b * LANES, b * LANES + SPAN)
            for f in range(freqs):
                if z == 0:
                    re, im = x_ref[f, :, window], x_ref[freqs + f, :, window]
                else:
                    ref = store.refs[z - 1]
                    re, im = (
                        jnp.concatenate([ref[p, 0:HALO, window], ref[p, HALO + rows:2 * HALO + rows, window]], axis=0)
                        for p in (f, freqs + f)
                    )
                got = dot(re, w_ref[block, f, 0], NT) + dot(im, w_ref[block, f, 1], NT)
                store(z, f, b, got[:, :LANES].astype(BF))
                store(z, freqs + f, b, got[:, LANES:].astype(BF))
            block += 1


def partner(me, j, count):
    if count & (count - 1) == 0:
        return me ^ j
    return (me + j) % count


def local_call(kernel, outs, scratch=(), flops=0, moved=0, vmem=16, **others):
    return pl.pallas_call(
        kernel,
        out_shape=[jax.ShapeDtypeStruct(s, d) for s, d in outs],
        scratch_shapes=[pltpu.VMEM(*s) if isinstance(s, tuple) else s for s in scratch],
        **others,
        compiler_params=pltpu.CompilerParams(vmem_limit_bytes=vmem << 20),
        cost_estimate=pl.CostEstimate(flops=flops, bytes_accessed=moved, transcendentals=0),
    )


def migrate(wave, tap_table, src_index, rec_index, offset_bin, bin_weight):
    freqs, rows, cols = wave.shape[1:]
    planes = 2 * freqs
    tiles = cols // LANES
    entries = tap_table.shape[1]
    count = lax.axis_size("freq")
    share = rows // count
    x = wave.reshape(planes, rows, cols)
    table = jnp.transpose(tap_table.astype(BF), (1, 2, 0, 3))
    table = jnp.pad(table, ((0, 0), (0, 0), (0, 0), (0, LANES - TAPS))).reshape(entries, planes * LANES)

    main = (planes * HALO, cols)
    beside = (planes * rows + IDX_ROWS, LANES)
    inputs = tuple(pltpu.with_memory_space_constraint(a, pltpu.HBM) for a in (x, rec_index, src_index, offset_bin, bin_weight))
    sa, sb, ra, rb, x, rec_index, src_index, offset_bin, bin_weight = local_call(
        pack_kernel,
        [(main, BF), (main, BF), (beside, BF), (beside, BF)] + [(a.shape, a.dtype) for a in inputs],
        [pltpu.SemaphoreType.DMA((len(inputs),))],
        moved=1 << 20,
        in_specs=[pl.BlockSpec(memory_space=pltpu.HBM)] * len(inputs),
    )(*inputs)
    sa = swap(sa, "src", 0)
    sb = swap(sb, "src", 1)
    ra = swap(ra, "rec", 0)
    rb = swap(rb, "rec", 1)
    corner = (planes * HALO + IDX_ROWS, LANES)
    ca, cb, edge = local_call(
        functools.partial(corner_kernel, rows),
        [(corner, BF), (corner, BF), ((planes * rows, LANES), BF)],
        moved=1 << 18,
    )(ra, rb, src_index)
    ca, cb = swap(ca, "src", 0), swap(cb, "src", 1)

    blocks = sum(step_blocks(cols, z) for z in range(DEPTHS))
    wide = (tiles + 2) * LANES
    w, o0, o1, o2, pair = local_call(
        own_kernel,
        [
            ((blocks, freqs, 2, SPAN, SPAN), BF),
            ((planes, rows, wide), BF),
            ((planes, rows, wide), BF),
            ((planes, rows, cols), BF),
            ((DEPTHS, rows, cols), F32),
        ],
        [((planes, rows, wide), BF), ((8, cols), F32), ((8, LANES), F32)],
        flops=1 << 31,
        moved=10 << 20,
        vmem=24,
    )(x, edge, ra, rb, rec_index, table, offset_bin, bin_weight)
    deep = -(-(rows + 2 * HALO) // SPAN) * SPAN
    final, send, keep = local_call(
        functools.partial(last_kernel, rows, cols),
        [((planes, rows, cols), BF), ((max(count - 1, 1), share, cols), BF), ((share, cols), F32)],
        [
            ((planes, 2 * HALO, wide), BF),
            ((planes, deep, wide), BF),
            ((planes, deep, wide), BF),
            ((planes, deep, cols), BF),
            ((8, LANES), F32),
            ((rows, cols), F32),
        ],
        flops=1 << 31,
        moved=10 << 20,
        vmem=28,
    )(sa, sb, ca, cb, src_index, table, w, o0, o1, o2, pair)
    total = keep
    for j in range(1, count):
        got = lax.ppermute(send[j - 1], "freq", [(i, partner(i, j, count)) for i in range(count)])
        total = total + got.astype(F32)
    scale = 1.0 / math.sqrt(freqs * count * DEPTHS)
    return final.reshape(wave.shape), total * scale


def solution(mesh):
    placed = (
        P(None, "freq", "src", "rec"),
        P(None, None, "freq", None),
        P(None, "src"),
        P(None, "rec"),
        P("src", "rec"),
        P(),
    )
    return jax.shard_map(
        migrate,
        mesh=mesh,
        in_specs=placed,
        out_specs=(P(None, "freq", "src", "rec"), P(("src", "freq"), "rec")),
        check_vma=False,
    )
```

```python
import math

import jax
import jax.numpy as jnp
from jax import lax
from jax.experimental import pallas as pl
from jax.experimental.pallas import tpu as pltpu
from jax.sharding import PartitionSpec as P

TAPS = 33
DEPTHS = 3
HALF = TAPS // 2
HALO = DEPTHS * HALF
LANES = 128
MID = LANES // 2
OUT = LANES - 2 * HALF
WROWS = LANES + OUT
IDX_ROWS = 16
BF = jnp.bfloat16
F32 = jnp.float32
NT = (((1,), (1,)), ((), ()))
NN = (((1,), (0,)), ((), ()))
TN = (((0,), (0,)), ((), ()))


def dot(a, b, dims=NN):
    return lax.dot_general(a, b, dims, preferred_element_type=F32)


def pairs_of(axis, odd):
    count, groups = lax.axis_size(axis), lax.axis_size("freq")
    pairs, alone = [], list(range(count))
    for i in range(odd, count - 1, 2):
        alone.remove(i)
        alone.remove(i + 1)
        for g in range(groups):
            pairs += [(i * groups + g, (i + 1) * groups + g), ((i + 1) * groups + g, i * groups + g)]
    for i in alone:
        for g in range(0, groups - 1, 2):
            pairs += [(i * groups + g, i * groups + g + 1), (i * groups + g + 1, i * groups + g)]
    return pairs


def swaps(a, b, axis):
    a = lax.ppermute(a, (axis, "freq"), pairs_of(axis, 0))
    b = lax.ppermute(b, (axis, "freq"), pairs_of(axis, 1))
    return a, b


def is_even(axis):
    return lax.rem(lax.axis_index(axis), 2) == 0


def has_left(axis):
    return lax.axis_index(axis) > 0


def has_right(axis):
    return lax.axis_index(axis) < lax.axis_size(axis) - 1


def lane_of(shape):
    return lax.broadcasted_iota(jnp.int32, shape, len(shape) - 1)


def roll(cells, amount):
    amount = amount % LANES
    return pltpu.roll(cells, amount, 1) if amount else cells


def from_sides(a, b, axis):
    even = is_even(axis)
    return jnp.where(even, b, a), jnp.where(even, a, b)


def join(pieces):
    tile = None
    for cells, start, amount in pieces:
        moved = roll(cells, amount)
        tile = moved if start == 0 else jnp.where(lane_of(moved.shape) < start, tile, moved)
    return tile


def gather(blocks, first, valid=OUT):
    pieces, at = [], 0
    while at < LANES:
        k, lane = divmod(first + at, OUT)
        if k >= len(blocks):
            break
        pieces.append((blocks[k], at, at - lane))
        at += valid - lane
    return join(pieces)


def load_kernel(*refs):
    count = 5
    sources, targets = refs[:count], refs[count + 4:2 * count + 4]
    ma_ref, mb_ref, sa_ref, sb_ref = refs[count:count + 4]
    sem, wave_sem = refs[2 * count + 4:]
    wave, x_ref = sources[0], targets[0]
    planes, tiles, rows, _ = x_ref.shape
    first = []
    for p in range(planes):
        for t in range(tiles):
            piece = wave.at[p, :, pl.ds(t * LANES, LANES)]
            first.append(pltpu.make_async_copy(piece, x_ref.at[p, t], wave_sem.at[p, t]))
    others = [
        pltpu.make_async_copy(s, t, sem.at[i]) for i, (s, t) in enumerate(zip(sources[1:], targets[1:]))
    ]
    for copy in others[:1] + first + others[1:]:
        copy.start()
    for copy in first:
        copy.wait()
    even = is_even("src")
    low = rows - HALO
    at_a = pl.multiple_of(jnp.where(even, low, 0), 16)
    at_b = pl.multiple_of(jnp.where(even, 0, low), 16)
    lane = lane_of((HALO, LANES))
    for p in range(planes):
        for at, main, small in ((at_a, ma_ref, sa_ref), (at_b, mb_ref, sb_ref)):
            for t in range(tiles):
                main[p, t] = x_ref[p, t, pl.ds(at, HALO), :]
            head, tail = x_ref[p, 0, pl.ds(at, HALO), :], x_ref[p, tiles - 1, pl.ds(at, HALO), :]
            small[p * HALO:(p + 1) * HALO, :] = jnp.where(lane < MID, head, tail)
    others[0].wait()
    base = planes * HALO
    index = targets[1][...].astype(F32).astype(BF)
    for small in (sa_ref, sb_ref):
        small[base:base + IDX_ROWS, :] = jnp.zeros((IDX_ROWS, LANES), BF)
        small[base:base + DEPTHS, 0:rows] = index
    for copy in others[1:]:
        copy.wait()


def edge_kernel(x_ref, ridx_ref, sa_ref, sb_ref, ra_ref, rb_ref):
    planes, tiles, rows, _ = x_ref.shape
    freqs = planes // 2
    full = rows + 2 * HALO
    even = is_even("rec")
    ends = (ra_ref, rb_ref)
    for f in range(freqs):
        at = f * full
        for start, size, tail, head in (
            (0, rows, [x_ref[p, tiles - 1] for p in (f, freqs + f)], [x_ref[p, 0] for p in (f, freqs + f)]),
            (rows, HALO, *[[side_of(sa_ref, sb_ref, p, 0) for p in (f, freqs + f)]] * 2),
            (rows + HALO, HALO, *[[side_of(sa_ref, sb_ref, p, 1) for p in (f, freqs + f)]] * 2),
        ):
            lane = lane_of((size, LANES))
            right = jnp.where(lane < MID, roll(tail[1], MID), tail[0])
            left = jnp.where(lane < MID, head[0], roll(head[1], MID))
            place = slice(at + start, at + start + size)
            ends[0][place, :] = jnp.where(even, right, left)
            ends[1][place, :] = jnp.where(even, left, right)
    base = freqs * full
    cols = tiles * LANES
    head = ridx_ref[:, 0:LANES].astype(F32).astype(BF)
    tail = ridx_ref[:, cols - LANES:cols].astype(F32).astype(BF)
    for ref, value in zip(ends, (jnp.where(even, tail, head), jnp.where(even, head, tail))):
        ref[base:base + IDX_ROWS, :] = jnp.zeros((IDX_ROWS, LANES), BF)
        ref[base:base + DEPTHS, :] = value


def side_of(a_ref, b_ref, p, side):
    at = slice(p * HALO, (p + 1) * HALO)
    return from_sides(a_ref[at, :], b_ref[at, :], "src")[side]


def index_sides(a_ref, b_ref, base, axis):
    left, right = from_sides(a_ref[base:base + IDX_ROWS, :], b_ref[base:base + IDX_ROWS, :], axis)
    left = jnp.where(has_left(axis), left.astype(F32)[0:8], -1.0)
    right = jnp.where(has_right(axis), right.astype(F32)[0:8], -1.0)
    return left, right


def taps_of(index_tiles, table, entries):
    hot = [
        (lax.broadcasted_iota(jnp.int32, (entries, LANES), 0) == tile.astype(jnp.int32)).astype(F32).astype(BF)
        for tile in index_tiles
    ]
    return dot(hot[0] if len(hot) == 1 else jnp.concatenate(hot, axis=1), table, TN)


def skew(taps):
    return pltpu.roll(taps, 0, 1, stride=1, stride_axis=0)


def source_kernel(
    sa_ref, sb_ref, sidx_ref, table_ref, bins_ref, weight_ref, near_ref, mid_ref, far_ref, pair_ref, sx_ref, wt_ref
):
    rows, cols = bins_ref.shape
    freqs = near_ref.shape[0]
    tiles = cols // LANES
    table = table_ref[...]
    entries = table.shape[0]
    wt_ref[...] = jnp.zeros(wt_ref.shape, F32)
    wt_ref[0:DEPTHS, 0:weight_ref.shape[1]] = weight_ref[...]
    for t in range(tiles):
        bins = bins_ref[:, t * LANES:(t + 1) * LANES]
        for z in range(DEPTHS):
            row = jnp.broadcast_to(wt_ref[z:z + 1, :], (rows, LANES))
            pair_ref[z, t] = jnp.take_along_axis(row, bins, axis=1)
    left, right = index_sides(sa_ref, sb_ref, 2 * freqs * HALO, "src")
    sx_ref[...] = jnp.zeros(sx_ref.shape, F32)
    sx_ref[0:DEPTHS, 0:rows] = sidx_ref[...].astype(F32)
    reach = HALO - HALF
    index = join([(left, 0, reach - rows), (sx_ref[...], reach, reach), (right, reach + rows, reach + rows)])
    out = lax.broadcasted_iota(jnp.int32, (LANES, LANES), 0)
    lane = lane_of((LANES, LANES))
    ops = []
    for z in range(DEPTHS):
        taps = taps_of([roll(index, -z * HALF)[z:z + 1]], table, entries)
        found = []
        for part in range(2 * freqs):
            skewed = skew(taps[:, part * LANES:(part + 1) * LANES])
            found.append((jnp.where(lane >= out, skewed, 0.0), jnp.where(lane < out, skewed, 0.0)))
        ops.append(found)
    narrow = lane_of((rows, LANES))
    for f in range(freqs):
        s0 = [[tile.astype(BF) for tile in ops[0][2 * f + part]] for part in range(2)]
        s1 = [ops[1][2 * f + part][0].astype(BF) for part in range(2)]
        s2 = [ops[2][2 * f + part][0][:rows].astype(BF) for part in range(2)]
        got = dot(jnp.concatenate(s2, axis=0), jnp.concatenate(s1, axis=1))
        re = (got[:rows, :LANES] - got[rows:, LANES:]).astype(BF)
        im = (got[:rows, LANES:] + got[rows:, :LANES]).astype(BF)
        stack = jnp.concatenate([re, s1[0][HALF:HALF + rows], im, s1[1][HALF:HALF + rows]], axis=0)
        by_re = dot(stack, jnp.concatenate(s0[0], axis=1))
        by_im = dot(stack, jnp.concatenate(s0[1], axis=1))
        pr = by_re[:2 * rows] - by_im[2 * rows:]
        pi = by_im[:2 * rows] + by_re[2 * rows:]
        size = rows + 2 * HALF
        own = slice(reach, reach + rows)
        parts = [
            join([(ops[0][2 * f + part][0][own], 0, -reach), (ops[0][2 * f + part][1][own], LANES - reach, -reach)])
            for part in range(2)
        ]
        parts = [jnp.where(narrow < size, part, 0.0) for part in parts]
        minus = -parts[1]
        near_ref[f, :, 0:LANES] = jnp.where(narrow < size, parts[0], roll(minus, size)).astype(BF)
        near_ref[f, :, LANES:] = jnp.where(narrow < 2 * size - LANES, roll(minus, size), 0.0).astype(BF)
        mids = [
            join([(g[rows:, :LANES], 0, -HALF), (g[rows:, LANES:], LANES - HALF, -HALF)]) for g in (pr, pi)
        ]
        mid_ref[f, :, 0:LANES] = mids[0].astype(BF)
        mid_ref[f, :, LANES:] = (-mids[1]).astype(BF)
        re, im = pr[:rows].astype(BF), pi[:rows].astype(BF)
        far_ref[f, 0] = jnp.concatenate([re, im], axis=0)
        far_ref[f, 1] = jnp.concatenate([-im, re], axis=0)


def windows(own, left, right, blocks):
    tiles, found = len(own), []
    for b in range(blocks):
        first = b * OUT - HALO
        j, s = divmod(first, LANES)
        pieces = []
        if b == 0:
            pieces = [(left[0], 0, left[1]), (own[0], HALO, HALO)]
        else:
            pieces.append((own[j], 0, -s))
            if s and j + 1 < tiles:
                pieces.append((own[j + 1], LANES - s, -s))
            end = tiles * LANES - first
            if end < LANES:
                pieces.append((right[0], end, end + right[1]))
        found.append(join(pieces))
    return found


def receiver_steps(first, w_ref, freqs, rows, keep):
    source = first
    blocks = len(first[0])
    for z in range(DEPTHS):
        after = [[None] * blocks for _ in range(2 * freqs)]
        for b in range(blocks):
            for f in range(freqs):
                both = jnp.concatenate([source[f][b], source[freqs + f][b]], axis=1)
                w = jnp.concatenate([w_ref[z, b, f, 0], w_ref[z, b, f, 1]], axis=1)
                got = dot(both, w, NT)
                for p, lanes in ((f, got[:, :OUT]), (freqs + f, got[:, LANES:LANES + OUT])):
                    after[p][b] = jnp.concatenate([lanes, jnp.zeros((rows, LANES - OUT), F32)], axis=1).astype(BF)
        if z < DEPTHS - 1:
            lane = lane_of((rows, LANES))
            source = [
                [
                    jnp.where(lane < OUT, plane[b], roll(plane[b + 1], OUT)) if b + 1 < blocks else plane[b]
                    for b in range(blocks)
                ]
                for plane in after
            ]
        else:
            source = after
        for p in range(2 * freqs):
            for b in range(blocks):
                keep(z, p, b, source[p][b])


def halo_sides(ra_ref, rb_ref, at, part):
    left, right = from_sides(ra_ref[at, :], rb_ref[at, :], "rec")
    left = jnp.where(has_left("rec"), left, jnp.zeros_like(left))
    right = jnp.where(has_right("rec"), right, jnp.zeros_like(right))
    return (left, HALO + part * MID), (right, -part * MID)


def own_kernel(x_ref, ra_ref, rb_ref, ridx_ref, table_ref, w_ref, a_ref, widx_ref):
    planes, tiles, rows, _ = x_ref.shape
    freqs = planes // 2
    full = rows + 2 * HALO
    blocks = w_ref.shape[1]
    table = table_ref[...]
    entries = table.shape[0]
    left, right = index_sides(ra_ref, rb_ref, freqs * full, "rec")
    widx_ref[...] = jnp.zeros(widx_ref.shape, F32)
    widx_ref[0:DEPTHS, :] = ridx_ref[...].astype(F32)
    own = [widx_ref[:, t * LANES:(t + 1) * LANES] for t in range(tiles)]
    none = jnp.full((8, LANES), -1.0, F32)
    for z in range(DEPTHS):
        before = HALF * (DEPTHS - 1 - z)
        index = []
        for t in range(tiles + 1):
            pieces = []
            if before:
                pieces.append(((left, own[0])[min(t, 1)] if t < 2 else own[t - 1], 0, before))
            if t < tiles:
                pieces.append((own[t], before, before))
            else:
                if before:
                    pieces.append((right, before, before))
                pieces.append((none, 2 * before, 0))
            index.append(join(pieces)[z:z + 1])
        taps = taps_of(index, table, entries)
        for b in range(blocks):
            at = slice(b * OUT, (b + 1) * OUT)
            for f in range(freqs):
                re, im = (
                    skew(taps[at, part * LANES:(part + 1) * LANES]) for part in (2 * f, 2 * f + 1)
                )
                minus, re, im = (-im).astype(BF), re.astype(BF), im.astype(BF)
                for half, (top, low) in enumerate(((re, im), (minus, re))):
                    w_ref[z, b, f, half, 0:OUT, :] = top
                    w_ref[z, b, f, half, OUT:LANES, :] = jnp.zeros((LANES - OUT, LANES), BF)
                    w_ref[z, b, f, half, LANES:, :] = low
    first = []
    for p in range(planes):
        part, f = divmod(p, freqs)
        sides = halo_sides(ra_ref, rb_ref, slice(f * full, f * full + rows), part)
        first.append(windows([x_ref[p, t] for t in range(tiles)], *sides, blocks))

    def keep(z, p, b, value):
        a_ref[z, p, b] = value

    receiver_steps(first, w_ref, freqs, rows, keep)


def last_kernel(
    ma_ref, mb_ref, ra_ref, rb_ref, w_ref, own_ref, near_ref, mid_ref, far_ref, pair_ref,
    final_ref, send_ref, keep_ref, a_ref, part_ref,
):
    _, planes, blocks, rows, _ = own_ref.shape
    freqs = planes // 2
    tiles = pair_ref.shape[1]
    full = rows + 2 * HALO
    first = []
    for p in range(planes):
        part, f = divmod(p, freqs)
        main = []
        for t in range(tiles):
            left, right = from_sides(ma_ref[p, t], mb_ref[p, t], "src")
            left = jnp.where(has_left("src"), left, jnp.zeros_like(left))
            right = jnp.where(has_right("src"), right, jnp.zeros_like(right))
            main.append(jnp.concatenate([left, right], axis=0))
        at = f * full + rows
        sides = []
        for cells, amount in halo_sides(ra_ref, rb_ref, slice(at, at + 2 * HALO), part):
            top = jnp.where(has_left("src"), cells[:HALO], jnp.zeros_like(cells[:HALO]))
            low = jnp.where(has_right("src"), cells[HALO:], jnp.zeros_like(cells[HALO:]))
            sides.append((jnp.concatenate([top, low], axis=0), amount))
        first.append(windows(main, *sides, blocks))

    def keep(z, p, b, value):
        a_ref[z, p, b, 0:HALO] = value[:HALO]
        a_ref[z, p, b, HALO:HALO + rows] = own_ref[z, p, b]
        a_ref[z, p, b, HALO + rows:] = value[HALO:]

    receiver_steps(first, w_ref, freqs, 2 * HALO, keep)

    def field(z, p, b, reach):
        at = slice(HALO - reach, HALO + rows + reach)
        return jnp.concatenate([a_ref[z, p, b, at], a_ref[z, p, b + 1, at]], axis=1)

    images = []
    for z, ref in ((0, near_ref), (1, mid_ref)):
        reach = HALF * (z + 1)
        size = rows + 2 * reach
        out = []
        for b in range(0, blocks, 2):
            total = None
            for f in range(freqs):
                both = jnp.concatenate([field(z, f, b, reach), field(z, freqs + f, b, reach)], axis=0)
                term = dot(ref[f, :, 0:2 * size], both)
                total = term if total is None else total + term
            out += [total[:, :LANES], total[:, LANES:]]
        images.append([gather(out, t * LANES + HALF * (DEPTHS - 1 - z), LANES) for t in range(tiles)])
    real = [None] * tiles
    for f in range(freqs):
        out = []
        for b in range(0, blocks, 2):
            got = dot(far_ref[f, 0][:, :full], field(2, f, b, HALO))
            got += dot(far_ref[f, 1][:, :full], field(2, freqs + f, b, HALO))
            got = got.astype(BF)
            out += [got[:, :LANES], got[:, LANES:]]
        for t in range(tiles):
            both = gather(out, t * LANES)
            final_ref[f, :, t * LANES:(t + 1) * LANES] = both[:rows]
            final_ref[freqs + f, :, t * LANES:(t + 1) * LANES] = both[rows:]
            term = both[:rows].astype(F32)
            real[t] = term if real[t] is None else real[t] + term
    for t in range(tiles):
        value = pair_ref[DEPTHS - 1, t] * real[t]
        for z in range(DEPTHS - 1):
            value += pair_ref[z, t] * images[z][t]
        part_ref[:, t * LANES:(t + 1) * LANES] = value
    count = lax.axis_size("freq")
    share = rows // count
    me = lax.axis_index("freq")
    keep_ref[...] = part_ref[pl.ds(pl.multiple_of(me * share, 8), share), :]
    for j in range(1, count):
        there = partner(me, j, count)
        send_ref[j - 1] = part_ref[pl.ds(pl.multiple_of(there * share, 8), share), :].astype(BF)


def partner(me, j, count):
    if count & (count - 1) == 0:
        return me ^ j
    return (me + j) % count


def local_call(kernel, outs, scratch=(), flops=0, moved=0, vmem=16, **others):
    return pl.pallas_call(
        kernel,
        out_shape=[jax.ShapeDtypeStruct(s, d) for s, d in outs],
        scratch_shapes=[pltpu.VMEM(*s) if isinstance(s, tuple) else s for s in scratch],
        **others,
        compiler_params=pltpu.CompilerParams(vmem_limit_bytes=vmem << 20),
        cost_estimate=pl.CostEstimate(flops=flops, bytes_accessed=moved, transcendentals=0),
    )


def migrate(wave, tap_table, src_index, rec_index, offset_bin, bin_weight):
    freqs, rows, cols = wave.shape[1:]
    planes = 2 * freqs
    tiles = cols // LANES
    entries = tap_table.shape[1]
    count = lax.axis_size("freq")
    share = rows // count
    full = rows + 2 * HALO
    blocks = -(-(cols + 2 * (HALO - HALF)) // OUT)
    table = jnp.transpose(tap_table.astype(BF), (1, 2, 0, 3))
    table = jnp.pad(table, ((0, 0), (0, 0), (0, 0), (0, LANES - TAPS))).reshape(entries, planes * LANES)

    main = ((planes, tiles, HALO, LANES), BF)
    small = ((planes * HALO + IDX_ROWS, LANES), BF)
    inputs = (wave.reshape(planes, rows, cols), src_index, rec_index, offset_bin, bin_weight)
    inputs = tuple(pltpu.with_memory_space_constraint(a, pltpu.HBM) for a in inputs)
    ma, mb, sa, sb, x, src_index, rec_index, offset_bin, bin_weight = local_call(
        load_kernel,
        [main, main, small, small, ((planes, tiles, rows, LANES), BF)] + [(a.shape, a.dtype) for a in inputs[1:]],
        [pltpu.SemaphoreType.DMA((len(inputs) - 1,)), pltpu.SemaphoreType.DMA((planes, tiles))],
        moved=1 << 20,
        in_specs=[pl.BlockSpec(memory_space=pltpu.HBM)] * len(inputs),
    )(*inputs)
    sa, sb = swaps(sa, sb, "src")
    ma, mb = swaps(ma, mb, "src")
    edge = ((freqs * full + IDX_ROWS, LANES), BF)
    ra, rb = local_call(edge_kernel, [edge, edge], moved=1 << 18)(x, rec_index, sa, sb)
    ra, rb = swaps(ra, rb, "rec")

    near, mid, far, pair = local_call(
        source_kernel,
        [
            ((freqs, rows, 2 * LANES), BF),
            ((freqs, rows, 2 * LANES), BF),
            ((freqs, 2, 2 * rows, 2 * LANES), BF),
            ((DEPTHS, tiles, rows, LANES), F32),
        ],
        [((8, LANES), F32), ((8, LANES), F32)],
        flops=1 << 28,
        moved=2 << 20,
    )(sa, sb, src_index, table, offset_bin, bin_weight)
    w, own = local_call(
        own_kernel,
        [
            ((DEPTHS, blocks, freqs, 2, WROWS, LANES), BF),
            ((DEPTHS, planes, blocks, rows, LANES), BF),
        ],
        [((8, cols), F32)],
        flops=1 << 31,
        moved=5 << 20,
    )(x, ra, rb, rec_index, table)
    final, send, keep = local_call(
        last_kernel,
        [((planes, rows, cols), BF), ((max(count - 1, 1), share, cols), BF), ((share, cols), F32)],
        [((DEPTHS, planes, blocks, full, LANES), BF), ((rows, cols), F32)],
        flops=1 << 31,
        moved=8 << 20,
        vmem=24,
    )(ma, mb, ra, rb, w, own, near, mid, far, pair)
    total = keep
    for j in range(1, count):
        got = lax.ppermute(send[j - 1], "freq", [(i, partner(i, j, count)) for i in range(count)])
        total = total + got.astype(F32)
    scale = 1.0 / math.sqrt(freqs * count * DEPTHS)
    return final.reshape(wave.shape), total * scale


def solution(mesh):
    placed = (
        P(None, "freq", "src", "rec"),
        P(None, None, "freq", None),
        P(None, "src"),
        P(None, "rec"),
        P("src", "rec"),
        P(),
    )
    return jax.shard_map(
        migrate,
        mesh=mesh,
        in_specs=placed,
        out_specs=(P(None, "freq", "src", "rec"), P(("src", "freq"), "rec")),
        check_vma=False,
    )
```

```python
import math

import jax
import jax.numpy as jnp
from jax import lax
from jax.experimental import pallas as pl
from jax.experimental.pallas import tpu as pltpu
from jax.sharding import PartitionSpec as P

TAPS = 33
DEPTHS = 3
HALF = TAPS // 2
HALO = DEPTHS * HALF
LANES = 128
MID = LANES // 2
OUT = LANES - 2 * HALF
WROWS = LANES + OUT
IDX_ROWS = 16
BF = jnp.bfloat16
F32 = jnp.float32
NT = (((1,), (1,)), ((), ()))
NN = (((1,), (0,)), ((), ()))
TT = (((0,), (1,)), ((), ()))


def dot(a, b, dims=NN):
    return lax.dot_general(a, b, dims, preferred_element_type=F32)


def pairs_of(axis, odd):
    count, groups = lax.axis_size(axis), lax.axis_size("freq")
    pairs, alone = [], list(range(count))
    for i in range(odd, count - 1, 2):
        alone.remove(i)
        alone.remove(i + 1)
        for g in range(groups):
            pairs += [(i * groups + g, (i + 1) * groups + g), ((i + 1) * groups + g, i * groups + g)]
    for i in alone:
        for g in range(0, groups - 1, 2):
            pairs += [(i * groups + g, i * groups + g + 1), (i * groups + g + 1, i * groups + g)]
    return pairs


def swaps(a, b, axis):
    a = lax.ppermute(a, (axis, "freq"), pairs_of(axis, 0))
    b = lax.ppermute(b, (axis, "freq"), pairs_of(axis, 1))
    return a, b


def is_even(axis):
    return lax.rem(lax.axis_index(axis), 2) == 0


def has_left(axis):
    return lax.axis_index(axis) > 0


def has_right(axis):
    return lax.axis_index(axis) < lax.axis_size(axis) - 1


def lane_of(shape):
    return lax.broadcasted_iota(jnp.int32, shape, len(shape) - 1)


def roll(cells, amount):
    amount = amount % LANES
    return pltpu.roll(cells, amount, 1) if amount else cells


def from_sides(a, b, axis):
    even = is_even(axis)
    return jnp.where(even, b, a), jnp.where(even, a, b)


def join(pieces):
    tile = None
    for cells, start, amount in pieces:
        moved = roll(cells, amount)
        tile = moved if start == 0 else jnp.where(lane_of(moved.shape) < start, tile, moved)
    return tile


def gather(blocks, first, valid=OUT):
    pieces, at = [], 0
    while at < LANES:
        k, lane = divmod(first + at, OUT)
        if k >= len(blocks):
            break
        pieces.append((blocks[k], at, at - lane))
        at += valid - lane
    return join(pieces)


def load_kernel(*refs):
    count = 6
    sources, targets = refs[:count], refs[count + 4:2 * count + 4]
    ma_ref, mb_ref, sa_ref, sb_ref = refs[count:count + 4]
    sem = refs[2 * count + 4]
    copies = [pltpu.make_async_copy(s, t, sem.at[i]) for i, (s, t) in enumerate(zip(sources, targets))]
    for copy in copies:
        copy.start()
    x_ref, sidx_ref = targets[:2]
    planes, rows, cols = x_ref.shape
    even = is_even("src")
    low = rows - HALO
    at_a = pl.multiple_of(jnp.where(even, low, 0), 16)
    at_b = pl.multiple_of(jnp.where(even, 0, low), 16)
    lane = lane_of((HALO, LANES))
    base = planes * HALO
    copies[1].wait()
    index = sidx_ref[...].astype(F32).astype(BF)
    for small in (sa_ref, sb_ref):
        small[base:base + IDX_ROWS, :] = jnp.zeros((IDX_ROWS, LANES), BF)
        small[base:base + DEPTHS, 0:rows] = index
    copies[0].wait()
    for p in range(planes):
        for at, main, small in ((at_a, ma_ref, sa_ref), (at_b, mb_ref, sb_ref)):
            tiles = [x_ref[p, pl.ds(at, HALO), t:t + LANES] for t in range(0, cols, LANES)]
            for t, tile in enumerate(tiles):
                main[p, t] = tile
            small[p * HALO:(p + 1) * HALO, :] = jnp.where(lane < MID, tiles[0], tiles[-1])
    for copy in copies[2:]:
        copy.wait()


def put_edges(ends, at, tail, head):
    lane = lane_of(tail[0].shape)
    right = jnp.where(lane < MID, roll(tail[1], MID), tail[0])
    left = jnp.where(lane < MID, head[0], roll(head[1], MID))
    even = is_even("rec")
    place = slice(at, at + right.shape[0])
    ends[0][place, :] = jnp.where(even, right, left)
    ends[1][place, :] = jnp.where(even, left, right)


def near_kernel(x_ref, ridx_ref, ra_ref, rb_ref):
    planes, rows, cols = x_ref.shape
    freqs = planes // 2
    ends = (ra_ref, rb_ref)
    last = cols - LANES
    for f in range(freqs):
        tail = [x_ref[p, :, last:] for p in (f, freqs + f)]
        head = [x_ref[p, :, :LANES] for p in (f, freqs + f)]
        put_edges(ends, f * rows, tail, head)
    base = freqs * rows
    head = ridx_ref[:, :LANES].astype(F32).astype(BF)
    tail = ridx_ref[:, last:].astype(F32).astype(BF)
    even = is_even("rec")
    for ref, value in zip(ends, (jnp.where(even, tail, head), jnp.where(even, head, tail))):
        ref[base:base + IDX_ROWS, :] = jnp.zeros((IDX_ROWS, LANES), BF)
        ref[base:base + DEPTHS, :] = value


def edge_kernel(sa_ref, sb_ref, ra_ref, rb_ref):
    freqs = ra_ref.shape[0] // (2 * HALO)
    for f in range(freqs):
        for side in range(2):
            both = [side_of(sa_ref, sb_ref, p, side) for p in (f, freqs + f)]
            put_edges((ra_ref, rb_ref), (2 * f + side) * HALO, both, both)


def side_of(a_ref, b_ref, p, side):
    at = slice(p * HALO, (p + 1) * HALO)
    return from_sides(a_ref[at, :], b_ref[at, :], "src")[side]


def index_sides(a_ref, b_ref, base, axis):
    left, right = from_sides(a_ref[base:base + IDX_ROWS, :], b_ref[base:base + IDX_ROWS, :], axis)
    left = jnp.where(has_left(axis), left.astype(F32)[0:8], -1.0)
    right = jnp.where(has_right(axis), right.astype(F32)[0:8], -1.0)
    return left, right


def taps_of(index_tiles, table, entries):
    hot = [
        (lax.broadcasted_iota(jnp.int32, (entries, LANES), 0) == tile.astype(jnp.int32)).astype(F32).astype(BF)
        for tile in index_tiles
    ]
    return dot(hot[0] if len(hot) == 1 else jnp.concatenate(hot, axis=1), table, TT)


def skew(taps):
    return pltpu.roll(taps, 0, 1, stride=1, stride_axis=0)


def source_kernel(
    sa_ref, sb_ref, sidx_ref, taps_ref, bins_ref, weight_ref,
    near_ref, mid_ref, far_ref, pair_ref, table_ref, sx_ref, wt_ref,
):
    rows, cols = bins_ref.shape
    freqs = near_ref.shape[0]
    tiles = cols // LANES
    for f in range(freqs):
        for part in range(2):
            at = (2 * f + part) * LANES
            table_ref[at:at + LANES, :] = jnp.zeros((LANES, table_ref.shape[1]), BF)
            table_ref[at:at + TAPS, :] = taps_ref[part, :, f, :].astype(BF)
    table = table_ref[...]
    entries = table.shape[1]
    wt_ref[...] = jnp.zeros(wt_ref.shape, F32)
    wt_ref[0:DEPTHS, 0:weight_ref.shape[1]] = weight_ref[...]
    for t in range(tiles):
        bins = bins_ref[:, t * LANES:(t + 1) * LANES]
        for z in range(DEPTHS):
            row = jnp.broadcast_to(wt_ref[z:z + 1, :], (rows, LANES))
            pair_ref[z, t] = jnp.take_along_axis(row, bins, axis=1)
    left, right = index_sides(sa_ref, sb_ref, 2 * freqs * HALO, "src")
    sx_ref[...] = jnp.zeros(sx_ref.shape, F32)
    sx_ref[0:DEPTHS, 0:rows] = sidx_ref[...].astype(F32)
    reach = HALO - HALF
    index = join([(left, 0, reach - rows), (sx_ref[...], reach, reach), (right, reach + rows, reach + rows)])
    out = lax.broadcasted_iota(jnp.int32, (LANES, LANES), 0)
    lane = lane_of((LANES, LANES))
    ops = []
    for z in range(DEPTHS):
        taps = taps_of([roll(index, -z * HALF)[z:z + 1]], table, entries)
        found = []
        for part in range(2 * freqs):
            skewed = skew(taps[:, part * LANES:(part + 1) * LANES])
            found.append((jnp.where(lane >= out, skewed, 0.0), jnp.where(lane < out, skewed, 0.0)))
        ops.append(found)
    narrow = lane_of((rows, LANES))
    for f in range(freqs):
        s0 = [[tile.astype(BF) for tile in ops[0][2 * f + part]] for part in range(2)]
        s1 = [ops[1][2 * f + part][0].astype(BF) for part in range(2)]
        s2 = [ops[2][2 * f + part][0][:rows].astype(BF) for part in range(2)]
        got = dot(jnp.concatenate(s2, axis=0), jnp.concatenate(s1, axis=1))
        re = (got[:rows, :LANES] - got[rows:, LANES:]).astype(BF)
        im = (got[:rows, LANES:] + got[rows:, :LANES]).astype(BF)
        stack = jnp.concatenate([re, s1[0][HALF:HALF + rows], im, s1[1][HALF:HALF + rows]], axis=0)
        by_re = dot(stack, jnp.concatenate(s0[0], axis=1))
        by_im = dot(stack, jnp.concatenate(s0[1], axis=1))
        pr = by_re[:2 * rows] - by_im[2 * rows:]
        pi = by_im[:2 * rows] + by_re[2 * rows:]
        size = rows + 2 * HALF
        own = slice(reach, reach + rows)
        parts = [
            join([(ops[0][2 * f + part][0][own], 0, -reach), (ops[0][2 * f + part][1][own], LANES - reach, -reach)])
            for part in range(2)
        ]
        parts = [jnp.where(narrow < size, part, 0.0) for part in parts]
        minus = -parts[1]
        near_ref[f, :, 0:LANES] = jnp.where(narrow < size, parts[0], roll(minus, size)).astype(BF)
        near_ref[f, :, LANES:] = jnp.where(narrow < 2 * size - LANES, roll(minus, size), 0.0).astype(BF)
        mids = [
            join([(g[rows:, :LANES], 0, -HALF), (g[rows:, LANES:], LANES - HALF, -HALF)]) for g in (pr, pi)
        ]
        mid_ref[f, :, 0:LANES] = mids[0].astype(BF)
        mid_ref[f, :, LANES:] = (-mids[1]).astype(BF)
        re, im = pr[:rows].astype(BF), pi[:rows].astype(BF)
        far_ref[f, 0] = jnp.concatenate([re, im], axis=0)
        far_ref[f, 1] = jnp.concatenate([-im, re], axis=0)


def windows(own, left, right, blocks):
    tiles, found = len(own), []
    for b in range(blocks):
        first = b * OUT - HALO
        j, s = divmod(first, LANES)
        pieces = []
        if b == 0:
            pieces = [(left[0], 0, left[1]), (own[0], HALO, HALO)]
        else:
            pieces.append((own[j], 0, -s))
            if s and j + 1 < tiles:
                pieces.append((own[j + 1], LANES - s, -s))
            end = tiles * LANES - first
            if end < LANES:
                pieces.append((right[0], end, end + right[1]))
        found.append(join(pieces))
    return found


def receiver_steps(first, w_ref, freqs, rows, keep):
    source = first
    blocks = len(first[0])
    for z in range(DEPTHS):
        after = [[None] * blocks for _ in range(2 * freqs)]
        for b in range(blocks):
            for f in range(freqs):
                both = jnp.concatenate([source[f][b], source[freqs + f][b]], axis=1)
                w = jnp.concatenate([w_ref[z, b, f, 0], w_ref[z, b, f, 1]], axis=1)
                got = dot(both, w, NT)
                for p, lanes in ((f, got[:, :OUT]), (freqs + f, got[:, LANES:LANES + OUT])):
                    after[p][b] = jnp.concatenate([lanes, jnp.zeros((rows, LANES - OUT), F32)], axis=1).astype(BF)
        if z < DEPTHS - 1:
            lane = lane_of((rows, LANES))
            source = [
                [
                    jnp.where(lane < OUT, plane[b], roll(plane[b + 1], OUT)) if b + 1 < blocks else plane[b]
                    for b in range(blocks)
                ]
                for plane in after
            ]
        else:
            source = after
        for p in range(2 * freqs):
            for b in range(blocks):
                keep(z, p, b, source[p][b])


def halo_sides(ra_ref, rb_ref, at, part):
    left, right = from_sides(ra_ref[at, :], rb_ref[at, :], "rec")
    left = jnp.where(has_left("rec"), left, jnp.zeros_like(left))
    right = jnp.where(has_right("rec"), right, jnp.zeros_like(right))
    return (left, HALO + part * MID), (right, -part * MID)


def own_kernel(x_ref, ra_ref, rb_ref, ridx_ref, table_ref, w_ref, a_ref, widx_ref):
    planes, rows, cols = x_ref.shape
    tiles = cols // LANES
    freqs = planes // 2
    blocks = w_ref.shape[1]
    table = table_ref[...]
    entries = table.shape[1]
    left, right = index_sides(ra_ref, rb_ref, freqs * rows, "rec")
    widx_ref[...] = jnp.zeros(widx_ref.shape, F32)
    widx_ref[0:DEPTHS, :] = ridx_ref[...].astype(F32)
    own = [widx_ref[:, t * LANES:(t + 1) * LANES] for t in range(tiles)]
    none = jnp.full((8, LANES), -1.0, F32)
    for z in range(DEPTHS):
        before = HALF * (DEPTHS - 1 - z)
        index = []
        for t in range(tiles + 1):
            pieces = []
            if before:
                pieces.append(((left, own[0])[min(t, 1)] if t < 2 else own[t - 1], 0, before))
            if t < tiles:
                pieces.append((own[t], before, before))
            else:
                if before:
                    pieces.append((right, before, before))
                pieces.append((none, 2 * before, 0))
            index.append(join(pieces)[z:z + 1])
        taps = taps_of(index, table, entries)
        for b in range(blocks):
            at = slice(b * OUT, (b + 1) * OUT)
            for f in range(freqs):
                re, im = (
                    skew(taps[at, part * LANES:(part + 1) * LANES]) for part in (2 * f, 2 * f + 1)
                )
                minus, re, im = (-im).astype(BF), re.astype(BF), im.astype(BF)
                for half, (top, low) in enumerate(((re, im), (minus, re))):
                    w_ref[z, b, f, half, 0:OUT, :] = top
                    w_ref[z, b, f, half, OUT:LANES, :] = jnp.zeros((LANES - OUT, LANES), BF)
                    w_ref[z, b, f, half, LANES:, :] = low
    first = []
    for p in range(planes):
        part, f = divmod(p, freqs)
        sides = halo_sides(ra_ref, rb_ref, slice(f * rows, (f + 1) * rows), part)
        first.append(windows([x_ref[p, :, t:t + LANES] for t in range(0, cols, LANES)], *sides, blocks))

    def keep(z, p, b, value):
        a_ref[z, p, b] = value

    receiver_steps(first, w_ref, freqs, rows, keep)


def image_kernel(
    ma_ref, mb_ref, ra_ref, rb_ref, w_ref, own_ref, near_ref, mid_ref, far_ref, pair_ref,
    send_ref, keep_ref, deep_ref, a_ref, part_ref,
):
    _, planes, blocks, rows, _ = own_ref.shape
    freqs = planes // 2
    tiles = pair_ref.shape[1]
    full = rows + 2 * HALO
    first = []
    for p in range(planes):
        part, f = divmod(p, freqs)
        main = []
        for t in range(tiles):
            left, right = from_sides(ma_ref[p, t], mb_ref[p, t], "src")
            left = jnp.where(has_left("src"), left, jnp.zeros_like(left))
            right = jnp.where(has_right("src"), right, jnp.zeros_like(right))
            main.append(jnp.concatenate([left, right], axis=0))
        sides = []
        for cells, amount in halo_sides(ra_ref, rb_ref, slice(2 * f * HALO, 2 * (f + 1) * HALO), part):
            top = jnp.where(has_left("src"), cells[:HALO], jnp.zeros_like(cells[:HALO]))
            low = jnp.where(has_right("src"), cells[HALO:], jnp.zeros_like(cells[HALO:]))
            sides.append((jnp.concatenate([top, low], axis=0), amount))
        first.append(windows(main, *sides, blocks))

    def place(z, p, b):
        return deep_ref.at[p, b] if z == DEPTHS - 1 else a_ref.at[z, p, b]

    def keep(z, p, b, value):
        to = place(z, p, b)
        to[0:HALO] = value[:HALO]
        to[HALO:HALO + rows] = own_ref[z, p, b]
        to[HALO + rows:] = value[HALO:]

    receiver_steps(first, w_ref, freqs, 2 * HALO, keep)

    def field(z, p, b, reach):
        at = slice(HALO - reach, HALO + rows + reach)
        return jnp.concatenate([place(z, p, b)[at], place(z, p, b + 1)[at]], axis=1)

    images = []
    for z, ref in ((0, near_ref), (1, mid_ref)):
        reach = HALF * (z + 1)
        size = rows + 2 * reach
        out = []
        for b in range(0, blocks, 2):
            total = None
            for f in range(freqs):
                both = jnp.concatenate([field(z, f, b, reach), field(z, freqs + f, b, reach)], axis=0)
                term = dot(ref[f, :, 0:2 * size], both)
                total = term if total is None else total + term
            out += [total[:, :LANES], total[:, LANES:]]
        images.append([gather(out, t * LANES + HALF * (DEPTHS - 1 - z), LANES) for t in range(tiles)])
    real = [None] * blocks
    for b in range(0, blocks, 2):
        for f in range(freqs):
            got = dot(far_ref[f, 0][:rows, :full], field(2, f, b, HALO))
            got += dot(far_ref[f, 1][:rows, :full], field(2, freqs + f, b, HALO))
            got = got.astype(BF).astype(F32)
            for k in range(2):
                term = got[:, k * LANES:(k + 1) * LANES]
                real[b + k] = term if real[b + k] is None else real[b + k] + term
    real = [gather(real, t * LANES) for t in range(tiles)]
    for t in range(tiles):
        value = pair_ref[DEPTHS - 1, t] * real[t]
        for z in range(DEPTHS - 1):
            value += pair_ref[z, t] * images[z][t]
        part_ref[:, t * LANES:(t + 1) * LANES] = value
    count = lax.axis_size("freq")
    share = rows // count
    me = lax.axis_index("freq")
    keep_ref[...] = part_ref[pl.ds(pl.multiple_of(me * share, 8), share), :]
    for j in range(1, count):
        there = partner(me, j, count)
        send_ref[j - 1] = part_ref[pl.ds(pl.multiple_of(there * share, 8), share), :].astype(BF)


def final_kernel(deep_ref, far_ref, final_ref):
    planes, blocks, full, _ = deep_ref.shape
    _, rows, cols = final_ref.shape
    freqs = planes // 2
    for f in range(freqs):
        out = []
        for b in range(0, blocks, 2):
            parts = [jnp.concatenate([deep_ref[p, b], deep_ref[p, b + 1]], axis=1) for p in (f, freqs + f)]
            got = dot(far_ref[f, 0][:, :full], parts[0]) + dot(far_ref[f, 1][:, :full], parts[1])
            got = got.astype(BF)
            out += [got[:, :LANES], got[:, LANES:]]
        for t in range(0, cols, LANES):
            both = gather(out, t)
            final_ref[f, :, t:t + LANES] = both[:rows]
            final_ref[freqs + f, :, t:t + LANES] = both[rows:]


def partner(me, j, count):
    if count & (count - 1) == 0:
        return me ^ j
    return (me + j) % count


def local_call(kernel, outs, scratch=(), flops=0, moved=0, vmem=16, **others):
    return pl.pallas_call(
        kernel,
        out_shape=[jax.ShapeDtypeStruct(s, d) for s, d in outs],
        scratch_shapes=[pltpu.VMEM(*s) if isinstance(s, tuple) else s for s in scratch],
        **others,
        compiler_params=pltpu.CompilerParams(vmem_limit_bytes=vmem << 20),
        cost_estimate=pl.CostEstimate(flops=flops, bytes_accessed=moved, transcendentals=0),
    )


def migrate(wave, tap_table, src_index, rec_index, offset_bin, bin_weight):
    freqs, rows, cols = wave.shape[1:]
    planes = 2 * freqs
    tiles = cols // LANES
    entries = tap_table.shape[1]
    count = lax.axis_size("freq")
    share = rows // count
    full = rows + 2 * HALO
    blocks = -(-(cols + 2 * (HALO - HALF)) // OUT)

    main = ((planes, tiles, HALO, LANES), BF)
    small = ((planes * HALO + IDX_ROWS, LANES), BF)
    inputs = (wave.reshape(planes, rows, cols), src_index, rec_index, jnp.transpose(tap_table, (0, 3, 2, 1)), offset_bin, bin_weight)
    inputs = tuple(pltpu.with_memory_space_constraint(a, pltpu.HBM) for a in inputs)
    ma, mb, sa, sb, x, src_index, rec_index, tap_table, offset_bin, bin_weight = local_call(
        load_kernel,
        [main, main, small, small] + [(a.shape, a.dtype) for a in inputs],
        [pltpu.SemaphoreType.DMA((len(inputs),))],
        moved=1 << 20,
        in_specs=[pl.BlockSpec(memory_space=pltpu.HBM)] * len(inputs),
    )(*inputs)
    sa, sb = swaps(sa, sb, "src")
    ma, mb = swaps(ma, mb, "src")
    near = ((freqs * rows + IDX_ROWS, LANES), BF)
    ra, rb = local_call(near_kernel, [near, near], moved=1 << 16)(x, rec_index)
    ra, rb = swaps(ra, rb, "rec")
    edge = ((freqs * 2 * HALO, LANES), BF)
    ea, eb = local_call(edge_kernel, [edge, edge], moved=1 << 16)(sa, sb)
    ea, eb = swaps(ea, eb, "rec")

    near, mid, far, pair, table = local_call(
        source_kernel,
        [
            ((freqs, rows, 2 * LANES), BF),
            ((freqs, rows, 2 * LANES), BF),
            ((freqs, 2, 2 * rows, 2 * LANES), BF),
            ((DEPTHS, tiles, rows, LANES), F32),
            ((planes * LANES, entries), BF),
        ],
        [((8, LANES), F32), ((8, LANES), F32)],
        flops=1 << 28,
        moved=2 << 20,
    )(sa, sb, src_index, tap_table, offset_bin, bin_weight)
    w, own = local_call(
        own_kernel,
        [
            ((DEPTHS, blocks, freqs, 2, WROWS, LANES), BF),
            ((DEPTHS, planes, blocks, rows, LANES), BF),
        ],
        [((8, cols), F32)],
        flops=1 << 31,
        moved=5 << 20,
    )(x, ra, rb, rec_index, table)
    send, keep, deep = local_call(
        image_kernel,
        [
            ((max(count - 1, 1), share, cols), BF),
            ((share, cols), F32),
            ((planes, blocks, full, LANES), BF),
        ],
        [((DEPTHS - 1, planes, blocks, full, LANES), BF), ((rows, cols), F32)],
        flops=1 << 31,
        moved=8 << 20,
        vmem=24,
    )(ma, mb, ea, eb, w, own, near, mid, far, pair)
    total = keep
    for j in range(1, count):
        got = lax.ppermute(send[j - 1], "freq", [(i, partner(i, j, count)) for i in range(count)])
        total = total + got.astype(F32)
    (final,) = local_call(final_kernel, [((planes, rows, cols), BF)], flops=1 << 28, moved=1 << 20)(deep, far)
    scale = 1.0 / math.sqrt(freqs * count * DEPTHS)
    return final.reshape(wave.shape), total * scale


def solution(mesh):
    placed = (
        P(None, "freq", "src", "rec"),
        P(None, None, "freq", None),
        P(None, "src"),
        P(None, "rec"),
        P("src", "rec"),
        P(),
    )
    return jax.shard_map(
        migrate,
        mesh=mesh,
        in_specs=placed,
        out_specs=(P(None, "freq", "src", "rec"), P(("src", "freq"), "rec")),
        check_vma=False,
    )
```

```python
import functools
import math

import jax
import jax.numpy as jnp
from jax import lax
from jax.experimental import pallas as pl
from jax.experimental.pallas import tpu as pltpu
from jax.sharding import PartitionSpec as P

TAPS = 33
DEPTHS = 3
HALF = TAPS // 2
HALO = DEPTHS * HALF
LANES = 128
MID = LANES // 2
OUT = LANES - 2 * HALF
WROWS = LANES + OUT
IDX_ROWS = 16
BF = jnp.bfloat16
F32 = jnp.float32
NT = (((1,), (1,)), ((), ()))
NN = (((1,), (0,)), ((), ()))
TT = (((0,), (1,)), ((), ()))


def dot(a, b, dims=NN):
    return lax.dot_general(a, b, dims, preferred_element_type=F32)


def pairs_of(axis, odd):
    count, groups = lax.axis_size(axis), lax.axis_size("freq")
    pairs, alone = [], list(range(count))
    for i in range(odd, count - 1, 2):
        alone.remove(i)
        alone.remove(i + 1)
        for g in range(groups):
            pairs += [(i * groups + g, (i + 1) * groups + g), ((i + 1) * groups + g, i * groups + g)]
    for i in alone:
        for g in range(0, groups - 1, 2):
            pairs += [(i * groups + g, i * groups + g + 1), (i * groups + g + 1, i * groups + g)]
    return pairs


def swaps(a, b, axis):
    a = lax.ppermute(a, (axis, "freq"), pairs_of(axis, 0))
    b = lax.ppermute(b, (axis, "freq"), pairs_of(axis, 1))
    return a, b


def is_even(axis):
    return lax.rem(lax.axis_index(axis), 2) == 0


def has_left(axis):
    return lax.axis_index(axis) > 0


def has_right(axis):
    return lax.axis_index(axis) < lax.axis_size(axis) - 1


def lane_of(shape):
    return lax.broadcasted_iota(jnp.int32, shape, len(shape) - 1)


def roll(cells, amount):
    amount = amount % LANES
    return pltpu.roll(cells, amount, 1) if amount else cells


def from_sides(a, b, axis):
    even = is_even(axis)
    return jnp.where(even, b, a), jnp.where(even, a, b)


def join(pieces):
    tile = None
    for cells, start, amount in pieces:
        moved = roll(cells, amount)
        tile = moved if start == 0 else jnp.where(lane_of(moved.shape) < start, tile, moved)
    return tile


def gather(blocks, first, valid=OUT):
    pieces, at = [], 0
    while at < LANES:
        k, lane = divmod(first + at, OUT)
        if k >= len(blocks):
            break
        pieces.append((blocks[k], at, at - lane))
        at += valid - lane
    return join(pieces)


def load_kernel(*refs):
    count = 6
    sources, targets = refs[:count], refs[count + 4:2 * count + 4]
    ma_ref, mb_ref, sa_ref, sb_ref = refs[count:count + 4]
    sem = refs[2 * count + 4]
    copies = [pltpu.make_async_copy(s, t, sem.at[i]) for i, (s, t) in enumerate(zip(sources, targets))]
    for copy in copies:
        copy.start()
    x_ref, sidx_ref = targets[:2]
    planes, rows, cols = x_ref.shape
    even = is_even("src")
    low = rows - HALO
    at_a = pl.multiple_of(jnp.where(even, low, 0), 16)
    at_b = pl.multiple_of(jnp.where(even, 0, low), 16)
    lane = lane_of((HALO, LANES))
    base = planes * HALO
    copies[1].wait()
    index = sidx_ref[...].astype(F32).astype(BF)
    for small in (sa_ref, sb_ref):
        small[base:base + IDX_ROWS, :] = jnp.zeros((IDX_ROWS, LANES), BF)
        small[base:base + DEPTHS, 0:rows] = index
    copies[0].wait()
    for p in range(planes):
        for at, main, small in ((at_a, ma_ref, sa_ref), (at_b, mb_ref, sb_ref)):
            tiles = [x_ref[p, pl.ds(at, HALO), t:t + LANES] for t in range(0, cols, LANES)]
            main[p, 0] = jnp.where(lane < MID, tiles[-1], tiles[0])
            for t, tile in enumerate(tiles[1:-1]):
                main[p, t + 1] = tile
            small[p * HALO:(p + 1) * HALO, :] = jnp.where(lane < MID, tiles[0], tiles[-1])
    for copy in copies[2:]:
        copy.wait()


def put_edges(ends, at, tail, head):
    lane = lane_of(tail[0].shape)
    right = jnp.where(lane < MID, roll(tail[1], MID), tail[0])
    left = jnp.where(lane < MID, head[0], roll(head[1], MID))
    even = is_even("rec")
    place = slice(at, at + right.shape[0])
    ends[0][place, :] = jnp.where(even, right, left)
    ends[1][place, :] = jnp.where(even, left, right)


def near_kernel(x_ref, ridx_ref, ra_ref, rb_ref):
    planes, rows, cols = x_ref.shape
    freqs = planes // 2
    ends = (ra_ref, rb_ref)
    last = cols - LANES
    for f in range(freqs):
        tail = [x_ref[p, :, last:] for p in (f, freqs + f)]
        head = [x_ref[p, :, :LANES] for p in (f, freqs + f)]
        put_edges(ends, f * rows, tail, head)
    base = freqs * rows
    head = ridx_ref[:, :LANES].astype(F32).astype(BF)
    tail = ridx_ref[:, last:].astype(F32).astype(BF)
    even = is_even("rec")
    for ref, value in zip(ends, (jnp.where(even, tail, head), jnp.where(even, head, tail))):
        ref[base:base + IDX_ROWS, :] = jnp.zeros((IDX_ROWS, LANES), BF)
        ref[base:base + DEPTHS, :] = value


def edge_kernel(sa_ref, sb_ref, ra_ref, rb_ref):
    freqs = ra_ref.shape[0] // (2 * HALO)
    for f in range(freqs):
        for side in range(2):
            both = [side_of(sa_ref, sb_ref, p, side) for p in (f, freqs + f)]
            put_edges((ra_ref, rb_ref), (2 * f + side) * HALO, both, both)


def side_of(a_ref, b_ref, p, side):
    at = slice(p * HALO, (p + 1) * HALO)
    return from_sides(a_ref[at, :], b_ref[at, :], "src")[side]


def index_sides(a_ref, b_ref, base, axis):
    left, right = from_sides(a_ref[base:base + IDX_ROWS, :], b_ref[base:base + IDX_ROWS, :], axis)
    left = jnp.where(has_left(axis), left.astype(F32)[0:8], -1.0)
    right = jnp.where(has_right(axis), right.astype(F32)[0:8], -1.0)
    return left, right


def taps_of(index_tiles, table, entries):
    hot = [
        (lax.broadcasted_iota(jnp.int32, (entries, LANES), 0) == tile.astype(jnp.int32)).astype(F32).astype(BF)
        for tile in index_tiles
    ]
    return dot(hot[0] if len(hot) == 1 else jnp.concatenate(hot, axis=1), table, TT)


def skew(taps):
    return pltpu.roll(taps, 0, 1, stride=1, stride_axis=0)


def block_places(cols, blocks):
    places, counts = {}, [0, 0]
    for z in range(DEPTHS):
        before = HALF * (DEPTHS - 1 - z)
        for b in range(blocks):
            outside = b * OUT < before or (before > 0 and (b + 1) * OUT - before > cols)
            places[z, b] = (outside, counts[outside])
            counts[outside] += 1
    return places, counts


def index_window(own, left, right, z, b):
    before = HALF * (DEPTHS - 1 - z)
    first = b * OUT - before
    tiles = len(own)
    j, s = divmod(first, LANES)
    pieces = [(left if j < 0 else own[j], 0, -s)]
    if s and j + 1 < tiles:
        pieces.append((own[j + 1], LANES - s, -s))
    end = tiles * LANES - first
    if end < LANES:
        if before:
            pieces.append((right, end, end))
        pieces.append((jnp.full((8, LANES), -1.0, F32), end + before, 0))
    return join(pieces)[z:z + 1]


def put_operators(outside, own, left, right, table, w_ref, cols, blocks):
    places, _ = block_places(cols, blocks)
    for z in range(DEPTHS):
        mine = [b for b in range(blocks) if places[z, b][0] == outside]
        if not mine:
            continue
        taps = taps_of([index_window(own, left, right, z, b) for b in mine], table, table.shape[1])
        for i, b in enumerate(mine):
            place = places[z, b][1]
            at = slice(i * LANES, i * LANES + OUT)
            for f in range(w_ref.shape[1]):
                re, im = (skew(taps[at, part * LANES:(part + 1) * LANES]) for part in (2 * f, 2 * f + 1))
                minus, re, im = (-im).astype(BF), re.astype(BF), im.astype(BF)
                for half, (top, low) in enumerate(((re, im), (minus, re))):
                    w_ref[place, f, half, 0:OUT, :] = top
                    w_ref[place, f, half, OUT:LANES, :] = jnp.zeros((LANES - OUT, LANES), BF)
                    w_ref[place, f, half, LANES:, :] = low


def wide_index(ridx_ref, widx_ref):
    widx_ref[...] = jnp.zeros(widx_ref.shape, F32)
    widx_ref[0:DEPTHS, :] = ridx_ref[...].astype(F32)
    return [widx_ref[:, t:t + LANES] for t in range(0, widx_ref.shape[1], LANES)]


def prep_kernel(blocks, taps_ref, ridx_ref, bins_ref, weight_ref, table_ref, pair_ref, w_ref, widx_ref, wt_ref):
    rows, cols = bins_ref.shape
    freqs = w_ref.shape[1]
    tiles = cols // LANES
    for f in range(freqs):
        for part in range(2):
            at = (2 * f + part) * LANES
            table_ref[at:at + LANES, :] = jnp.zeros((LANES, table_ref.shape[1]), BF)
            table_ref[at:at + TAPS, :] = taps_ref[part, :, f, :].astype(BF)
    wt_ref[...] = jnp.zeros(wt_ref.shape, F32)
    wt_ref[0:DEPTHS, 0:weight_ref.shape[1]] = weight_ref[...]
    for t in range(tiles):
        bins = bins_ref[:, t * LANES:(t + 1) * LANES]
        for z in range(DEPTHS):
            row = jnp.broadcast_to(wt_ref[z:z + 1, :], (rows, LANES))
            pair_ref[z, t] = jnp.take_along_axis(row, bins, axis=1)
    own = wide_index(ridx_ref, widx_ref)
    put_operators(False, own, None, None, table_ref[...], w_ref, cols, blocks)


def source_kernel(sa_ref, sb_ref, sidx_ref, table_ref, near_ref, mid_ref, far_ref, sx_ref):
    freqs, rows, _ = near_ref.shape
    table = table_ref[...]
    entries = table.shape[1]
    left, right = index_sides(sa_ref, sb_ref, 2 * freqs * HALO, "src")
    sx_ref[...] = jnp.zeros(sx_ref.shape, F32)
    sx_ref[0:DEPTHS, 0:rows] = sidx_ref[...].astype(F32)
    reach = HALO - HALF
    index = join([(left, 0, reach - rows), (sx_ref[...], reach, reach), (right, reach + rows, reach + rows)])
    out = lax.broadcasted_iota(jnp.int32, (LANES, LANES), 0)
    lane = lane_of((LANES, LANES))
    ops = []
    for z in range(DEPTHS):
        taps = taps_of([roll(index, -z * HALF)[z:z + 1]], table, entries)
        found = []
        for part in range(2 * freqs):
            skewed = skew(taps[:, part * LANES:(part + 1) * LANES])
            found.append((jnp.where(lane >= out, skewed, 0.0), jnp.where(lane < out, skewed, 0.0)))
        ops.append(found)
    narrow = lane_of((rows, LANES))
    for f in range(freqs):
        s0 = [[tile.astype(BF) for tile in ops[0][2 * f + part]] for part in range(2)]
        s1 = [ops[1][2 * f + part][0].astype(BF) for part in range(2)]
        s2 = [ops[2][2 * f + part][0][:rows].astype(BF) for part in range(2)]
        got = dot(jnp.concatenate(s2, axis=0), jnp.concatenate(s1, axis=1))
        re = (got[:rows, :LANES] - got[rows:, LANES:]).astype(BF)
        im = (got[:rows, LANES:] + got[rows:, :LANES]).astype(BF)
        stack = jnp.concatenate([re, s1[0][HALF:HALF + rows], im, s1[1][HALF:HALF + rows]], axis=0)
        by_re = dot(stack, jnp.concatenate(s0[0], axis=1))
        by_im = dot(stack, jnp.concatenate(s0[1], axis=1))
        pr = by_re[:2 * rows] - by_im[2 * rows:]
        pi = by_im[:2 * rows] + by_re[2 * rows:]
        size = rows + 2 * HALF
        own = slice(reach, reach + rows)
        parts = [
            join([(ops[0][2 * f + part][0][own], 0, -reach), (ops[0][2 * f + part][1][own], LANES - reach, -reach)])
            for part in range(2)
        ]
        parts = [jnp.where(narrow < size, part, 0.0) for part in parts]
        minus = -parts[1]
        near_ref[f, :, 0:LANES] = jnp.where(narrow < size, parts[0], roll(minus, size)).astype(BF)
        near_ref[f, :, LANES:] = jnp.where(narrow < 2 * size - LANES, roll(minus, size), 0.0).astype(BF)
        mids = [
            join([(g[rows:, :LANES], 0, -HALF), (g[rows:, LANES:], LANES - HALF, -HALF)]) for g in (pr, pi)
        ]
        mid_ref[f, :, 0:LANES] = mids[0].astype(BF)
        mid_ref[f, :, LANES:] = (-mids[1]).astype(BF)
        re, im = pr[:rows].astype(BF), pi[:rows].astype(BF)
        far_ref[f, 0] = jnp.concatenate([re, im], axis=0)
        far_ref[f, 1] = jnp.concatenate([-im, re], axis=0)


def windows(own, left, right, blocks):
    tiles, found = len(own), []
    for b in range(blocks):
        first = b * OUT - HALO
        j, s = divmod(first, LANES)
        pieces = []
        if b == 0:
            pieces = [(left[0], 0, left[1]), (own[0], HALO, HALO)]
        else:
            pieces.append((own[j], 0, -s))
            if s and j + 1 < tiles:
                pieces.append((own[j + 1], LANES - s, -s))
            end = tiles * LANES - first
            if end < LANES:
                pieces.append((right[0], end, end + right[1]))
        found.append(join(pieces))
    return found


def receiver_steps(first, w_refs, freqs, rows, cols, keep):
    places, _ = block_places(cols, len(first[0]))
    source = first
    blocks = len(first[0])
    for z in range(DEPTHS):
        after = [[None] * blocks for _ in range(2 * freqs)]
        for b in range(blocks):
            for f in range(freqs):
                both = jnp.concatenate([source[f][b], source[freqs + f][b]], axis=1)
                outside, place = places[z, b]
                w = jnp.concatenate([w_refs[outside][place, f, half] for half in range(2)], axis=1)
                got = dot(both, w, NT)
                for p, lanes in ((f, got[:, :OUT]), (freqs + f, got[:, LANES:LANES + OUT])):
                    after[p][b] = jnp.concatenate([lanes, jnp.zeros((rows, LANES - OUT), F32)], axis=1).astype(BF)
        if z < DEPTHS - 1:
            lane = lane_of((rows, LANES))
            source = [
                [
                    jnp.where(lane < OUT, plane[b], roll(plane[b + 1], OUT)) if b + 1 < blocks else plane[b]
                    for b in range(blocks)
                ]
                for plane in after
            ]
        else:
            source = after
        for p in range(2 * freqs):
            for b in range(blocks):
                keep(z, p, b, source[p][b])


def halo_sides(ra_ref, rb_ref, at, part):
    left, right = from_sides(ra_ref[at, :], rb_ref[at, :], "rec")
    left = jnp.where(has_left("rec"), left, jnp.zeros_like(left))
    right = jnp.where(has_right("rec"), right, jnp.zeros_like(right))
    return (left, HALO + part * MID), (right, -part * MID)


def own_kernel(x_ref, ra_ref, rb_ref, ridx_ref, table_ref, wi_ref, wo_ref, a_ref, widx_ref):
    planes, rows, cols = x_ref.shape
    freqs = planes // 2
    blocks = a_ref.shape[2]
    left, right = index_sides(ra_ref, rb_ref, freqs * rows, "rec")
    own = wide_index(ridx_ref, widx_ref)
    put_operators(True, own, left, right, table_ref[...], wo_ref, cols, blocks)
    first = []
    for p in range(planes):
        part, f = divmod(p, freqs)
        sides = halo_sides(ra_ref, rb_ref, slice(f * rows, (f + 1) * rows), part)
        first.append(windows([x_ref[p, :, t:t + LANES] for t in range(0, cols, LANES)], *sides, blocks))

    def keep(z, p, b, value):
        a_ref[z, p, b] = value

    receiver_steps(first, (wi_ref, wo_ref), freqs, rows, cols, keep)


def image_kernel(
    ma_ref, mb_ref, sa_ref, sb_ref, ra_ref, rb_ref, wi_ref, wo_ref, own_ref, near_ref, mid_ref, far_ref, pair_ref,
    send_ref, keep_ref, deep_ref, a_ref, part_ref,
):
    _, planes, blocks, rows, _ = own_ref.shape
    freqs = planes // 2
    tiles = pair_ref.shape[1]
    full = rows + 2 * HALO
    first = []
    for p in range(planes):
        part, f = divmod(p, freqs)
        at = slice(p * HALO, (p + 1) * HALO)
        parts = [(sa_ref[at, :], sb_ref[at, :])] + [(ma_ref[p, t], mb_ref[p, t]) for t in range(tiles - 1)]
        main = []
        for a, b in parts:
            left, right = from_sides(a, b, "src")
            left = jnp.where(has_left("src"), left, jnp.zeros_like(left))
            right = jnp.where(has_right("src"), right, jnp.zeros_like(right))
            main.append(jnp.concatenate([left, right], axis=0))
        ends, mixed = main[:2]
        lane = lane_of(ends.shape)
        main = [jnp.where(lane < MID, ends, mixed)] + main[2:] + [jnp.where(lane < MID, mixed, ends)]
        sides = []
        for cells, amount in halo_sides(ra_ref, rb_ref, slice(2 * f * HALO, 2 * (f + 1) * HALO), part):
            top = jnp.where(has_left("src"), cells[:HALO], jnp.zeros_like(cells[:HALO]))
            low = jnp.where(has_right("src"), cells[HALO:], jnp.zeros_like(cells[HALO:]))
            sides.append((jnp.concatenate([top, low], axis=0), amount))
        first.append(windows(main, *sides, blocks))

    def place(z, p, b):
        return deep_ref.at[p, b] if z == DEPTHS - 1 else a_ref.at[z, p, b]

    def keep(z, p, b, value):
        to = place(z, p, b)
        to[0:HALO] = value[:HALO]
        to[HALO:HALO + rows] = own_ref[z, p, b]
        to[HALO + rows:] = value[HALO:]

    receiver_steps(first, (wi_ref, wo_ref), freqs, 2 * HALO, tiles * LANES, keep)

    def field(z, p, b, reach):
        at = slice(HALO - reach, HALO + rows + reach)
        return jnp.concatenate([place(z, p, b)[at], place(z, p, b + 1)[at]], axis=1)

    images = []
    for z, ref in ((0, near_ref), (1, mid_ref)):
        reach = HALF * (z + 1)
        size = rows + 2 * reach
        out = []
        for b in range(0, blocks, 2):
            total = None
            for f in range(freqs):
                both = jnp.concatenate([field(z, f, b, reach), field(z, freqs + f, b, reach)], axis=0)
                term = dot(ref[f, :, 0:2 * size], both)
                total = term if total is None else total + term
            out += [total[:, :LANES], total[:, LANES:]]
        images.append([gather(out, t * LANES + HALF * (DEPTHS - 1 - z), LANES) for t in range(tiles)])
    real = [None] * blocks
    for b in range(0, blocks, 2):
        for f in range(freqs):
            got = dot(far_ref[f, 0][:rows, :full], field(2, f, b, HALO))
            got += dot(far_ref[f, 1][:rows, :full], field(2, freqs + f, b, HALO))
            got = got.astype(BF).astype(F32)
            for k in range(2):
                term = got[:, k * LANES:(k + 1) * LANES]
                real[b + k] = term if real[b + k] is None else real[b + k] + term
    real = [gather(real, t * LANES) for t in range(tiles)]
    for t in range(tiles):
        value = pair_ref[DEPTHS - 1, t] * real[t]
        for z in range(DEPTHS - 1):
            value += pair_ref[z, t] * images[z][t]
        part_ref[:, t * LANES:(t + 1) * LANES] = value
    count = lax.axis_size("freq")
    share = rows // count
    me = lax.axis_index("freq")
    keep_ref[...] = part_ref[pl.ds(pl.multiple_of(me * share, 8), share), :]
    for j in range(1, count):
        there = partner(me, j, count)
        send_ref[j - 1] = part_ref[pl.ds(pl.multiple_of(there * share, 8), share), :].astype(BF)


def final_kernel(deep_ref, far_ref, final_ref):
    planes, blocks, full, _ = deep_ref.shape
    _, rows, cols = final_ref.shape
    freqs = planes // 2
    for f in range(freqs):
        out = []
        for b in range(0, blocks, 2):
            parts = [jnp.concatenate([deep_ref[p, b], deep_ref[p, b + 1]], axis=1) for p in (f, freqs + f)]
            got = dot(far_ref[f, 0][:, :full], parts[0]) + dot(far_ref[f, 1][:, :full], parts[1])
            got = got.astype(BF)
            out += [got[:, :LANES], got[:, LANES:]]
        for t in range(0, cols, LANES):
            both = gather(out, t)
            final_ref[f, :, t:t + LANES] = both[:rows]
            final_ref[freqs + f, :, t:t + LANES] = both[rows:]


def partner(me, j, count):
    if count & (count - 1) == 0:
        return me ^ j
    return (me + j) % count


def local_call(kernel, outs, scratch=(), flops=0, moved=0, vmem=16, **others):
    return pl.pallas_call(
        kernel,
        out_shape=[jax.ShapeDtypeStruct(s, d) for s, d in outs],
        scratch_shapes=[pltpu.VMEM(*s) if isinstance(s, tuple) else s for s in scratch],
        **others,
        compiler_params=pltpu.CompilerParams(vmem_limit_bytes=vmem << 20),
        cost_estimate=pl.CostEstimate(flops=flops, bytes_accessed=moved, transcendentals=0),
    )


def migrate(wave, tap_table, src_index, rec_index, offset_bin, bin_weight):
    freqs, rows, cols = wave.shape[1:]
    planes = 2 * freqs
    tiles = cols // LANES
    entries = tap_table.shape[1]
    count = lax.axis_size("freq")
    share = rows // count
    full = rows + 2 * HALO
    blocks = -(-(cols + 2 * (HALO - HALF)) // OUT)

    main = ((planes, tiles - 1, HALO, LANES), BF)
    small = ((planes * HALO + IDX_ROWS, LANES), BF)
    inputs = (wave.reshape(planes, rows, cols), src_index, rec_index, jnp.transpose(tap_table, (0, 3, 2, 1)), offset_bin, bin_weight)
    inputs = tuple(pltpu.with_memory_space_constraint(a, pltpu.HBM) for a in inputs)
    ma, mb, sa, sb, x, src_index, rec_index, tap_table, offset_bin, bin_weight = local_call(
        load_kernel,
        [main, main, small, small] + [(a.shape, a.dtype) for a in inputs],
        [pltpu.SemaphoreType.DMA((len(inputs),))],
        moved=1 << 20,
        in_specs=[pl.BlockSpec(memory_space=pltpu.HBM)] * len(inputs),
    )(*inputs)
    sa, sb = swaps(sa, sb, "src")
    ma, mb = swaps(ma, mb, "src")
    near = ((freqs * rows + IDX_ROWS, LANES), BF)
    ra, rb = local_call(near_kernel, [near, near], moved=1 << 16)(x, rec_index)
    ra, rb = swaps(ra, rb, "rec")
    edge = ((freqs * 2 * HALO, LANES), BF)
    ea, eb = local_call(edge_kernel, [edge, edge], moved=1 << 16)(sa, sb)
    ea, eb = swaps(ea, eb, "rec")

    _, (inner, outer) = block_places(cols, blocks)
    table, pair, wi = local_call(
        functools.partial(prep_kernel, blocks),
        [((planes * LANES, entries), BF), ((DEPTHS, tiles, rows, LANES), F32), ((inner, freqs, 2, WROWS, LANES), BF)],
        [((8, cols), F32), ((8, LANES), F32)],
        flops=1 << 28,
        moved=4 << 20,
    )(tap_table, rec_index, offset_bin, bin_weight)
    near, mid, far = local_call(
        source_kernel,
        [
            ((freqs, rows, 2 * LANES), BF),
            ((freqs, rows, 2 * LANES), BF),
            ((freqs, 2, 2 * rows, 2 * LANES), BF),
        ],
        [((8, LANES), F32)],
        flops=1 << 28,
        moved=1 << 20,
    )(sa, sb, src_index, table)
    wo, own = local_call(
        own_kernel,
        [
            ((outer, freqs, 2, WROWS, LANES), BF),
            ((DEPTHS, planes, blocks, rows, LANES), BF),
        ],
        [((8, cols), F32)],
        flops=1 << 31,
        moved=5 << 20,
    )(x, ra, rb, rec_index, table, wi)
    send, keep, deep = local_call(
        image_kernel,
        [
            ((max(count - 1, 1), share, cols), BF),
            ((share, cols), F32),
            ((planes, blocks, full, LANES), BF),
        ],
        [((DEPTHS - 1, planes, blocks, full, LANES), BF), ((rows, cols), F32)],
        flops=1 << 31,
        moved=8 << 20,
        vmem=24,
    )(ma, mb, sa, sb, ea, eb, wi, wo, own, near, mid, far, pair)
    total = keep
    for j in range(1, count):
        got = lax.ppermute(send[j - 1], "freq", [(i, partner(i, j, count)) for i in range(count)])
        total = total + got.astype(F32)
    (final,) = local_call(final_kernel, [((planes, rows, cols), BF)], flops=1 << 28, moved=1 << 20)(deep, far)
    scale = 1.0 / math.sqrt(freqs * count * DEPTHS)
    return final.reshape(wave.shape), total * scale


def solution(mesh):
    placed = (
        P(None, "freq", "src", "rec"),
        P(None, None, "freq", None),
        P(None, "src"),
        P(None, "rec"),
        P("src", "rec"),
        P(),
    )
    return jax.shard_map(
        migrate,
        mesh=mesh,
        in_specs=placed,
        out_specs=(P(None, "freq", "src", "rec"), P(("src", "freq"), "rec")),
        check_vma=False,
    )
```

```python
import math

import jax
import jax.numpy as jnp
from jax import lax
from jax.experimental import pallas as pl
from jax.experimental.pallas import tpu as pltpu
from jax.sharding import PartitionSpec as P

TAPS = 33
DEPTHS = 3
HALF = TAPS // 2
HALO = DEPTHS * HALF
LANES = 128
MID = LANES // 2
OUT = LANES - 2 * HALF
WROWS = LANES + OUT
IDX_ROWS = 16
BF = jnp.bfloat16
F32 = jnp.float32
NT = (((1,), (1,)), ((), ()))
NN = (((1,), (0,)), ((), ()))
TT = (((0,), (1,)), ((), ()))


def dot(a, b, dims=NN):
    return lax.dot_general(a, b, dims, preferred_element_type=F32)


def pairs_of(axis, odd):
    count, groups = lax.axis_size(axis), lax.axis_size("freq")
    pairs, alone = [], list(range(count))
    for i in range(odd, count - 1, 2):
        alone.remove(i)
        alone.remove(i + 1)
        for g in range(groups):
            pairs += [(i * groups + g, (i + 1) * groups + g), ((i + 1) * groups + g, i * groups + g)]
    for i in alone:
        for g in range(0, groups - 1, 2):
            pairs += [(i * groups + g, i * groups + g + 1), (i * groups + g + 1, i * groups + g)]
    return pairs


def swaps(a, b, axis):
    a = lax.ppermute(a, (axis, "freq"), pairs_of(axis, 0))
    b = lax.ppermute(b, (axis, "freq"), pairs_of(axis, 1))
    return a, b


def is_even(axis):
    return lax.rem(lax.axis_index(axis), 2) == 0


def has_left(axis):
    return lax.axis_index(axis) > 0


def has_right(axis):
    return lax.axis_index(axis) < lax.axis_size(axis) - 1


def lane_of(shape):
    return lax.broadcasted_iota(jnp.int32, shape, len(shape) - 1)


def roll(cells, amount):
    amount = amount % LANES
    return pltpu.roll(cells, amount, 1) if amount else cells


def from_sides(a, b, axis):
    even = is_even(axis)
    return jnp.where(even, b, a), jnp.where(even, a, b)


def join(pieces):
    tile = None
    for cells, start, amount in pieces:
        moved = roll(cells, amount)
        tile = moved if start == 0 else jnp.where(lane_of(moved.shape) < start, tile, moved)
    return tile


def gather(blocks, first, valid=OUT):
    pieces, at = [], 0
    while at < LANES:
        k, lane = divmod(first + at, OUT)
        if k >= len(blocks):
            break
        pieces.append((blocks[k], at, at - lane))
        at += valid - lane
    return join(pieces)


def load_kernel(*refs):
    count = 6
    sources, targets = refs[:count], refs[count + 4:2 * count + 4]
    ma_ref, mb_ref, sa_ref, sb_ref = refs[count:count + 4]
    sem = refs[2 * count + 4]
    copies = [pltpu.make_async_copy(s, t, sem.at[i]) for i, (s, t) in enumerate(zip(sources, targets))]
    for copy in copies:
        copy.start()
    x_ref, sidx_ref = targets[:2]
    planes, rows, cols = x_ref.shape
    even = is_even("src")
    low = rows - HALO
    at_a = pl.multiple_of(jnp.where(even, low, 0), 16)
    at_b = pl.multiple_of(jnp.where(even, 0, low), 16)
    lane = lane_of((HALO, LANES))
    base = planes * HALO
    copies[1].wait()
    index = sidx_ref[...].astype(F32).astype(BF)
    for small in (sa_ref, sb_ref):
        small[base:base + IDX_ROWS, :] = jnp.zeros((IDX_ROWS, LANES), BF)
        small[base:base + DEPTHS, 0:rows] = index
    copies[0].wait()
    for p in range(planes):
        for at, main, small in ((at_a, ma_ref, sa_ref), (at_b, mb_ref, sb_ref)):
            tiles = [x_ref[p, pl.ds(at, HALO), t:t + LANES] for t in range(0, cols, LANES)]
            main[p, 0] = jnp.where(lane < MID, tiles[-1], tiles[0])
            for t, tile in enumerate(tiles[1:-1]):
                main[p, t + 1] = tile
            small[p * HALO:(p + 1) * HALO, :] = jnp.where(lane < MID, tiles[0], tiles[-1])
    for copy in copies[2:]:
        copy.wait()


def put_edges(ends, at, tail, head):
    lane = lane_of(tail[0].shape)
    right = jnp.where(lane < MID, roll(tail[1], MID), tail[0])
    left = jnp.where(lane < MID, head[0], roll(head[1], MID))
    even = is_even("rec")
    place = slice(at, at + right.shape[0])
    ends[0][place, :] = jnp.where(even, right, left)
    ends[1][place, :] = jnp.where(even, left, right)


def near_kernel(x_ref, ridx_ref, ra_ref, rb_ref):
    planes, rows, cols = x_ref.shape
    freqs = planes // 2
    ends = (ra_ref, rb_ref)
    last = cols - LANES
    for f in range(freqs):
        tail = [x_ref[p, :, last:] for p in (f, freqs + f)]
        head = [x_ref[p, :, :LANES] for p in (f, freqs + f)]
        put_edges(ends, f * rows, tail, head)
    base = freqs * rows
    head = ridx_ref[:, :LANES].astype(F32).astype(BF)
    tail = ridx_ref[:, last:].astype(F32).astype(BF)
    even = is_even("rec")
    for ref, value in zip(ends, (jnp.where(even, tail, head), jnp.where(even, head, tail))):
        ref[base:base + IDX_ROWS, :] = jnp.zeros((IDX_ROWS, LANES), BF)
        ref[base:base + DEPTHS, :] = value


def edge_kernel(sa_ref, sb_ref, ra_ref, rb_ref):
    freqs = ra_ref.shape[0] // (2 * HALO)
    for f in range(freqs):
        for side in range(2):
            both = [side_of(sa_ref, sb_ref, p, side) for p in (f, freqs + f)]
            put_edges((ra_ref, rb_ref), (2 * f + side) * HALO, both, both)


def side_of(a_ref, b_ref, p, side):
    at = slice(p * HALO, (p + 1) * HALO)
    return from_sides(a_ref[at, :], b_ref[at, :], "src")[side]


def index_sides(a_ref, b_ref, base, axis):
    left, right = from_sides(a_ref[base:base + IDX_ROWS, :], b_ref[base:base + IDX_ROWS, :], axis)
    left = jnp.where(has_left(axis), left.astype(F32)[0:8], -1.0)
    right = jnp.where(has_right(axis), right.astype(F32)[0:8], -1.0)
    return left, right


def taps_of(index_tiles, table, entries):
    hot = [
        (lax.broadcasted_iota(jnp.int32, (entries, LANES), 0) == tile.astype(jnp.int32)).astype(F32).astype(BF)
        for tile in index_tiles
    ]
    return dot(hot[0] if len(hot) == 1 else jnp.concatenate(hot, axis=1), table, TT)


def skew(taps):
    return pltpu.roll(taps, 0, 1, stride=1, stride_axis=0)


def source_kernel(
    sa_ref, sb_ref, sidx_ref, taps_ref, bins_ref, weight_ref,
    near_ref, mid_ref, far_ref, pair_ref, table_ref, sx_ref, wt_ref,
):
    rows, cols = bins_ref.shape
    freqs = near_ref.shape[0]
    tiles = cols // LANES
    for f in range(freqs):
        for part in range(2):
            at = (2 * f + part) * LANES
            table_ref[at:at + LANES, :] = jnp.zeros((LANES, table_ref.shape[1]), BF)
            table_ref[at:at + TAPS, :] = taps_ref[part, :, f, :].astype(BF)
    table = table_ref[...]
    entries = table.shape[1]
    wt_ref[...] = jnp.zeros(wt_ref.shape, F32)
    wt_ref[0:DEPTHS, 0:weight_ref.shape[1]] = weight_ref[...]
    for t in range(tiles):
        bins = bins_ref[:, t * LANES:(t + 1) * LANES]
        for z in range(DEPTHS):
            row = jnp.broadcast_to(wt_ref[z:z + 1, :], (rows, LANES))
            pair_ref[z, t] = jnp.take_along_axis(row, bins, axis=1)
    left, right = index_sides(sa_ref, sb_ref, 2 * freqs * HALO, "src")
    sx_ref[...] = jnp.zeros(sx_ref.shape, F32)
    sx_ref[0:DEPTHS, 0:rows] = sidx_ref[...].astype(F32)
    reach = HALO - HALF
    index = join([(left, 0, reach - rows), (sx_ref[...], reach, reach), (right, reach + rows, reach + rows)])
    out = lax.broadcasted_iota(jnp.int32, (LANES, LANES), 0)
    lane = lane_of((LANES, LANES))
    ops = []
    for z in range(DEPTHS):
        taps = taps_of([roll(index, -z * HALF)[z:z + 1]], table, entries)
        found = []
        for part in range(2 * freqs):
            skewed = skew(taps[:, part * LANES:(part + 1) * LANES])
            found.append((jnp.where(lane >= out, skewed, 0.0), jnp.where(lane < out, skewed, 0.0)))
        ops.append(found)
    narrow = lane_of((rows, LANES))
    for f in range(freqs):
        s0 = [[tile.astype(BF) for tile in ops[0][2 * f + part]] for part in range(2)]
        s1 = [ops[1][2 * f + part][0].astype(BF) for part in range(2)]
        s2 = [ops[2][2 * f + part][0][:rows].astype(BF) for part in range(2)]
        got = dot(jnp.concatenate(s2, axis=0), jnp.concatenate(s1, axis=1))
        re = (got[:rows, :LANES] - got[rows:, LANES:]).astype(BF)
        im = (got[:rows, LANES:] + got[rows:, :LANES]).astype(BF)
        stack = jnp.concatenate([re, s1[0][HALF:HALF + rows], im, s1[1][HALF:HALF + rows]], axis=0)
        by_re = dot(stack, jnp.concatenate(s0[0], axis=1))
        by_im = dot(stack, jnp.concatenate(s0[1], axis=1))
        pr = by_re[:2 * rows] - by_im[2 * rows:]
        pi = by_im[:2 * rows] + by_re[2 * rows:]
        size = rows + 2 * HALF
        own = slice(reach, reach + rows)
        parts = [
            join([(ops[0][2 * f + part][0][own], 0, -reach), (ops[0][2 * f + part][1][own], LANES - reach, -reach)])
            for part in range(2)
        ]
        parts = [jnp.where(narrow < size, part, 0.0) for part in parts]
        minus = -parts[1]
        near_ref[f, :, 0:LANES] = jnp.where(narrow < size, parts[0], roll(minus, size)).astype(BF)
        near_ref[f, :, LANES:] = jnp.where(narrow < 2 * size - LANES, roll(minus, size), 0.0).astype(BF)
        mids = [
            join([(g[rows:, :LANES], 0, -HALF), (g[rows:, LANES:], LANES - HALF, -HALF)]) for g in (pr, pi)
        ]
        mid_ref[f, :, 0:LANES] = mids[0].astype(BF)
        mid_ref[f, :, LANES:] = (-mids[1]).astype(BF)
        re, im = pr[:rows].astype(BF), pi[:rows].astype(BF)
        far_ref[f, 0] = jnp.concatenate([re, im], axis=0)
        far_ref[f, 1] = jnp.concatenate([-im, re], axis=0)


def windows(own, left, right, blocks):
    tiles, found = len(own), []
    for b in range(blocks):
        first = b * OUT - HALO
        j, s = divmod(first, LANES)
        pieces = []
        if b == 0:
            pieces = [(left[0], 0, left[1]), (own[0], HALO, HALO)]
        else:
            pieces.append((own[j], 0, -s))
            if s and j + 1 < tiles:
                pieces.append((own[j + 1], LANES - s, -s))
            end = tiles * LANES - first
            if end < LANES:
                pieces.append((right[0], end, end + right[1]))
        found.append(join(pieces))
    return found


def receiver_steps(first, w_ref, freqs, rows, keep):
    source = first
    blocks = len(first[0])
    for z in range(DEPTHS):
        after = [[None] * blocks for _ in range(2 * freqs)]
        for b in range(blocks):
            for f in range(freqs):
                both = jnp.concatenate([source[f][b], source[freqs + f][b]], axis=1)
                w = jnp.concatenate([w_ref[z, b, f, 0], w_ref[z, b, f, 1]], axis=1)
                got = dot(both, w, NT)
                for p, lanes in ((f, got[:, :OUT]), (freqs + f, got[:, LANES:LANES + OUT])):
                    after[p][b] = jnp.concatenate([lanes, jnp.zeros((rows, LANES - OUT), F32)], axis=1).astype(BF)
        if z < DEPTHS - 1:
            lane = lane_of((rows, LANES))
            source = [
                [
                    jnp.where(lane < OUT, plane[b], roll(plane[b + 1], OUT)) if b + 1 < blocks else plane[b]
                    for b in range(blocks)
                ]
                for plane in after
            ]
        else:
            source = after
        for p in range(2 * freqs):
            for b in range(blocks):
                keep(z, p, b, source[p][b])


def halo_sides(ra_ref, rb_ref, at, part):
    left, right = from_sides(ra_ref[at, :], rb_ref[at, :], "rec")
    left = jnp.where(has_left("rec"), left, jnp.zeros_like(left))
    right = jnp.where(has_right("rec"), right, jnp.zeros_like(right))
    return (left, HALO + part * MID), (right, -part * MID)


def own_kernel(x_ref, ra_ref, rb_ref, ridx_ref, table_ref, w_ref, a_ref, widx_ref):
    planes, rows, cols = x_ref.shape
    tiles = cols // LANES
    freqs = planes // 2
    blocks = w_ref.shape[1]
    table = table_ref[...]
    entries = table.shape[1]
    left, right = index_sides(ra_ref, rb_ref, freqs * rows, "rec")
    widx_ref[...] = jnp.zeros(widx_ref.shape, F32)
    widx_ref[0:DEPTHS, :] = ridx_ref[...].astype(F32)
    own = [widx_ref[:, t * LANES:(t + 1) * LANES] for t in range(tiles)]
    none = jnp.full((8, LANES), -1.0, F32)
    for z in range(DEPTHS):
        before = HALF * (DEPTHS - 1 - z)
        index = []
        for t in range(tiles + 1):
            pieces = []
            if before:
                pieces.append(((left, own[0])[min(t, 1)] if t < 2 else own[t - 1], 0, before))
            if t < tiles:
                pieces.append((own[t], before, before))
            else:
                if before:
                    pieces.append((right, before, before))
                pieces.append((none, 2 * before, 0))
            index.append(join(pieces)[z:z + 1])
        taps = taps_of(index, table, entries)
        for b in range(blocks):
            at = slice(b * OUT, (b + 1) * OUT)
            for f in range(freqs):
                re, im = (
                    skew(taps[at, part * LANES:(part + 1) * LANES]) for part in (2 * f, 2 * f + 1)
                )
                minus, re, im = (-im).astype(BF), re.astype(BF), im.astype(BF)
                for half, (top, low) in enumerate(((re, im), (minus, re))):
                    w_ref[z, b, f, half, 0:OUT, :] = top
                    w_ref[z, b, f, half, OUT:LANES, :] = jnp.zeros((LANES - OUT, LANES), BF)
                    w_ref[z, b, f, half, LANES:, :] = low
    first = []
    for p in range(planes):
        part, f = divmod(p, freqs)
        sides = halo_sides(ra_ref, rb_ref, slice(f * rows, (f + 1) * rows), part)
        first.append(windows([x_ref[p, :, t:t + LANES] for t in range(0, cols, LANES)], *sides, blocks))

    def keep(z, p, b, value):
        a_ref[z, p, b] = value

    receiver_steps(first, w_ref, freqs, rows, keep)


def image_kernel(
    ma_ref, mb_ref, sa_ref, sb_ref, ra_ref, rb_ref, w_ref, own_ref, near_ref, mid_ref, far_ref, pair_ref,
    send_ref, keep_ref, deep_ref, a_ref, part_ref,
):
    _, planes, blocks, rows, _ = own_ref.shape
    freqs = planes // 2
    tiles = pair_ref.shape[1]
    full = rows + 2 * HALO
    first = []
    for p in range(planes):
        part, f = divmod(p, freqs)
        at = slice(p * HALO, (p + 1) * HALO)
        parts = [(sa_ref[at, :], sb_ref[at, :])] + [(ma_ref[p, t], mb_ref[p, t]) for t in range(tiles - 1)]
        main = []
        for a, b in parts:
            left, right = from_sides(a, b, "src")
            left = jnp.where(has_left("src"), left, jnp.zeros_like(left))
            right = jnp.where(has_right("src"), right, jnp.zeros_like(right))
            main.append(jnp.concatenate([left, right], axis=0))
        ends, mixed = main[:2]
        lane = lane_of(ends.shape)
        main = [jnp.where(lane < MID, ends, mixed)] + main[2:] + [jnp.where(lane < MID, mixed, ends)]
        sides = []
        for cells, amount in halo_sides(ra_ref, rb_ref, slice(2 * f * HALO, 2 * (f + 1) * HALO), part):
            top = jnp.where(has_left("src"), cells[:HALO], jnp.zeros_like(cells[:HALO]))
            low = jnp.where(has_right("src"), cells[HALO:], jnp.zeros_like(cells[HALO:]))
            sides.append((jnp.concatenate([top, low], axis=0), amount))
        first.append(windows(main, *sides, blocks))

    def place(z, p, b):
        return deep_ref.at[p, b] if z == DEPTHS - 1 else a_ref.at[z, p, b]

    def keep(z, p, b, value):
        to = place(z, p, b)
        to[0:HALO] = value[:HALO]
        to[HALO:HALO + rows] = own_ref[z, p, b]
        to[HALO + rows:] = value[HALO:]

    receiver_steps(first, w_ref, freqs, 2 * HALO, keep)

    def field(z, p, b, reach):
        at = slice(HALO - reach, HALO + rows + reach)
        return jnp.concatenate([place(z, p, b)[at], place(z, p, b + 1)[at]], axis=1)

    images = []
    for z, ref in ((0, near_ref), (1, mid_ref)):
        reach = HALF * (z + 1)
        size = rows + 2 * reach
        out = []
        for b in range(0, blocks, 2):
            total = None
            for f in range(freqs):
                both = jnp.concatenate([field(z, f, b, reach), field(z, freqs + f, b, reach)], axis=0)
                term = dot(ref[f, :, 0:2 * size], both)
                total = term if total is None else total + term
            out += [total[:, :LANES], total[:, LANES:]]
        images.append([gather(out, t * LANES + HALF * (DEPTHS - 1 - z), LANES) for t in range(tiles)])
    real = [None] * blocks
    for b in range(0, blocks, 2):
        for f in range(freqs):
            got = dot(far_ref[f, 0][:rows, :full], field(2, f, b, HALO))
            got += dot(far_ref[f, 1][:rows, :full], field(2, freqs + f, b, HALO))
            got = got.astype(BF).astype(F32)
            for k in range(2):
                term = got[:, k * LANES:(k + 1) * LANES]
                real[b + k] = term if real[b + k] is None else real[b + k] + term
    real = [gather(real, t * LANES) for t in range(tiles)]
    for t in range(tiles):
        value = pair_ref[DEPTHS - 1, t] * real[t]
        for z in range(DEPTHS - 1):
            value += pair_ref[z, t] * images[z][t]
        part_ref[:, t * LANES:(t + 1) * LANES] = value
    count = lax.axis_size("freq")
    share = rows // count
    me = lax.axis_index("freq")
    keep_ref[...] = part_ref[pl.ds(pl.multiple_of(me * share, 8), share), :]
    for j in range(1, count):
        there = partner(me, j, count)
        send_ref[j - 1] = part_ref[pl.ds(pl.multiple_of(there * share, 8), share), :].astype(BF)


def final_kernel(deep_ref, far_ref, final_ref):
    planes, blocks, full, _ = deep_ref.shape
    _, rows, cols = final_ref.shape
    freqs = planes // 2
    for f in range(freqs):
        out = []
        for b in range(0, blocks, 2):
            parts = [jnp.concatenate([deep_ref[p, b], deep_ref[p, b + 1]], axis=1) for p in (f, freqs + f)]
            got = dot(far_ref[f, 0][:, :full], parts[0]) + dot(far_ref[f, 1][:, :full], parts[1])
            got = got.astype(BF)
            out += [got[:, :LANES], got[:, LANES:]]
        for t in range(0, cols, LANES):
            both = gather(out, t)
            final_ref[f, :, t:t + LANES] = both[:rows]
            final_ref[freqs + f, :, t:t + LANES] = both[rows:]


def partner(me, j, count):
    if count & (count - 1) == 0:
        return me ^ j
    return (me + j) % count


def local_call(kernel, outs, scratch=(), flops=0, moved=0, vmem=16, **others):
    return pl.pallas_call(
        kernel,
        out_shape=[jax.ShapeDtypeStruct(s, d) for s, d in outs],
        scratch_shapes=[pltpu.VMEM(*s) if isinstance(s, tuple) else s for s in scratch],
        **others,
        compiler_params=pltpu.CompilerParams(vmem_limit_bytes=vmem << 20),
        cost_estimate=pl.CostEstimate(flops=flops, bytes_accessed=moved, transcendentals=0),
    )


def migrate(wave, tap_table, src_index, rec_index, offset_bin, bin_weight):
    freqs, rows, cols = wave.shape[1:]
    planes = 2 * freqs
    tiles = cols // LANES
    entries = tap_table.shape[1]
    count = lax.axis_size("freq")
    share = rows // count
    full = rows + 2 * HALO
    blocks = -(-(cols + 2 * (HALO - HALF)) // OUT)

    main = ((planes, tiles - 1, HALO, LANES), BF)
    small = ((planes * HALO + IDX_ROWS, LANES), BF)
    inputs = (wave.reshape(planes, rows, cols), src_index, rec_index, jnp.transpose(tap_table, (0, 3, 2, 1)), offset_bin, bin_weight)
    inputs = tuple(pltpu.with_memory_space_constraint(a, pltpu.HBM) for a in inputs)
    ma, mb, sa, sb, x, src_index, rec_index, tap_table, offset_bin, bin_weight = local_call(
        load_kernel,
        [main, main, small, small] + [(a.shape, a.dtype) for a in inputs],
        [pltpu.SemaphoreType.DMA((len(inputs),))],
        moved=1 << 20,
        in_specs=[pl.BlockSpec(memory_space=pltpu.HBM)] * len(inputs),
    )(*inputs)
    sa, sb = swaps(sa, sb, "src")
    ma, mb = swaps(ma, mb, "src")
    near = ((freqs * rows + IDX_ROWS, LANES), BF)
    ra, rb = local_call(near_kernel, [near, near], moved=1 << 16)(x, rec_index)
    ra, rb = swaps(ra, rb, "rec")
    edge = ((freqs * 2 * HALO, LANES), BF)
    ea, eb = local_call(edge_kernel, [edge, edge], moved=1 << 16)(sa, sb)
    ea, eb = swaps(ea, eb, "rec")

    near, mid, far, pair, table = local_call(
        source_kernel,
        [
            ((freqs, rows, 2 * LANES), BF),
            ((freqs, rows, 2 * LANES), BF),
            ((freqs, 2, 2 * rows, 2 * LANES), BF),
            ((DEPTHS, tiles, rows, LANES), F32),
            ((planes * LANES, entries), BF),
        ],
        [((8, LANES), F32), ((8, LANES), F32)],
        flops=1 << 28,
        moved=2 << 20,
    )(sa, sb, src_index, tap_table, offset_bin, bin_weight)
    w, own = local_call(
        own_kernel,
        [
            ((DEPTHS, blocks, freqs, 2, WROWS, LANES), BF),
            ((DEPTHS, planes, blocks, rows, LANES), BF),
        ],
        [((8, cols), F32)],
        flops=1 << 31,
        moved=5 << 20,
    )(x, ra, rb, rec_index, table)
    send, keep, deep = local_call(
        image_kernel,
        [
            ((max(count - 1, 1), share, cols), BF),
            ((share, cols), F32),
            ((planes, blocks, full, LANES), BF),
        ],
        [((DEPTHS - 1, planes, blocks, full, LANES), BF), ((rows, cols), F32)],
        flops=1 << 31,
        moved=8 << 20,
        vmem=24,
    )(ma, mb, sa, sb, ea, eb, w, own, near, mid, far, pair)
    total = keep
    for j in range(1, count):
        got = lax.ppermute(send[j - 1], "freq", [(i, partner(i, j, count)) for i in range(count)])
        total = total + got.astype(F32)
    (final,) = local_call(final_kernel, [((planes, rows, cols), BF)], flops=1 << 28, moved=1 << 20)(deep, far)
    scale = 1.0 / math.sqrt(freqs * count * DEPTHS)
    return final.reshape(wave.shape), total * scale


def solution(mesh):
    placed = (
        P(None, "freq", "src", "rec"),
        P(None, None, "freq", None),
        P(None, "src"),
        P(None, "rec"),
        P("src", "rec"),
        P(),
    )
    return jax.shard_map(
        migrate,
        mesh=mesh,
        in_specs=placed,
        out_specs=(P(None, "freq", "src", "rec"), P(("src", "freq"), "rec")),
        check_vma=False,
    )
```

```python
import math

import jax
import jax.numpy as jnp
from jax import lax
from jax.experimental import pallas as pl
from jax.experimental.pallas import tpu as pltpu
from jax.sharding import PartitionSpec as P

TAPS = 33
DEPTHS = 3
HALF = TAPS // 2
HALO = DEPTHS * HALF
LANES = 128
MID = LANES // 2
OUT = LANES - 2 * HALF
WROWS = LANES + OUT
IDX_ROWS = 16
BF = jnp.bfloat16
F32 = jnp.float32
NT = (((1,), (1,)), ((), ()))
NN = (((1,), (0,)), ((), ()))
TT = (((0,), (1,)), ((), ()))


def dot(a, b, dims=NN):
    return lax.dot_general(a, b, dims, preferred_element_type=F32)


def pairs_of(axis, odd):
    count, groups = lax.axis_size(axis), lax.axis_size("freq")
    pairs, alone = [], list(range(count))
    for i in range(odd, count - 1, 2):
        alone.remove(i)
        alone.remove(i + 1)
        for g in range(groups):
            pairs += [(i * groups + g, (i + 1) * groups + g), ((i + 1) * groups + g, i * groups + g)]
    for i in alone:
        for g in range(0, groups - 1, 2):
            pairs += [(i * groups + g, i * groups + g + 1), (i * groups + g + 1, i * groups + g)]
    return pairs


def swaps(a, b, axis):
    a = lax.ppermute(a, (axis, "freq"), pairs_of(axis, 0))
    b = lax.ppermute(b, (axis, "freq"), pairs_of(axis, 1))
    return a, b


def is_even(axis):
    return lax.rem(lax.axis_index(axis), 2) == 0


def has_left(axis):
    return lax.axis_index(axis) > 0


def has_right(axis):
    return lax.axis_index(axis) < lax.axis_size(axis) - 1


def lane_of(shape):
    return lax.broadcasted_iota(jnp.int32, shape, len(shape) - 1)


def roll(cells, amount):
    amount = amount % LANES
    return pltpu.roll(cells, amount, 1) if amount else cells


def from_sides(a, b, axis):
    even = is_even(axis)
    return jnp.where(even, b, a), jnp.where(even, a, b)


def join(pieces):
    tile = None
    for cells, start, amount in pieces:
        moved = roll(cells, amount)
        tile = moved if start == 0 else jnp.where(lane_of(moved.shape) < start, tile, moved)
    return tile


def gather(blocks, first, valid=OUT):
    pieces, at = [], 0
    while at < LANES:
        k, lane = divmod(first + at, OUT)
        if k >= len(blocks):
            break
        pieces.append((blocks[k], at, at - lane))
        at += valid - lane
    return join(pieces)


def load_kernel(*refs):
    count = 6
    sources, targets = refs[:count], refs[count + 4:2 * count + 4]
    ma_ref, mb_ref, sa_ref, sb_ref = refs[count:count + 4]
    sem = refs[2 * count + 4]
    copies = [pltpu.make_async_copy(s, t, sem.at[i]) for i, (s, t) in enumerate(zip(sources, targets))]
    for copy in copies:
        copy.start()
    x_ref, sidx_ref = targets[:2]
    planes, rows, cols = x_ref.shape
    even = is_even("src")
    low = rows - HALO
    at_a = pl.multiple_of(jnp.where(even, low, 0), 16)
    at_b = pl.multiple_of(jnp.where(even, 0, low), 16)
    lane = lane_of((HALO, LANES))
    base = planes * HALO
    copies[1].wait()
    index = sidx_ref[...].astype(F32).astype(BF)
    for small in (sa_ref, sb_ref):
        small[base:base + IDX_ROWS, :] = jnp.zeros((IDX_ROWS, LANES), BF)
        small[base:base + DEPTHS, 0:rows] = index
    copies[0].wait()
    for p in range(planes):
        for at, main, small in ((at_a, ma_ref, sa_ref), (at_b, mb_ref, sb_ref)):
            tiles = [x_ref[p, pl.ds(at, HALO), t:t + LANES] for t in range(0, cols, LANES)]
            main[p, 0] = jnp.where(lane < MID, tiles[-1], tiles[0])
            for t, tile in enumerate(tiles[1:-1]):
                main[p, t + 1] = tile
            small[p * HALO:(p + 1) * HALO, :] = jnp.where(lane < MID, tiles[0], tiles[-1])
    for copy in copies[2:]:
        copy.wait()


def put_edges(ends, at, tail, head):
    lane = lane_of(tail[0].shape)
    right = jnp.where(lane < MID, roll(tail[1], MID), tail[0])
    left = jnp.where(lane < MID, head[0], roll(head[1], MID))
    even = is_even("rec")
    place = slice(at, at + right.shape[0])
    ends[0][place, :] = jnp.where(even, right, left)
    ends[1][place, :] = jnp.where(even, left, right)


def near_kernel(x_ref, ridx_ref, ra_ref, rb_ref):
    planes, rows, cols = x_ref.shape
    freqs = planes // 2
    ends = (ra_ref, rb_ref)
    last = cols - LANES
    for f in range(freqs):
        tail = [x_ref[p, :, last:] for p in (f, freqs + f)]
        head = [x_ref[p, :, :LANES] for p in (f, freqs + f)]
        put_edges(ends, f * rows, tail, head)
    base = freqs * rows
    head = ridx_ref[:, :LANES].astype(F32).astype(BF)
    tail = ridx_ref[:, last:].astype(F32).astype(BF)
    even = is_even("rec")
    for ref, value in zip(ends, (jnp.where(even, tail, head), jnp.where(even, head, tail))):
        ref[base:base + IDX_ROWS, :] = jnp.zeros((IDX_ROWS, LANES), BF)
        ref[base:base + DEPTHS, :] = value


def edge_kernel(sa_ref, sb_ref, ra_ref, rb_ref):
    freqs = ra_ref.shape[0] // (2 * HALO)
    for f in range(freqs):
        for side in range(2):
            both = [side_of(sa_ref, sb_ref, p, side) for p in (f, freqs + f)]
            put_edges((ra_ref, rb_ref), (2 * f + side) * HALO, both, both)


def side_of(a_ref, b_ref, p, side):
    at = slice(p * HALO, (p + 1) * HALO)
    return from_sides(a_ref[at, :], b_ref[at, :], "src")[side]


def index_sides(a_ref, b_ref, base, axis):
    left, right = from_sides(a_ref[base:base + IDX_ROWS, :], b_ref[base:base + IDX_ROWS, :], axis)
    left = jnp.where(has_left(axis), left.astype(F32)[0:8], -1.0)
    right = jnp.where(has_right(axis), right.astype(F32)[0:8], -1.0)
    return left, right


def taps_of(index_tiles, table, entries):
    hot = [
        (lax.broadcasted_iota(jnp.int32, (entries, LANES), 0) == tile.astype(jnp.int32)).astype(F32).astype(BF)
        for tile in index_tiles
    ]
    return dot(hot[0] if len(hot) == 1 else jnp.concatenate(hot, axis=1), table, TT)


def skew(taps):
    return pltpu.roll(taps, 0, 1, stride=1, stride_axis=0)


def put_lanes(parts, width):
    out, pieces, at = [], [], 0
    for tiles, first, count in parts:
        while count:
            j, lane = divmod(first, LANES)
            size = min(count, LANES - lane, LANES - at)
            pieces.append((tiles[j], at, at - lane))
            first, count, at = first + size, count - size, at + size
            if at == LANES:
                out.append(join(pieces))
                pieces, at = [], 0
    if pieces:
        pieces.append((jnp.zeros_like(pieces[0][0]), at, 0))
        out.append(join(pieces))
    assert len(out) * LANES == width
    return jnp.concatenate(out, axis=1).astype(BF)


def pair_weights(bins_ref, weight_ref, pair_ref, wt_ref):
    rows, cols = bins_ref.shape
    wt_ref[...] = jnp.zeros(wt_ref.shape, F32)
    wt_ref[0:DEPTHS, 0:weight_ref.shape[1]] = weight_ref[...]
    for t in range(cols // LANES):
        bins = bins_ref[:, t * LANES:(t + 1) * LANES]
        for z in range(DEPTHS):
            row = jnp.broadcast_to(wt_ref[z:z + 1, :], (rows, LANES))
            pair_ref[z, t] = jnp.take_along_axis(row, bins, axis=1)


def tap_rows(taps_ref, table_ref, freqs):
    for f in range(freqs):
        for part in range(2):
            at = (2 * f + part) * LANES
            table_ref[at:at + LANES, :] = jnp.zeros((LANES, table_ref.shape[1]), BF)
            table_ref[at:at + TAPS, :] = taps_ref[part, :, f, :].astype(BF)
    return table_ref[...]


def source_operators(sa_ref, sb_ref, sidx_ref, table, freqs, rows, own_refs, halo_refs, sx_ref):
    entries = table.shape[1]
    left, right = index_sides(sa_ref, sb_ref, 2 * freqs * HALO, "src")
    sx_ref[...] = jnp.zeros(sx_ref.shape, F32)
    sx_ref[0:DEPTHS, 0:rows] = sidx_ref[...].astype(F32)
    reach = HALO - HALF
    index = join([(left, 0, reach - rows), (sx_ref[...], reach, reach), (right, reach + rows, reach + rows)])
    out = lax.broadcasted_iota(jnp.int32, (LANES, LANES), 0)
    lane = lane_of((LANES, LANES))
    ops = []
    for z in range(DEPTHS):
        taps = taps_of([roll(index, -z * HALF)[z:z + 1]], table, entries)
        found = []
        for part in range(2 * freqs):
            skewed = skew(taps[:, part * LANES:(part + 1) * LANES])
            found.append((jnp.where(lane >= out, skewed, 0.0), jnp.where(lane < out, skewed, 0.0)))
        ops.append(found)
    own = slice(reach, reach + rows)
    fields = []
    for f in range(freqs):
        s0 = [[tile.astype(BF) for tile in ops[0][2 * f + part]] for part in range(2)]
        s1 = [ops[1][2 * f + part][0].astype(BF) for part in range(2)]
        s2 = [ops[2][2 * f + part][0][:rows].astype(BF) for part in range(2)]
        got = dot(jnp.concatenate(s2, axis=0), jnp.concatenate(s1, axis=1))
        re = (got[:rows, :LANES] - got[rows:, LANES:]).astype(BF)
        im = (got[:rows, LANES:] + got[rows:, :LANES]).astype(BF)
        stack = jnp.concatenate([re, s1[0][HALF:HALF + rows], im, s1[1][HALF:HALF + rows]], axis=0)
        by_re = dot(stack, jnp.concatenate(s0[0], axis=1))
        by_im = dot(stack, jnp.concatenate(s0[1], axis=1))
        pr = by_re[:2 * rows] - by_im[2 * rows:]
        pi = by_im[:2 * rows] + by_re[2 * rows:]
        cut = [[p[:, :LANES], p[:, LANES:]] for p in (pr, pi)]
        fields.append((
            [[tile[own] for tile in ops[0][2 * f + part]] for part in range(2)],
            [[tile[rows:] for tile in tiles] for tiles in cut],
            [[tile[:rows] for tile in tiles] for tiles in cut],
        ))

    def negative(tiles):
        return [-tile for tile in tiles]

    for z in range(DEPTHS - 1):
        near = HALF * (z + 1)
        planes = [fields[f][z][0] for f in range(freqs)] + [negative(fields[f][z][1]) for f in range(freqs)]
        own_refs[z][...] = put_lanes([(tiles, HALO, rows) for tiles in planes], own_refs[z].shape[1])
        sides = []
        for tiles in planes:
            sides += [(tiles, HALO - near, near), (tiles, HALO + rows, near)]
        halo_refs[z][...] = put_lanes(sides, halo_refs[z].shape[1])
    for f in range(freqs):
        re, im = fields[f][DEPTHS - 1]
        for half, planes in enumerate(((re, negative(im)), (im, re))):
            at = slice(half * rows, (half + 1) * rows)
            own_refs[-1][f, at, :] = put_lanes([(tiles, HALO, rows) for tiles in planes], own_refs[-1].shape[2])
            sides = []
            for tiles in planes:
                sides += [(tiles, 0, HALO), (tiles, HALO + rows, HALO)]
            halo_refs[-1][f, at, :] = put_lanes(sides, halo_refs[-1].shape[2])


def windows(own, left, right, blocks):
    tiles, found = len(own), []
    for b in range(blocks):
        first = b * OUT - HALO
        j, s = divmod(first, LANES)
        pieces = []
        if b == 0:
            pieces = [(left[0], 0, left[1]), (own[0], HALO, HALO)]
        else:
            pieces.append((own[j], 0, -s))
            if s and j + 1 < tiles:
                pieces.append((own[j + 1], LANES - s, -s))
            end = tiles * LANES - first
            if end < LANES:
                pieces.append((right[0], end, end + right[1]))
        found.append(join(pieces))
    return found


def receiver_steps(first, w_ref, freqs, rows, keep):
    source = first
    blocks = len(first[0])
    for z in range(DEPTHS):
        after = [[None] * blocks for _ in range(2 * freqs)]
        for b in range(blocks):
            for f in range(freqs):
                both = jnp.concatenate([source[f][b], source[freqs + f][b]], axis=1)
                w = jnp.concatenate([w_ref[z, b, f, 0], w_ref[z, b, f, 1]], axis=1)
                got = dot(both, w, NT)
                for p, lanes in ((f, got[:, :OUT]), (freqs + f, got[:, LANES:LANES + OUT])):
                    after[p][b] = jnp.concatenate([lanes, jnp.zeros((rows, LANES - OUT), F32)], axis=1).astype(BF)
        if z < DEPTHS - 1:
            lane = lane_of((rows, LANES))
            source = [
                [
                    jnp.where(lane < OUT, plane[b], roll(plane[b + 1], OUT)) if b + 1 < blocks else plane[b]
                    for b in range(blocks)
                ]
                for plane in after
            ]
        else:
            source = after
        for p in range(2 * freqs):
            for b in range(blocks):
                keep(z, p, b, source[p][b])


def halo_sides(ra_ref, rb_ref, at, part):
    left, right = from_sides(ra_ref[at, :], rb_ref[at, :], "rec")
    left = jnp.where(has_left("rec"), left, jnp.zeros_like(left))
    right = jnp.where(has_right("rec"), right, jnp.zeros_like(right))
    return (left, HALO + part * MID), (right, -part * MID)


def own_kernel(
    x_ref, ra_ref, rb_ref, ridx_ref, sa_ref, sb_ref, sidx_ref, taps_ref, bins_ref, weight_ref,
    w_ref, a_ref, pair_ref, own0_ref, own1_ref, own2_ref, halo0_ref, halo1_ref, halo2_ref,
    widx_ref, table_ref, sx_ref, wt_ref,
):
    planes, rows, cols = x_ref.shape
    tiles = cols // LANES
    freqs = planes // 2
    blocks = w_ref.shape[1]
    table = tap_rows(taps_ref, table_ref, freqs)
    entries = table.shape[1]
    left, right = index_sides(ra_ref, rb_ref, freqs * rows, "rec")
    widx_ref[...] = jnp.zeros(widx_ref.shape, F32)
    widx_ref[0:DEPTHS, :] = ridx_ref[...].astype(F32)
    own = [widx_ref[:, t * LANES:(t + 1) * LANES] for t in range(tiles)]
    none = jnp.full((8, LANES), -1.0, F32)
    for z in range(DEPTHS):
        before = HALF * (DEPTHS - 1 - z)
        index = []
        for t in range(tiles + 1):
            pieces = []
            if before:
                pieces.append(((left, own[0])[min(t, 1)] if t < 2 else own[t - 1], 0, before))
            if t < tiles:
                pieces.append((own[t], before, before))
            else:
                if before:
                    pieces.append((right, before, before))
                pieces.append((none, 2 * before, 0))
            index.append(join(pieces)[z:z + 1])
        taps = taps_of(index, table, entries)
        for b in range(blocks):
            at = slice(b * OUT, (b + 1) * OUT)
            for f in range(freqs):
                re, im = (
                    skew(taps[at, part * LANES:(part + 1) * LANES]) for part in (2 * f, 2 * f + 1)
                )
                minus, re, im = (-im).astype(BF), re.astype(BF), im.astype(BF)
                for half, (top, low) in enumerate(((re, im), (minus, re))):
                    w_ref[z, b, f, half, 0:OUT, :] = top
                    w_ref[z, b, f, half, OUT:LANES, :] = jnp.zeros((LANES - OUT, LANES), BF)
                    w_ref[z, b, f, half, LANES:, :] = low
    first = []
    for p in range(planes):
        part, f = divmod(p, freqs)
        sides = halo_sides(ra_ref, rb_ref, slice(f * rows, (f + 1) * rows), part)
        first.append(windows([x_ref[p, :, t:t + LANES] for t in range(0, cols, LANES)], *sides, blocks))

    def keep(z, p, b, value):
        a_ref[z, p, b] = value

    receiver_steps(first, w_ref, freqs, rows, keep)
    source_operators(
        sa_ref, sb_ref, sidx_ref, table, freqs, rows,
        (own0_ref, own1_ref, own2_ref), (halo0_ref, halo1_ref, halo2_ref), sx_ref,
    )
    pair_weights(bins_ref, weight_ref, pair_ref, wt_ref)


def stacked(ref, planes, b, first, size):
    at = slice(first, first + size)
    return jnp.concatenate([jnp.concatenate([ref[p, b + k, at] for p in planes], axis=0) for k in range(2)], axis=1)


def last_step(own, halo, own2_ref, halo2_ref, f, b, out):
    planes = (f, own.shape[0] // 2 + f)
    rows = own.shape[2]
    got = dot(own2_ref[f, :out], stacked(own, planes, b, 0, rows))
    width = len(planes) * 2 * HALO
    return got + dot(halo2_ref[f, :out, :width], stacked(halo, planes, b, 0, 2 * HALO))


def image_kernel(
    ma_ref, mb_ref, sa_ref, sb_ref, ra_ref, rb_ref, w_ref, own_ref, own0_ref, own1_ref, own2_ref,
    halo0_ref, halo1_ref, halo2_ref, pair_ref, send_ref, keep_ref, deep_ref, a_ref, part_ref,
):
    _, planes, blocks, rows, _ = own_ref.shape
    freqs = planes // 2
    tiles = pair_ref.shape[1]
    first = []
    for p in range(planes):
        part, f = divmod(p, freqs)
        at = slice(p * HALO, (p + 1) * HALO)
        parts = [(sa_ref[at, :], sb_ref[at, :])] + [(ma_ref[p, t], mb_ref[p, t]) for t in range(tiles - 1)]
        main = []
        for a, b in parts:
            left, right = from_sides(a, b, "src")
            left = jnp.where(has_left("src"), left, jnp.zeros_like(left))
            right = jnp.where(has_right("src"), right, jnp.zeros_like(right))
            main.append(jnp.concatenate([left, right], axis=0))
        ends, mixed = main[:2]
        lane = lane_of(ends.shape)
        main = [jnp.where(lane < MID, ends, mixed)] + main[2:] + [jnp.where(lane < MID, mixed, ends)]
        sides = []
        for cells, amount in halo_sides(ra_ref, rb_ref, slice(2 * f * HALO, 2 * (f + 1) * HALO), part):
            top = jnp.where(has_left("src"), cells[:HALO], jnp.zeros_like(cells[:HALO]))
            low = jnp.where(has_right("src"), cells[HALO:], jnp.zeros_like(cells[HALO:]))
            sides.append((jnp.concatenate([top, low], axis=0), amount))
        first.append(windows(main, *sides, blocks))

    def halo(z):
        return deep_ref if z == DEPTHS - 1 else a_ref.at[z]

    def keep(z, p, b, value):
        halo(z)[p, b] = value

    receiver_steps(first, w_ref, freqs, 2 * HALO, keep)
    images = []
    for z, lhs, side in ((0, own0_ref, halo0_ref), (1, own1_ref, halo1_ref)):
        near = HALF * (z + 1)
        out = []
        for b in range(0, blocks, 2):
            total = dot(lhs[...], stacked(own_ref.at[z], range(planes), b, 0, rows))
            total += dot(side[...], stacked(halo(z), range(planes), b, HALO - near, 2 * near))
            out += [total[:, :LANES], total[:, LANES:]]
        images.append([gather(out, t * LANES + HALF * (DEPTHS - 1 - z), LANES) for t in range(tiles)])
    real = [None] * blocks
    for b in range(0, blocks, 2):
        for f in range(freqs):
            got = last_step(own_ref.at[DEPTHS - 1], deep_ref, own2_ref, halo2_ref, f, b, rows)
            got = got.astype(BF).astype(F32)
            for k in range(2):
                term = got[:, k * LANES:(k + 1) * LANES]
                real[b + k] = term if real[b + k] is None else real[b + k] + term
    real = [gather(real, t * LANES) for t in range(tiles)]
    for t in range(tiles):
        value = pair_ref[DEPTHS - 1, t] * real[t]
        for z in range(DEPTHS - 1):
            value += pair_ref[z, t] * images[z][t]
        part_ref[:, t * LANES:(t + 1) * LANES] = value
    count = lax.axis_size("freq")
    share = rows // count
    me = lax.axis_index("freq")
    keep_ref[...] = part_ref[pl.ds(pl.multiple_of(me * share, 8), share), :]
    for j in range(1, count):
        there = partner(me, j, count)
        send_ref[j - 1] = part_ref[pl.ds(pl.multiple_of(there * share, 8), share), :].astype(BF)


def final_kernel(own_ref, deep_ref, own2_ref, halo2_ref, final_ref):
    _, planes, blocks, rows, _ = own_ref.shape
    cols = final_ref.shape[2]
    freqs = planes // 2
    for f in range(freqs):
        out = []
        for b in range(0, blocks, 2):
            got = last_step(own_ref.at[DEPTHS - 1], deep_ref, own2_ref, halo2_ref, f, b, 2 * rows).astype(BF)
            out += [got[:, :LANES], got[:, LANES:]]
        for t in range(0, cols, LANES):
            both = gather(out, t)
            final_ref[f, :, t:t + LANES] = both[:rows]
            final_ref[freqs + f, :, t:t + LANES] = both[rows:]


def partner(me, j, count):
    if count & (count - 1) == 0:
        return me ^ j
    return (me + j) % count


def local_call(kernel, outs, scratch=(), flops=0, moved=0, vmem=16, **others):
    return pl.pallas_call(
        kernel,
        out_shape=[jax.ShapeDtypeStruct(s, d) for s, d in outs],
        scratch_shapes=[pltpu.VMEM(*s) if isinstance(s, tuple) else s for s in scratch],
        **others,
        compiler_params=pltpu.CompilerParams(vmem_limit_bytes=vmem << 20),
        cost_estimate=pl.CostEstimate(flops=flops, bytes_accessed=moved, transcendentals=0),
    )


def migrate(wave, tap_table, src_index, rec_index, offset_bin, bin_weight):
    freqs, rows, cols = wave.shape[1:]
    planes = 2 * freqs
    tiles = cols // LANES
    entries = tap_table.shape[1]
    count = lax.axis_size("freq")
    share = rows // count
    blocks = -(-(cols + 2 * (HALO - HALF)) // OUT)

    main = ((planes, tiles - 1, HALO, LANES), BF)
    small = ((planes * HALO + IDX_ROWS, LANES), BF)
    inputs = (wave.reshape(planes, rows, cols), src_index, rec_index, jnp.transpose(tap_table, (0, 3, 2, 1)), offset_bin, bin_weight)
    inputs = tuple(pltpu.with_memory_space_constraint(a, pltpu.HBM) for a in inputs)
    ma, mb, sa, sb, x, src_index, rec_index, tap_table, offset_bin, bin_weight = local_call(
        load_kernel,
        [main, main, small, small] + [(a.shape, a.dtype) for a in inputs],
        [pltpu.SemaphoreType.DMA((len(inputs),))],
        moved=1 << 20,
        in_specs=[pl.BlockSpec(memory_space=pltpu.HBM)] * len(inputs),
    )(*inputs)
    sa, sb = swaps(sa, sb, "src")
    ma, mb = swaps(ma, mb, "src")
    near = ((freqs * rows + IDX_ROWS, LANES), BF)
    ra, rb = local_call(near_kernel, [near, near], moved=1 << 16)(x, rec_index)
    ra, rb = swaps(ra, rb, "rec")
    edge = ((freqs * 2 * HALO, LANES), BF)
    ea, eb = local_call(edge_kernel, [edge, edge], moved=1 << 16)(sa, sb)
    ea, eb = swaps(ea, eb, "rec")

    sizes = [-(-planes * n // LANES) * LANES for n in (rows, 2 * HALF, 4 * HALF)]
    deep = -(-4 * HALO // LANES) * LANES
    w, own, pair, *lhs = local_call(
        own_kernel,
        [
            ((DEPTHS, blocks, freqs, 2, WROWS, LANES), BF),
            ((DEPTHS, planes, blocks, rows, LANES), BF),
            ((DEPTHS, tiles, rows, LANES), F32),
            ((rows, sizes[0]), BF),
            ((rows, sizes[0]), BF),
            ((freqs, 2 * rows, 2 * rows), BF),
            ((rows, sizes[1]), BF),
            ((rows, sizes[2]), BF),
            ((freqs, 2 * rows, deep), BF),
        ],
        [((8, cols), F32), ((planes * LANES, entries), BF), ((8, LANES), F32), ((8, LANES), F32)],
        flops=1 << 31,
        moved=5 << 20,
    )(x, ra, rb, rec_index, sa, sb, src_index, tap_table, offset_bin, bin_weight)
    send, keep, deep = local_call(
        image_kernel,
        [
            ((max(count - 1, 1), share, cols), BF),
            ((share, cols), F32),
            ((planes, blocks, 2 * HALO, LANES), BF),
        ],
        [((DEPTHS - 1, planes, blocks, 2 * HALO, LANES), BF), ((rows, cols), F32)],
        flops=1 << 31,
        moved=8 << 20,
        vmem=24,
    )(ma, mb, sa, sb, ea, eb, w, own, *lhs, pair)
    total = keep
    for j in range(1, count):
        got = lax.ppermute(send[j - 1], "freq", [(i, partner(i, j, count)) for i in range(count)])
        total = total + got.astype(F32)
    (final,) = local_call(final_kernel, [((planes, rows, cols), BF)], flops=1 << 28, moved=1 << 20)(
        own, deep, lhs[2], lhs[5]
    )
    scale = 1.0 / math.sqrt(freqs * count * DEPTHS)
    return final.reshape(wave.shape), total * scale


def solution(mesh):
    placed = (
        P(None, "freq", "src", "rec"),
        P(None, None, "freq", None),
        P(None, "src"),
        P(None, "rec"),
        P("src", "rec"),
        P(),
    )
    return jax.shard_map(
        migrate,
        mesh=mesh,
        in_specs=placed,
        out_specs=(P(None, "freq", "src", "rec"), P(("src", "freq"), "rec")),
        check_vma=False,
    )
```

```python
import math

import jax
import jax.numpy as jnp
from jax import lax
from jax.experimental import pallas as pl
from jax.experimental.pallas import tpu as pltpu
from jax.sharding import PartitionSpec as P

TAPS = 33
DEPTHS = 3
HALF = TAPS // 2
HALO = DEPTHS * HALF
LANES = 128
MID = LANES // 2
OUT = LANES - 2 * HALF
WROWS = LANES + OUT
IDX_ROWS = 16
BF = jnp.bfloat16
F32 = jnp.float32
NT = (((1,), (1,)), ((), ()))
NN = (((1,), (0,)), ((), ()))
TT = (((0,), (1,)), ((), ()))


def dot(a, b, dims=NN):
    return lax.dot_general(a, b, dims, preferred_element_type=F32)


def pairs_of(axis, odd):
    count, groups = lax.axis_size(axis), lax.axis_size("freq")
    pairs, alone = [], list(range(count))
    for i in range(odd, count - 1, 2):
        alone.remove(i)
        alone.remove(i + 1)
        for g in range(groups):
            pairs += [(i * groups + g, (i + 1) * groups + g), ((i + 1) * groups + g, i * groups + g)]
    for i in alone:
        for g in range(0, groups - 1, 2):
            pairs += [(i * groups + g, i * groups + g + 1), (i * groups + g + 1, i * groups + g)]
    return pairs


def swaps(a, b, axis):
    a = lax.ppermute(a, (axis, "freq"), pairs_of(axis, 0))
    b = lax.ppermute(b, (axis, "freq"), pairs_of(axis, 1))
    return a, b


def is_even(axis):
    return lax.rem(lax.axis_index(axis), 2) == 0


def has_left(axis):
    return lax.axis_index(axis) > 0


def has_right(axis):
    return lax.axis_index(axis) < lax.axis_size(axis) - 1


def lane_of(shape):
    return lax.broadcasted_iota(jnp.int32, shape, len(shape) - 1)


def roll(cells, amount):
    amount = amount % LANES
    return pltpu.roll(cells, amount, 1) if amount else cells


def from_sides(a, b, axis):
    even = is_even(axis)
    return jnp.where(even, b, a), jnp.where(even, a, b)


def join(pieces):
    tile = None
    for cells, start, amount in pieces:
        moved = roll(cells, amount)
        tile = moved if start == 0 else jnp.where(lane_of(moved.shape) < start, tile, moved)
    return tile


def gather(blocks, first, valid=OUT):
    pieces, at = [], 0
    while at < LANES:
        k, lane = divmod(first + at, OUT)
        if k >= len(blocks):
            break
        pieces.append((blocks[k], at, at - lane))
        at += valid - lane
    return join(pieces)


def load_kernel(*refs):
    count = len(refs) // 2 - 1
    sources, targets = refs[:count], refs[count + 2:2 * count + 2]
    sa_ref, sb_ref = refs[count:count + 2]
    sem = refs[2 * count + 2]
    copies = [pltpu.make_async_copy(s, t, sem.at[i]) for i, (s, t) in enumerate(zip(sources, targets))]
    for copy in copies:
        copy.start()
    x_ref, sidx_ref = targets[:2]
    planes, rows, cols = x_ref.shape
    at_a, at_b = halo_rows(rows)
    lane = lane_of((HALO, LANES))
    base = planes * HALO
    copies[1].wait()
    index = sidx_ref[...].astype(F32).astype(BF)
    for small in (sa_ref, sb_ref):
        small[base:base + IDX_ROWS, :] = jnp.zeros((IDX_ROWS, LANES), BF)
        small[base:base + DEPTHS, 0:rows] = index
    copies[0].wait()
    for p in range(planes):
        for at, small in ((at_a, sa_ref), (at_b, sb_ref)):
            ends = [x_ref[p, pl.ds(at, HALO), t:t + LANES] for t in (0, cols - LANES)]
            small[p * HALO:(p + 1) * HALO, :] = jnp.where(lane < MID, *ends)
    for copy in copies[2:]:
        copy.wait()


def halo_rows(rows):
    even = is_even("src")
    low = rows - HALO
    return (
        pl.multiple_of(jnp.where(even, low, 0), 16),
        pl.multiple_of(jnp.where(even, 0, low), 16),
    )


def put_edges(ends, at, tail, head):
    lane = lane_of(tail[0].shape)
    right = jnp.where(lane < MID, roll(tail[1], MID), tail[0])
    left = jnp.where(lane < MID, head[0], roll(head[1], MID))
    even = is_even("rec")
    place = slice(at, at + right.shape[0])
    ends[0][place, :] = jnp.where(even, right, left)
    ends[1][place, :] = jnp.where(even, left, right)


def pack_kernel(x_ref, ridx_ref, ma_ref, mb_ref, ra_ref, rb_ref):
    planes, rows, cols = x_ref.shape
    freqs = planes // 2
    lane = lane_of((HALO, LANES))
    for p in range(planes):
        for at, main in zip(halo_rows(rows), (ma_ref, mb_ref)):
            tiles = [x_ref[p, pl.ds(at, HALO), t:t + LANES] for t in range(0, cols, LANES)]
            main[p, 0] = jnp.where(lane < MID, tiles[-1], tiles[0])
            for t, tile in enumerate(tiles[1:-1]):
                main[p, t + 1] = tile
    ends = (ra_ref, rb_ref)
    last = cols - LANES
    for f in range(freqs):
        tail = [x_ref[p, :, last:] for p in (f, freqs + f)]
        head = [x_ref[p, :, :LANES] for p in (f, freqs + f)]
        put_edges(ends, f * rows, tail, head)
    base = freqs * rows
    head = ridx_ref[:, :LANES].astype(F32).astype(BF)
    tail = ridx_ref[:, last:].astype(F32).astype(BF)
    even = is_even("rec")
    for ref, value in zip(ends, (jnp.where(even, tail, head), jnp.where(even, head, tail))):
        ref[base:base + IDX_ROWS, :] = jnp.zeros((IDX_ROWS, LANES), BF)
        ref[base:base + DEPTHS, :] = value


def edge_kernel(sa_ref, sb_ref, ra_ref, rb_ref):
    freqs = ra_ref.shape[0] // (2 * HALO)
    for f in range(freqs):
        for side in range(2):
            both = [side_of(sa_ref, sb_ref, p, side) for p in (f, freqs + f)]
            put_edges((ra_ref, rb_ref), (2 * f + side) * HALO, both, both)


def side_of(a_ref, b_ref, p, side):
    at = slice(p * HALO, (p + 1) * HALO)
    return from_sides(a_ref[at, :], b_ref[at, :], "src")[side]


def index_sides(a_ref, b_ref, base, axis):
    left, right = from_sides(a_ref[base:base + IDX_ROWS, :], b_ref[base:base + IDX_ROWS, :], axis)
    left = jnp.where(has_left(axis), left.astype(F32)[0:8], -1.0)
    right = jnp.where(has_right(axis), right.astype(F32)[0:8], -1.0)
    return left, right


def taps_of(index_tiles, table, entries):
    hot = [
        (lax.broadcasted_iota(jnp.int32, (entries, LANES), 0) == tile.astype(jnp.int32)).astype(F32).astype(BF)
        for tile in index_tiles
    ]
    return dot(hot[0] if len(hot) == 1 else jnp.concatenate(hot, axis=1), table, TT)


def skew(taps):
    return pltpu.roll(taps, 0, 1, stride=1, stride_axis=0)


def source_kernel(
    sa_ref, sb_ref, sidx_ref, taps_ref, bins_hbm, weight_hbm,
    near_ref, mid_ref, far_ref, pair_ref, table_ref, sx_ref, wt_ref, bins_ref, weight_ref, sem,
):
    copies = [
        pltpu.make_async_copy(source, target, sem.at[i])
        for i, (source, target) in enumerate(((bins_hbm, bins_ref), (weight_hbm, weight_ref)))
    ]
    for copy in copies:
        copy.start()
    rows, cols = bins_ref.shape
    freqs = near_ref.shape[0]
    tiles = cols // LANES
    for f in range(freqs):
        for part in range(2):
            at = (2 * f + part) * LANES
            table_ref[at:at + LANES, :] = jnp.zeros((LANES, table_ref.shape[1]), BF)
            table_ref[at:at + TAPS, :] = taps_ref[part, :, f, :].astype(BF)
    table = table_ref[...]
    entries = table.shape[1]
    left, right = index_sides(sa_ref, sb_ref, 2 * freqs * HALO, "src")
    sx_ref[...] = jnp.zeros(sx_ref.shape, F32)
    sx_ref[0:DEPTHS, 0:rows] = sidx_ref[...].astype(F32)
    reach = HALO - HALF
    index = join([(left, 0, reach - rows), (sx_ref[...], reach, reach), (right, reach + rows, reach + rows)])
    out = lax.broadcasted_iota(jnp.int32, (LANES, LANES), 0)
    lane = lane_of((LANES, LANES))
    ops = []
    for z in range(DEPTHS):
        taps = taps_of([roll(index, -z * HALF)[z:z + 1]], table, entries)
        found = []
        for part in range(2 * freqs):
            skewed = skew(taps[:, part * LANES:(part + 1) * LANES])
            found.append((jnp.where(lane >= out, skewed, 0.0), jnp.where(lane < out, skewed, 0.0)))
        ops.append(found)
    narrow = lane_of((rows, LANES))
    for f in range(freqs):
        s0 = [[tile.astype(BF) for tile in ops[0][2 * f + part]] for part in range(2)]
        s1 = [ops[1][2 * f + part][0].astype(BF) for part in range(2)]
        s2 = [ops[2][2 * f + part][0][:rows].astype(BF) for part in range(2)]
        got = dot(jnp.concatenate(s2, axis=0), jnp.concatenate(s1, axis=1))
        re = (got[:rows, :LANES] - got[rows:, LANES:]).astype(BF)
        im = (got[:rows, LANES:] + got[rows:, :LANES]).astype(BF)
        stack = jnp.concatenate([re, s1[0][HALF:HALF + rows], im, s1[1][HALF:HALF + rows]], axis=0)
        by_re = dot(stack, jnp.concatenate(s0[0], axis=1))
        by_im = dot(stack, jnp.concatenate(s0[1], axis=1))
        pr = by_re[:2 * rows] - by_im[2 * rows:]
        pi = by_im[:2 * rows] + by_re[2 * rows:]
        size = rows + 2 * HALF
        own = slice(reach, reach + rows)
        parts = [
            join([(ops[0][2 * f + part][0][own], 0, -reach), (ops[0][2 * f + part][1][own], LANES - reach, -reach)])
            for part in range(2)
        ]
        parts = [jnp.where(narrow < size, part, 0.0) for part in parts]
        minus = -parts[1]
        near_ref[f, :, 0:LANES] = jnp.where(narrow < size, parts[0], roll(minus, size)).astype(BF)
        near_ref[f, :, LANES:] = jnp.where(narrow < 2 * size - LANES, roll(minus, size), 0.0).astype(BF)
        mids = [
            join([(g[rows:, :LANES], 0, -HALF), (g[rows:, LANES:], LANES - HALF, -HALF)]) for g in (pr, pi)
        ]
        mid_ref[f, :, 0:LANES] = mids[0].astype(BF)
        mid_ref[f, :, LANES:] = (-mids[1]).astype(BF)
        re, im = pr[:rows].astype(BF), pi[:rows].astype(BF)
        far_ref[f, 0] = jnp.concatenate([re, im], axis=0)
        far_ref[f, 1] = jnp.concatenate([-im, re], axis=0)
    for copy in copies:
        copy.wait()
    wt_ref[...] = jnp.zeros(wt_ref.shape, F32)
    wt_ref[0:DEPTHS, 0:weight_ref.shape[1]] = weight_ref[...]
    for t in range(tiles):
        bins = bins_ref[:, t * LANES:(t + 1) * LANES]
        for z in range(DEPTHS):
            row = jnp.broadcast_to(wt_ref[z:z + 1, :], (rows, LANES))
            pair_ref[z, t] = jnp.take_along_axis(row, bins, axis=1)


def windows(own, left, right, blocks):
    tiles, found = len(own), []
    for b in range(blocks):
        first = b * OUT - HALO
        j, s = divmod(first, LANES)
        pieces = []
        if b == 0:
            pieces = [(left[0], 0, left[1]), (own[0], HALO, HALO)]
        else:
            pieces.append((own[j], 0, -s))
            if s and j + 1 < tiles:
                pieces.append((own[j + 1], LANES - s, -s))
            end = tiles * LANES - first
            if end < LANES:
                pieces.append((right[0], end, end + right[1]))
        found.append(join(pieces))
    return found


def receiver_steps(first, w_ref, freqs, rows, keep):
    source = first
    blocks = len(first[0])
    for z in range(DEPTHS):
        after = [[None] * blocks for _ in range(2 * freqs)]
        for b in range(blocks):
            for f in range(freqs):
                both = jnp.concatenate([source[f][b], source[freqs + f][b]], axis=1)
                w = jnp.concatenate([w_ref[z, b, f, 0], w_ref[z, b, f, 1]], axis=1)
                got = dot(both, w, NT)
                for p, lanes in ((f, got[:, :OUT]), (freqs + f, got[:, LANES:LANES + OUT])):
                    after[p][b] = jnp.concatenate([lanes, jnp.zeros((rows, LANES - OUT), F32)], axis=1).astype(BF)
        if z < DEPTHS - 1:
            lane = lane_of((rows, LANES))
            source = [
                [
                    jnp.where(lane < OUT, plane[b], roll(plane[b + 1], OUT)) if b + 1 < blocks else plane[b]
                    for b in range(blocks)
                ]
                for plane in after
            ]
        else:
            source = after
        for p in range(2 * freqs):
            for b in range(blocks):
                keep(z, p, b, source[p][b])


def halo_sides(ra_ref, rb_ref, at, part):
    left, right = from_sides(ra_ref[at, :], rb_ref[at, :], "rec")
    left = jnp.where(has_left("rec"), left, jnp.zeros_like(left))
    right = jnp.where(has_right("rec"), right, jnp.zeros_like(right))
    return (left, HALO + part * MID), (right, -part * MID)


def own_kernel(x_ref, ra_ref, rb_ref, ridx_ref, table_ref, w_ref, a_ref, widx_ref):
    planes, rows, cols = x_ref.shape
    tiles = cols // LANES
    freqs = planes // 2
    blocks = w_ref.shape[1]
    table = table_ref[...]
    entries = table.shape[1]
    left, right = index_sides(ra_ref, rb_ref, freqs * rows, "rec")
    widx_ref[...] = jnp.zeros(widx_ref.shape, F32)
    widx_ref[0:DEPTHS, :] = ridx_ref[...].astype(F32)
    own = [widx_ref[:, t * LANES:(t + 1) * LANES] for t in range(tiles)]
    none = jnp.full((8, LANES), -1.0, F32)
    for z in range(DEPTHS):
        before = HALF * (DEPTHS - 1 - z)
        index = []
        for t in range(tiles + 1):
            pieces = []
            if before:
                pieces.append(((left, own[0])[min(t, 1)] if t < 2 else own[t - 1], 0, before))
            if t < tiles:
                pieces.append((own[t], before, before))
            else:
                if before:
                    pieces.append((right, before, before))
                pieces.append((none, 2 * before, 0))
            index.append(join(pieces)[z:z + 1])
        taps = taps_of(index, table, entries)
        for b in range(blocks):
            at = slice(b * OUT, (b + 1) * OUT)
            for f in range(freqs):
                re, im = (
                    skew(taps[at, part * LANES:(part + 1) * LANES]) for part in (2 * f, 2 * f + 1)
                )
                minus, re, im = (-im).astype(BF), re.astype(BF), im.astype(BF)
                for half, (top, low) in enumerate(((re, im), (minus, re))):
                    w_ref[z, b, f, half, 0:OUT, :] = top
                    w_ref[z, b, f, half, OUT:LANES, :] = jnp.zeros((LANES - OUT, LANES), BF)
                    w_ref[z, b, f, half, LANES:, :] = low
    first = []
    for p in range(planes):
        part, f = divmod(p, freqs)
        sides = halo_sides(ra_ref, rb_ref, slice(f * rows, (f + 1) * rows), part)
        first.append(windows([x_ref[p, :, t:t + LANES] for t in range(0, cols, LANES)], *sides, blocks))

    def keep(z, p, b, value):
        a_ref[z, p, b] = value

    receiver_steps(first, w_ref, freqs, rows, keep)


def image_kernel(
    ma_ref, mb_ref, sa_ref, sb_ref, ra_ref, rb_ref, w_ref, own_ref, near_ref, mid_ref, far_ref, pair_ref,
    send_ref, keep_ref, deep_ref, a_ref, part_ref,
):
    _, planes, blocks, rows, _ = own_ref.shape
    freqs = planes // 2
    tiles = pair_ref.shape[1]
    full = rows + 2 * HALO
    first = []
    for p in range(planes):
        part, f = divmod(p, freqs)
        at = slice(p * HALO, (p + 1) * HALO)
        parts = [(sa_ref[at, :], sb_ref[at, :])] + [(ma_ref[p, t], mb_ref[p, t]) for t in range(tiles - 1)]
        main = []
        for a, b in parts:
            left, right = from_sides(a, b, "src")
            left = jnp.where(has_left("src"), left, jnp.zeros_like(left))
            right = jnp.where(has_right("src"), right, jnp.zeros_like(right))
            main.append(jnp.concatenate([left, right], axis=0))
        ends, mixed = main[:2]
        lane = lane_of(ends.shape)
        main = [jnp.where(lane < MID, ends, mixed)] + main[2:] + [jnp.where(lane < MID, mixed, ends)]
        sides = []
        for cells, amount in halo_sides(ra_ref, rb_ref, slice(2 * f * HALO, 2 * (f + 1) * HALO), part):
            top = jnp.where(has_left("src"), cells[:HALO], jnp.zeros_like(cells[:HALO]))
            low = jnp.where(has_right("src"), cells[HALO:], jnp.zeros_like(cells[HALO:]))
            sides.append((jnp.concatenate([top, low], axis=0), amount))
        first.append(windows(main, *sides, blocks))

    def place(z, p, b):
        return deep_ref.at[p, b] if z == DEPTHS - 1 else a_ref.at[z, p, b]

    def keep(z, p, b, value):
        to = place(z, p, b)
        to[0:HALO] = value[:HALO]
        to[HALO:HALO + rows] = own_ref[z, p, b]
        to[HALO + rows:] = value[HALO:]

    receiver_steps(first, w_ref, freqs, 2 * HALO, keep)

    def field(z, p, b, reach):
        at = slice(HALO - reach, HALO + rows + reach)
        return jnp.concatenate([place(z, p, b)[at], place(z, p, b + 1)[at]], axis=1)

    images = []
    for z, ref in ((0, near_ref), (1, mid_ref)):
        reach = HALF * (z + 1)
        size = rows + 2 * reach
        out = []
        for b in range(0, blocks, 2):
            total = None
            for f in range(freqs):
                both = jnp.concatenate([field(z, f, b, reach), field(z, freqs + f, b, reach)], axis=0)
                term = dot(ref[f, :, 0:2 * size], both)
                total = term if total is None else total + term
            out += [total[:, :LANES], total[:, LANES:]]
        images.append([gather(out, t * LANES + HALF * (DEPTHS - 1 - z), LANES) for t in range(tiles)])
    real = [None] * blocks
    for b in range(0, blocks, 2):
        for f in range(freqs):
            got = dot(far_ref[f, 0][:rows, :full], field(2, f, b, HALO))
            got += dot(far_ref[f, 1][:rows, :full], field(2, freqs + f, b, HALO))
            got = got.astype(BF).astype(F32)
            for k in range(2):
                term = got[:, k * LANES:(k + 1) * LANES]
                real[b + k] = term if real[b + k] is None else real[b + k] + term
    real = [gather(real, t * LANES) for t in range(tiles)]
    for t in range(tiles):
        value = pair_ref[DEPTHS - 1, t] * real[t]
        for z in range(DEPTHS - 1):
            value += pair_ref[z, t] * images[z][t]
        part_ref[:, t * LANES:(t + 1) * LANES] = value
    count = lax.axis_size("freq")
    share = rows // count
    me = lax.axis_index("freq")
    keep_ref[...] = part_ref[pl.ds(pl.multiple_of(me * share, 8), share), :]
    for j in range(1, count):
        there = partner(me, j, count)
        send_ref[j - 1] = part_ref[pl.ds(pl.multiple_of(there * share, 8), share), :].astype(BF)


def final_kernel(deep_ref, far_ref, final_ref):
    planes, blocks, full, _ = deep_ref.shape
    _, rows, cols = final_ref.shape
    freqs = planes // 2
    for f in range(freqs):
        out = []
        for b in range(0, blocks, 2):
            parts = [jnp.concatenate([deep_ref[p, b], deep_ref[p, b + 1]], axis=1) for p in (f, freqs + f)]
            got = dot(far_ref[f, 0][:, :full], parts[0]) + dot(far_ref[f, 1][:, :full], parts[1])
            got = got.astype(BF)
            out += [got[:, :LANES], got[:, LANES:]]
        for t in range(0, cols, LANES):
            both = gather(out, t)
            final_ref[f, :, t:t + LANES] = both[:rows]
            final_ref[freqs + f, :, t:t + LANES] = both[rows:]


def partner(me, j, count):
    if count & (count - 1) == 0:
        return me ^ j
    return (me + j) % count


def local_call(kernel, outs, scratch=(), flops=0, moved=0, vmem=16, **others):
    return pl.pallas_call(
        kernel,
        out_shape=[jax.ShapeDtypeStruct(s, d) for s, d in outs],
        scratch_shapes=[pltpu.VMEM(*s) if isinstance(s, tuple) else s for s in scratch],
        **others,
        compiler_params=pltpu.CompilerParams(vmem_limit_bytes=vmem << 20),
        cost_estimate=pl.CostEstimate(flops=flops, bytes_accessed=moved, transcendentals=0),
    )


def migrate(wave, tap_table, src_index, rec_index, offset_bin, bin_weight):
    freqs, rows, cols = wave.shape[1:]
    planes = 2 * freqs
    tiles = cols // LANES
    entries = tap_table.shape[1]
    count = lax.axis_size("freq")
    share = rows // count
    full = rows + 2 * HALO
    blocks = -(-(cols + 2 * (HALO - HALF)) // OUT)

    main = ((planes, tiles - 1, HALO, LANES), BF)
    small = ((planes * HALO + IDX_ROWS, LANES), BF)
    inputs = (wave.reshape(planes, rows, cols), src_index, rec_index, jnp.transpose(tap_table, (0, 3, 2, 1)))
    inputs = tuple(pltpu.with_memory_space_constraint(a, pltpu.HBM) for a in inputs)
    sa, sb, x, src_index, rec_index, tap_table = local_call(
        load_kernel,
        [small, small] + [(a.shape, a.dtype) for a in inputs],
        [pltpu.SemaphoreType.DMA((len(inputs),))],
        moved=1 << 20,
        in_specs=[pl.BlockSpec(memory_space=pltpu.HBM)] * len(inputs),
    )(*inputs)
    sa, sb = swaps(sa, sb, "src")
    near = ((freqs * rows + IDX_ROWS, LANES), BF)
    ma, mb, ra, rb = local_call(pack_kernel, [main, main, near, near], moved=1 << 18)(x, rec_index)
    ma, mb = swaps(ma, mb, "src")
    ra, rb = swaps(ra, rb, "rec")
    edge = ((freqs * 2 * HALO, LANES), BF)
    ea, eb = local_call(edge_kernel, [edge, edge], moved=1 << 16)(sa, sb)
    ea, eb = swaps(ea, eb, "rec")

    late = tuple(pltpu.with_memory_space_constraint(a, pltpu.HBM) for a in (offset_bin, bin_weight))
    near, mid, far, pair, table = local_call(
        source_kernel,
        [
            ((freqs, rows, 2 * LANES), BF),
            ((freqs, rows, 2 * LANES), BF),
            ((freqs, 2, 2 * rows, 2 * LANES), BF),
            ((DEPTHS, tiles, rows, LANES), F32),
            ((planes * LANES, entries), BF),
        ],
        [((8, LANES), F32), ((8, LANES), F32)]
        + [(a.shape, a.dtype) for a in late]
        + [pltpu.SemaphoreType.DMA((len(late),))],
        flops=1 << 28,
        moved=2 << 20,
        in_specs=[pl.BlockSpec(memory_space=pltpu.VMEM)] * 4
        + [pl.BlockSpec(memory_space=pltpu.HBM)] * len(late),
    )(sa, sb, src_index, tap_table, *late)
    w, own = local_call(
        own_kernel,
        [
            ((DEPTHS, blocks, freqs, 2, WROWS, LANES), BF),
            ((DEPTHS, planes, blocks, rows, LANES), BF),
        ],
        [((8, cols), F32)],
        flops=1 << 31,
        moved=5 << 20,
    )(x, ra, rb, rec_index, table)
    send, keep, deep = local_call(
        image_kernel,
        [
            ((max(count - 1, 1), share, cols), BF),
            ((share, cols), F32),
            ((planes, blocks, full, LANES), BF),
        ],
        [((DEPTHS - 1, planes, blocks, full, LANES), BF), ((rows, cols), F32)],
        flops=1 << 31,
        moved=8 << 20,
        vmem=24,
    )(ma, mb, sa, sb, ea, eb, w, own, near, mid, far, pair)
    total = keep
    for j in range(1, count):
        got = lax.ppermute(send[j - 1], "freq", [(i, partner(i, j, count)) for i in range(count)])
        total = total + got.astype(F32)
    (final,) = local_call(final_kernel, [((planes, rows, cols), BF)], flops=1 << 28, moved=1 << 20)(deep, far)
    scale = 1.0 / math.sqrt(freqs * count * DEPTHS)
    return final.reshape(wave.shape), total * scale


def solution(mesh):
    placed = (
        P(None, "freq", "src", "rec"),
        P(None, None, "freq", None),
        P(None, "src"),
        P(None, "rec"),
        P("src", "rec"),
        P(),
    )
    return jax.shard_map(
        migrate,
        mesh=mesh,
        in_specs=placed,
        out_specs=(P(None, "freq", "src", "rec"), P(("src", "freq"), "rec")),
        check_vma=False,
    )
```

```python
import math

import jax
import jax.numpy as jnp
from jax import lax
from jax.experimental import pallas as pl
from jax.experimental.pallas import tpu as pltpu
from jax.sharding import PartitionSpec as P

TAPS = 33
DEPTHS = 3
HALF = TAPS // 2
HALO = DEPTHS * HALF
LANES = 128
MID = LANES // 2
OUT = LANES - 2 * HALF
WROWS = LANES + OUT
IDX_ROWS = 16
BF = jnp.bfloat16
F32 = jnp.float32
NT = (((1,), (1,)), ((), ()))
NN = (((1,), (0,)), ((), ()))
TT = (((0,), (1,)), ((), ()))


def dot(a, b, dims=NN):
    return lax.dot_general(a, b, dims, preferred_element_type=F32)


def pairs_of(axis, odd):
    count, groups = lax.axis_size(axis), lax.axis_size("freq")
    pairs, alone = [], list(range(count))
    for i in range(odd, count - 1, 2):
        alone.remove(i)
        alone.remove(i + 1)
        for g in range(groups):
            pairs += [(i * groups + g, (i + 1) * groups + g), ((i + 1) * groups + g, i * groups + g)]
    for i in alone:
        for g in range(0, groups - 1, 2):
            pairs += [(i * groups + g, i * groups + g + 1), (i * groups + g + 1, i * groups + g)]
    return pairs


def swaps(a, b, axis):
    a = lax.ppermute(a, (axis, "freq"), pairs_of(axis, 0))
    b = lax.ppermute(b, (axis, "freq"), pairs_of(axis, 1))
    return a, b


def is_even(axis):
    return lax.rem(lax.axis_index(axis), 2) == 0


def has_left(axis):
    return lax.axis_index(axis) > 0


def has_right(axis):
    return lax.axis_index(axis) < lax.axis_size(axis) - 1


def lane_of(shape):
    return lax.broadcasted_iota(jnp.int32, shape, len(shape) - 1)


def roll(cells, amount):
    amount = amount % LANES
    return pltpu.roll(cells, amount, 1) if amount else cells


def from_sides(a, b, axis):
    even = is_even(axis)
    return jnp.where(even, b, a), jnp.where(even, a, b)


def join(pieces):
    tile = None
    for cells, start, amount in pieces:
        moved = roll(cells, amount)
        tile = moved if start == 0 else jnp.where(lane_of(moved.shape) < start, tile, moved)
    return tile


def gather(blocks, first, valid=OUT):
    pieces, at = [], 0
    while at < LANES:
        k, lane = divmod(first + at, OUT)
        if k >= len(blocks):
            break
        pieces.append((blocks[k], at, at - lane))
        at += valid - lane
    return join(pieces)


def load_kernel(*refs):
    count, made = 6, 6
    sources, targets = refs[:count], refs[count + made:2 * count + made]
    ma_ref, mb_ref, sa_ref, sb_ref, ra_ref, rb_ref = refs[count:count + made]
    sem = refs[2 * count + made]
    copies = [pltpu.make_async_copy(s, t, sem.at[i]) for i, (s, t) in enumerate(zip(sources, targets))]
    for copy in copies:
        copy.start()
    x_ref, sidx_ref = targets[:2]
    planes, rows, cols = x_ref.shape
    even = is_even("src")
    low = rows - HALO
    at_a = pl.multiple_of(jnp.where(even, low, 0), 16)
    at_b = pl.multiple_of(jnp.where(even, 0, low), 16)
    lane = lane_of((HALO, LANES))
    base = planes * HALO
    copies[1].wait()
    index = sidx_ref[...].astype(F32).astype(BF)
    for small in (sa_ref, sb_ref):
        small[base:base + IDX_ROWS, :] = jnp.zeros((IDX_ROWS, LANES), BF)
        small[base:base + DEPTHS, 0:rows] = index
    copies[0].wait()
    for p in range(planes):
        for at, main, small in ((at_a, ma_ref, sa_ref), (at_b, mb_ref, sb_ref)):
            tiles = [x_ref[p, pl.ds(at, HALO), t:t + LANES] for t in range(0, cols, LANES)]
            main[p, 0] = jnp.where(lane < MID, tiles[-1], tiles[0])
            for t, tile in enumerate(tiles[1:-1]):
                main[p, t + 1] = tile
            small[p * HALO:(p + 1) * HALO, :] = jnp.where(lane < MID, tiles[0], tiles[-1])
    copies[2].wait()
    pack_edges(x_ref, targets[2], ra_ref, rb_ref)
    for copy in copies[3:]:
        copy.wait()


def put_edges(ends, at, tail, head):
    lane = lane_of(tail[0].shape)
    right = jnp.where(lane < MID, roll(tail[1], MID), tail[0])
    left = jnp.where(lane < MID, head[0], roll(head[1], MID))
    even = is_even("rec")
    place = slice(at, at + right.shape[0])
    ends[0][place, :] = jnp.where(even, right, left)
    ends[1][place, :] = jnp.where(even, left, right)


def pack_edges(x_ref, ridx_ref, ra_ref, rb_ref):
    planes, rows, cols = x_ref.shape
    freqs = planes // 2
    ends = (ra_ref, rb_ref)
    last = cols - LANES
    for f in range(freqs):
        tail = [x_ref[p, :, last:] for p in (f, freqs + f)]
        head = [x_ref[p, :, :LANES] for p in (f, freqs + f)]
        put_edges(ends, f * rows, tail, head)
    base = freqs * rows
    head = ridx_ref[:, :LANES].astype(F32).astype(BF)
    tail = ridx_ref[:, last:].astype(F32).astype(BF)
    even = is_even("rec")
    for ref, value in zip(ends, (jnp.where(even, tail, head), jnp.where(even, head, tail))):
        ref[base:base + IDX_ROWS, :] = jnp.zeros((IDX_ROWS, LANES), BF)
        ref[base:base + DEPTHS, :] = value


def edge_kernel(sa_ref, sb_ref, ra_ref, rb_ref):
    freqs = ra_ref.shape[0] // (2 * HALO)
    for f in range(freqs):
        for side in range(2):
            both = [side_of(sa_ref, sb_ref, p, side) for p in (f, freqs + f)]
            put_edges((ra_ref, rb_ref), (2 * f + side) * HALO, both, both)


def side_of(a_ref, b_ref, p, side):
    at = slice(p * HALO, (p + 1) * HALO)
    return from_sides(a_ref[at, :], b_ref[at, :], "src")[side]


def index_sides(a_ref, b_ref, base, axis):
    left, right = from_sides(a_ref[base:base + IDX_ROWS, :], b_ref[base:base + IDX_ROWS, :], axis)
    left = jnp.where(has_left(axis), left.astype(F32)[0:8], -1.0)
    right = jnp.where(has_right(axis), right.astype(F32)[0:8], -1.0)
    return left, right


def taps_of(index_tiles, table, entries):
    hot = [
        (lax.broadcasted_iota(jnp.int32, (entries, LANES), 0) == tile.astype(jnp.int32)).astype(F32).astype(BF)
        for tile in index_tiles
    ]
    return dot(hot[0] if len(hot) == 1 else jnp.concatenate(hot, axis=1), table, TT)


def skew(taps):
    return pltpu.roll(taps, 0, 1, stride=1, stride_axis=0)


def source_kernel(
    sa_ref, sb_ref, sidx_ref, taps_ref, bins_ref, weight_ref,
    near_ref, mid_ref, far_ref, pair_ref, table_ref, sx_ref, wt_ref,
):
    rows, cols = bins_ref.shape
    freqs = near_ref.shape[0]
    tiles = cols // LANES
    for f in range(freqs):
        for part in range(2):
            at = (2 * f + part) * LANES
            table_ref[at:at + LANES, :] = jnp.zeros((LANES, table_ref.shape[1]), BF)
            table_ref[at:at + TAPS, :] = taps_ref[part, :, f, :].astype(BF)
    table = table_ref[...]
    entries = table.shape[1]
    wt_ref[...] = jnp.zeros(wt_ref.shape, F32)
    wt_ref[0:DEPTHS, 0:weight_ref.shape[1]] = weight_ref[...]
    for t in range(tiles):
        bins = bins_ref[:, t * LANES:(t + 1) * LANES]
        for z in range(DEPTHS):
            row = jnp.broadcast_to(wt_ref[z:z + 1, :], (rows, LANES))
            pair_ref[z, t] = jnp.take_along_axis(row, bins, axis=1)
    left, right = index_sides(sa_ref, sb_ref, 2 * freqs * HALO, "src")
    sx_ref[...] = jnp.zeros(sx_ref.shape, F32)
    sx_ref[0:DEPTHS, 0:rows] = sidx_ref[...].astype(F32)
    reach = HALO - HALF
    index = join([(left, 0, reach - rows), (sx_ref[...], reach, reach), (right, reach + rows, reach + rows)])
    out = lax.broadcasted_iota(jnp.int32, (LANES, LANES), 0)
    lane = lane_of((LANES, LANES))
    ops = []
    for z in range(DEPTHS):
        taps = taps_of([roll(index, -z * HALF)[z:z + 1]], table, entries)
        found = []
        for part in range(2 * freqs):
            skewed = skew(taps[:, part * LANES:(part + 1) * LANES])
            found.append((jnp.where(lane >= out, skewed, 0.0), jnp.where(lane < out, skewed, 0.0)))
        ops.append(found)
    narrow = lane_of((rows, LANES))
    for f in range(freqs):
        s0 = [[tile.astype(BF) for tile in ops[0][2 * f + part]] for part in range(2)]
        s1 = [ops[1][2 * f + part][0].astype(BF) for part in range(2)]
        s2 = [ops[2][2 * f + part][0][:rows].astype(BF) for part in range(2)]
        got = dot(jnp.concatenate(s2, axis=0), jnp.concatenate(s1, axis=1))
        re = (got[:rows, :LANES] - got[rows:, LANES:]).astype(BF)
        im = (got[:rows, LANES:] + got[rows:, :LANES]).astype(BF)
        stack = jnp.concatenate([re, s1[0][HALF:HALF + rows], im, s1[1][HALF:HALF + rows]], axis=0)
        by_re = dot(stack, jnp.concatenate(s0[0], axis=1))
        by_im = dot(stack, jnp.concatenate(s0[1], axis=1))
        pr = by_re[:2 * rows] - by_im[2 * rows:]
        pi = by_im[:2 * rows] + by_re[2 * rows:]
        size = rows + 2 * HALF
        own = slice(reach, reach + rows)
        parts = [
            join([(ops[0][2 * f + part][0][own], 0, -reach), (ops[0][2 * f + part][1][own], LANES - reach, -reach)])
            for part in range(2)
        ]
        parts = [jnp.where(narrow < size, part, 0.0) for part in parts]
        minus = -parts[1]
        near_ref[f, :, 0:LANES] = jnp.where(narrow < size, parts[0], roll(minus, size)).astype(BF)
        near_ref[f, :, LANES:] = jnp.where(narrow < 2 * size - LANES, roll(minus, size), 0.0).astype(BF)
        mids = [
            join([(g[rows:, :LANES], 0, -HALF), (g[rows:, LANES:], LANES - HALF, -HALF)]) for g in (pr, pi)
        ]
        mid_ref[f, :, 0:LANES] = mids[0].astype(BF)
        mid_ref[f, :, LANES:] = (-mids[1]).astype(BF)
        re, im = pr[:rows].astype(BF), pi[:rows].astype(BF)
        far_ref[f, 0] = jnp.concatenate([re, im], axis=0)
        far_ref[f, 1] = jnp.concatenate([-im, re], axis=0)


def windows(own, left, right, blocks):
    tiles, found = len(own), []
    for b in range(blocks):
        first = b * OUT - HALO
        j, s = divmod(first, LANES)
        pieces = []
        if b == 0:
            pieces = [(left[0], 0, left[1]), (own[0], HALO, HALO)]
        else:
            pieces.append((own[j], 0, -s))
            if s and j + 1 < tiles:
                pieces.append((own[j + 1], LANES - s, -s))
            end = tiles * LANES - first
            if end < LANES:
                pieces.append((right[0], end, end + right[1]))
        found.append(join(pieces))
    return found


def receiver_steps(first, w_ref, freqs, rows, keep):
    source = first
    blocks = len(first[0])
    for z in range(DEPTHS):
        after = [[None] * blocks for _ in range(2 * freqs)]
        for b in range(blocks):
            for f in range(freqs):
                both = jnp.concatenate([source[f][b], source[freqs + f][b]], axis=1)
                w = jnp.concatenate([w_ref[z, b, f, 0], w_ref[z, b, f, 1]], axis=1)
                got = dot(both, w, NT)
                for p, lanes in ((f, got[:, :OUT]), (freqs + f, got[:, LANES:LANES + OUT])):
                    after[p][b] = jnp.concatenate([lanes, jnp.zeros((rows, LANES - OUT), F32)], axis=1).astype(BF)
        if z < DEPTHS - 1:
            lane = lane_of((rows, LANES))
            source = [
                [
                    jnp.where(lane < OUT, plane[b], roll(plane[b + 1], OUT)) if b + 1 < blocks else plane[b]
                    for b in range(blocks)
                ]
                for plane in after
            ]
        else:
            source = after
        for p in range(2 * freqs):
            for b in range(blocks):
                keep(z, p, b, source[p][b])


def halo_sides(ra_ref, rb_ref, at, part):
    left, right = from_sides(ra_ref[at, :], rb_ref[at, :], "rec")
    left = jnp.where(has_left("rec"), left, jnp.zeros_like(left))
    right = jnp.where(has_right("rec"), right, jnp.zeros_like(right))
    return (left, HALO + part * MID), (right, -part * MID)


def own_kernel(x_ref, ra_ref, rb_ref, ridx_ref, table_ref, w_ref, a_ref, widx_ref):
    planes, rows, cols = x_ref.shape
    tiles = cols // LANES
    freqs = planes // 2
    blocks = w_ref.shape[1]
    table = table_ref[...]
    entries = table.shape[1]
    left, right = index_sides(ra_ref, rb_ref, freqs * rows, "rec")
    widx_ref[...] = jnp.zeros(widx_ref.shape, F32)
    widx_ref[0:DEPTHS, :] = ridx_ref[...].astype(F32)
    own = [widx_ref[:, t * LANES:(t + 1) * LANES] for t in range(tiles)]
    none = jnp.full((8, LANES), -1.0, F32)
    for z in range(DEPTHS):
        before = HALF * (DEPTHS - 1 - z)
        index = []
        for t in range(tiles + 1):
            pieces = []
            if before:
                pieces.append(((left, own[0])[min(t, 1)] if t < 2 else own[t - 1], 0, before))
            if t < tiles:
                pieces.append((own[t], before, before))
            else:
                if before:
                    pieces.append((right, before, before))
                pieces.append((none, 2 * before, 0))
            index.append(join(pieces)[z:z + 1])
        taps = taps_of(index, table, entries)
        for b in range(blocks):
            at = slice(b * OUT, (b + 1) * OUT)
            for f in range(freqs):
                re, im = (
                    skew(taps[at, part * LANES:(part + 1) * LANES]) for part in (2 * f, 2 * f + 1)
                )
                minus, re, im = (-im).astype(BF), re.astype(BF), im.astype(BF)
                for half, (top, low) in enumerate(((re, im), (minus, re))):
                    w_ref[z, b, f, half, 0:OUT, :] = top
                    w_ref[z, b, f, half, OUT:LANES, :] = jnp.zeros((LANES - OUT, LANES), BF)
                    w_ref[z, b, f, half, LANES:, :] = low
    first = []
    for p in range(planes):
        part, f = divmod(p, freqs)
        sides = halo_sides(ra_ref, rb_ref, slice(f * rows, (f + 1) * rows), part)
        first.append(windows([x_ref[p, :, t:t + LANES] for t in range(0, cols, LANES)], *sides, blocks))

    def keep(z, p, b, value):
        a_ref[z, p, b] = value

    receiver_steps(first, w_ref, freqs, rows, keep)


def image_kernel(
    ma_ref, mb_ref, sa_ref, sb_ref, ra_ref, rb_ref, w_ref, own_ref, near_ref, mid_ref, far_ref, pair_ref,
    send_ref, keep_ref, deep_ref, a_ref, part_ref,
):
    _, planes, blocks, rows, _ = own_ref.shape
    freqs = planes // 2
    tiles = pair_ref.shape[1]
    full = rows + 2 * HALO
    first = []
    for p in range(planes):
        part, f = divmod(p, freqs)
        at = slice(p * HALO, (p + 1) * HALO)
        parts = [(sa_ref[at, :], sb_ref[at, :])] + [(ma_ref[p, t], mb_ref[p, t]) for t in range(tiles - 1)]
        main = []
        for a, b in parts:
            left, right = from_sides(a, b, "src")
            left = jnp.where(has_left("src"), left, jnp.zeros_like(left))
            right = jnp.where(has_right("src"), right, jnp.zeros_like(right))
            main.append(jnp.concatenate([left, right], axis=0))
        ends, mixed = main[:2]
        lane = lane_of(ends.shape)
        main = [jnp.where(lane < MID, ends, mixed)] + main[2:] + [jnp.where(lane < MID, mixed, ends)]
        sides = []
        for cells, amount in halo_sides(ra_ref, rb_ref, slice(2 * f * HALO, 2 * (f + 1) * HALO), part):
            top = jnp.where(has_left("src"), cells[:HALO], jnp.zeros_like(cells[:HALO]))
            low = jnp.where(has_right("src"), cells[HALO:], jnp.zeros_like(cells[HALO:]))
            sides.append((jnp.concatenate([top, low], axis=0), amount))
        first.append(windows(main, *sides, blocks))

    def place(z, p, b):
        return deep_ref.at[p, b] if z == DEPTHS - 1 else a_ref.at[z, p, b]

    def keep(z, p, b, value):
        to = place(z, p, b)
        to[0:HALO] = value[:HALO]
        to[HALO:HALO + rows] = own_ref[z, p, b]
        to[HALO + rows:] = value[HALO:]

    receiver_steps(first, w_ref, freqs, 2 * HALO, keep)

    def field(z, p, b, reach):
        at = slice(HALO - reach, HALO + rows + reach)
        return jnp.concatenate([place(z, p, b)[at], place(z, p, b + 1)[at]], axis=1)

    images = []
    for z, ref in ((0, near_ref), (1, mid_ref)):
        reach = HALF * (z + 1)
        size = rows + 2 * reach
        out = []
        for b in range(0, blocks, 2):
            total = None
            for f in range(freqs):
                both = jnp.concatenate([field(z, f, b, reach), field(z, freqs + f, b, reach)], axis=0)
                term = dot(ref[f, :, 0:2 * size], both)
                total = term if total is None else total + term
            out += [total[:, :LANES], total[:, LANES:]]
        images.append([gather(out, t * LANES + HALF * (DEPTHS - 1 - z), LANES) for t in range(tiles)])
    real = [None] * blocks
    for b in range(0, blocks, 2):
        for f in range(freqs):
            got = dot(far_ref[f, 0][:rows, :full], field(2, f, b, HALO))
            got += dot(far_ref[f, 1][:rows, :full], field(2, freqs + f, b, HALO))
            got = got.astype(BF).astype(F32)
            for k in range(2):
                term = got[:, k * LANES:(k + 1) * LANES]
                real[b + k] = term if real[b + k] is None else real[b + k] + term
    real = [gather(real, t * LANES) for t in range(tiles)]
    for t in range(tiles):
        value = pair_ref[DEPTHS - 1, t] * real[t]
        for z in range(DEPTHS - 1):
            value += pair_ref[z, t] * images[z][t]
        part_ref[:, t * LANES:(t + 1) * LANES] = value
    count = lax.axis_size("freq")
    share = rows // count
    me = lax.axis_index("freq")
    keep_ref[...] = part_ref[pl.ds(pl.multiple_of(me * share, 8), share), :]
    for j in range(1, count):
        there = partner(me, j, count)
        send_ref[j - 1] = part_ref[pl.ds(pl.multiple_of(there * share, 8), share), :].astype(BF)


def final_kernel(deep_ref, far_ref, final_ref):
    planes, blocks, full, _ = deep_ref.shape
    _, rows, cols = final_ref.shape
    freqs = planes // 2
    for f in range(freqs):
        out = []
        for b in range(0, blocks, 2):
            parts = [jnp.concatenate([deep_ref[p, b], deep_ref[p, b + 1]], axis=1) for p in (f, freqs + f)]
            got = dot(far_ref[f, 0][:, :full], parts[0]) + dot(far_ref[f, 1][:, :full], parts[1])
            got = got.astype(BF)
            out += [got[:, :LANES], got[:, LANES:]]
        for t in range(0, cols, LANES):
            both = gather(out, t)
            final_ref[f, :, t:t + LANES] = both[:rows]
            final_ref[freqs + f, :, t:t + LANES] = both[rows:]


def partner(me, j, count):
    if count & (count - 1) == 0:
        return me ^ j
    return (me + j) % count


def local_call(kernel, outs, scratch=(), flops=0, moved=0, vmem=16, **others):
    return pl.pallas_call(
        kernel,
        out_shape=[jax.ShapeDtypeStruct(s, d) for s, d in outs],
        scratch_shapes=[pltpu.VMEM(*s) if isinstance(s, tuple) else s for s in scratch],
        **others,
        compiler_params=pltpu.CompilerParams(vmem_limit_bytes=vmem << 20),
        cost_estimate=pl.CostEstimate(flops=flops, bytes_accessed=moved, transcendentals=0),
    )


def migrate(wave, tap_table, src_index, rec_index, offset_bin, bin_weight):
    freqs, rows, cols = wave.shape[1:]
    planes = 2 * freqs
    tiles = cols // LANES
    entries = tap_table.shape[1]
    count = lax.axis_size("freq")
    share = rows // count
    full = rows + 2 * HALO
    blocks = -(-(cols + 2 * (HALO - HALF)) // OUT)

    main = ((planes, tiles - 1, HALO, LANES), BF)
    small = ((planes * HALO + IDX_ROWS, LANES), BF)
    inputs = (wave.reshape(planes, rows, cols), src_index, rec_index, jnp.transpose(tap_table, (0, 3, 2, 1)), offset_bin, bin_weight)
    inputs = tuple(pltpu.with_memory_space_constraint(a, pltpu.HBM) for a in inputs)
    near = ((freqs * rows + IDX_ROWS, LANES), BF)
    ma, mb, sa, sb, ra, rb, x, src_index, rec_index, tap_table, offset_bin, bin_weight = local_call(
        load_kernel,
        [main, main, small, small, near, near] + [(a.shape, a.dtype) for a in inputs],
        [pltpu.SemaphoreType.DMA((len(inputs),))],
        moved=1 << 20,
        in_specs=[pl.BlockSpec(memory_space=pltpu.HBM)] * len(inputs),
    )(*inputs)
    sa, sb = swaps(sa, sb, "src")
    ma, mb = swaps(ma, mb, "src")
    ra, rb = swaps(ra, rb, "rec")
    edge = ((freqs * 2 * HALO, LANES), BF)
    ea, eb = local_call(edge_kernel, [edge, edge], moved=1 << 16)(sa, sb)
    ea, eb = swaps(ea, eb, "rec")

    near, mid, far, pair, table = local_call(
        source_kernel,
        [
            ((freqs, rows, 2 * LANES), BF),
            ((freqs, rows, 2 * LANES), BF),
            ((freqs, 2, 2 * rows, 2 * LANES), BF),
            ((DEPTHS, tiles, rows, LANES), F32),
            ((planes * LANES, entries), BF),
        ],
        [((8, LANES), F32), ((8, LANES), F32)],
        flops=1 << 28,
        moved=2 << 20,
    )(sa, sb, src_index, tap_table, offset_bin, bin_weight)
    w, own = local_call(
        own_kernel,
        [
            ((DEPTHS, blocks, freqs, 2, WROWS, LANES), BF),
            ((DEPTHS, planes, blocks, rows, LANES), BF),
        ],
        [((8, cols), F32)],
        flops=1 << 31,
        moved=5 << 20,
    )(x, ra, rb, rec_index, table)
    send, keep, deep = local_call(
        image_kernel,
        [
            ((max(count - 1, 1), share, cols), BF),
            ((share, cols), F32),
            ((planes, blocks, full, LANES), BF),
        ],
        [((DEPTHS - 1, planes, blocks, full, LANES), BF), ((rows, cols), F32)],
        flops=1 << 31,
        moved=8 << 20,
        vmem=24,
    )(ma, mb, sa, sb, ea, eb, w, own, near, mid, far, pair)
    total = keep
    for j in range(1, count):
        got = lax.ppermute(send[j - 1], "freq", [(i, partner(i, j, count)) for i in range(count)])
        total = total + got.astype(F32)
    (final,) = local_call(final_kernel, [((planes, rows, cols), BF)], flops=1 << 28, moved=1 << 20)(deep, far)
    scale = 1.0 / math.sqrt(freqs * count * DEPTHS)
    return final.reshape(wave.shape), total * scale


def solution(mesh):
    placed = (
        P(None, "freq", "src", "rec"),
        P(None, None, "freq", None),
        P(None, "src"),
        P(None, "rec"),
        P("src", "rec"),
        P(),
    )
    return jax.shard_map(
        migrate,
        mesh=mesh,
        in_specs=placed,
        out_specs=(P(None, "freq", "src", "rec"), P(("src", "freq"), "rec")),
        check_vma=False,
    )
```

```python
import math

import jax
import jax.numpy as jnp
from jax import lax
from jax.experimental import pallas as pl
from jax.experimental.pallas import tpu as pltpu
from jax.sharding import PartitionSpec as P

TAPS = 33
DEPTHS = 3
HALF = TAPS // 2
HALO = DEPTHS * HALF
LANES = 128
MID = LANES // 2
OUT = LANES - 2 * HALF
WROWS = LANES + OUT
IDX_ROWS = 16
BF = jnp.bfloat16
F32 = jnp.float32
NT = (((1,), (1,)), ((), ()))
NN = (((1,), (0,)), ((), ()))
TT = (((0,), (1,)), ((), ()))


def dot(a, b, dims=NN):
    return lax.dot_general(a, b, dims, preferred_element_type=F32)


def pairs_of(axis, odd):
    count, groups = lax.axis_size(axis), lax.axis_size("freq")
    pairs, alone = [], list(range(count))
    for i in range(odd, count - 1, 2):
        alone.remove(i)
        alone.remove(i + 1)
        for g in range(groups):
            pairs += [(i * groups + g, (i + 1) * groups + g), ((i + 1) * groups + g, i * groups + g)]
    for i in alone:
        for g in range(0, groups - 1, 2):
            pairs += [(i * groups + g, i * groups + g + 1), (i * groups + g + 1, i * groups + g)]
    return pairs


def swaps(a, b, axis):
    a = lax.ppermute(a, (axis, "freq"), pairs_of(axis, 0))
    b = lax.ppermute(b, (axis, "freq"), pairs_of(axis, 1))
    return a, b


def is_even(axis):
    return lax.rem(lax.axis_index(axis), 2) == 0


def has_left(axis):
    return lax.axis_index(axis) > 0


def has_right(axis):
    return lax.axis_index(axis) < lax.axis_size(axis) - 1


def lane_of(shape):
    return lax.broadcasted_iota(jnp.int32, shape, len(shape) - 1)


def roll(cells, amount):
    amount = amount % LANES
    return pltpu.roll(cells, amount, 1) if amount else cells


def from_sides(a, b, axis):
    even = is_even(axis)
    return jnp.where(even, b, a), jnp.where(even, a, b)


def join(pieces):
    tile = None
    for cells, start, amount in pieces:
        moved = roll(cells, amount)
        tile = moved if start == 0 else jnp.where(lane_of(moved.shape) < start, tile, moved)
    return tile


def gather(blocks, first, valid=OUT):
    pieces, at = [], 0
    while at < LANES:
        k, lane = divmod(first + at, OUT)
        if k >= len(blocks):
            break
        pieces.append((blocks[k], at, at - lane))
        at += valid - lane
    return join(pieces)


def load_kernel(*refs):
    count = 6
    sources, targets = refs[:count], refs[count + 4:2 * count + 4]
    ma_ref, mb_ref, sa_ref, sb_ref = refs[count:count + 4]
    sem = refs[2 * count + 4]
    copies = [pltpu.make_async_copy(s, t, sem.at[i]) for i, (s, t) in enumerate(zip(sources, targets))]
    for copy in copies:
        copy.start()
    x_ref, sidx_ref = targets[:2]
    planes, rows, cols = x_ref.shape
    even = is_even("src")
    low = rows - HALO
    at_a = pl.multiple_of(jnp.where(even, low, 0), 16)
    at_b = pl.multiple_of(jnp.where(even, 0, low), 16)
    lane = lane_of((HALO, LANES))
    base = planes * HALO
    copies[1].wait()
    index = sidx_ref[...].astype(F32).astype(BF)
    for small in (sa_ref, sb_ref):
        small[base:base + IDX_ROWS, :] = jnp.zeros((IDX_ROWS, LANES), BF)
        small[base:base + DEPTHS, 0:rows] = index
    copies[0].wait()
    for p in range(planes):
        for at, main, small in ((at_a, ma_ref, sa_ref), (at_b, mb_ref, sb_ref)):
            tiles = [x_ref[p, pl.ds(at, HALO), t:t + LANES] for t in range(0, cols, LANES)]
            main[p, 0] = jnp.where(lane < MID, tiles[-1], tiles[0])
            for t, tile in enumerate(tiles[1:-1]):
                main[p, t + 1] = tile
            small[p * HALO:(p + 1) * HALO, :] = jnp.where(lane < MID, tiles[0], tiles[-1])
    for copy in copies[2:]:
        copy.wait()


def put_edges(ends, at, tail, head):
    lane = lane_of(tail[0].shape)
    right = jnp.where(lane < MID, roll(tail[1], MID), tail[0])
    left = jnp.where(lane < MID, head[0], roll(head[1], MID))
    even = is_even("rec")
    place = slice(at, at + right.shape[0])
    ends[0][place, :] = jnp.where(even, right, left)
    ends[1][place, :] = jnp.where(even, left, right)


def near_kernel(x_ref, ridx_ref, ra_ref, rb_ref):
    planes, rows, cols = x_ref.shape
    freqs = planes // 2
    ends = (ra_ref, rb_ref)
    last = cols - LANES
    for f in range(freqs):
        tail = [x_ref[p, :, last:] for p in (f, freqs + f)]
        head = [x_ref[p, :, :LANES] for p in (f, freqs + f)]
        put_edges(ends, f * rows, tail, head)
    base = freqs * rows
    head = ridx_ref[:, :LANES].astype(F32).astype(BF)
    tail = ridx_ref[:, last:].astype(F32).astype(BF)
    even = is_even("rec")
    for ref, value in zip(ends, (jnp.where(even, tail, head), jnp.where(even, head, tail))):
        ref[base:base + IDX_ROWS, :] = jnp.zeros((IDX_ROWS, LANES), BF)
        ref[base:base + DEPTHS, :] = value


def edge_kernel(sa_ref, sb_ref, ra_ref, rb_ref):
    freqs = ra_ref.shape[0] // (2 * HALO)
    for f in range(freqs):
        for side in range(2):
            both = [side_of(sa_ref, sb_ref, p, side) for p in (f, freqs + f)]
            put_edges((ra_ref, rb_ref), (2 * f + side) * HALO, both, both)


def side_of(a_ref, b_ref, p, side):
    at = slice(p * HALO, (p + 1) * HALO)
    return from_sides(a_ref[at, :], b_ref[at, :], "src")[side]


def index_sides(a_ref, b_ref, base, axis):
    left, right = from_sides(a_ref[base:base + IDX_ROWS, :], b_ref[base:base + IDX_ROWS, :], axis)
    left = jnp.where(has_left(axis), left.astype(F32)[0:8], -1.0)
    right = jnp.where(has_right(axis), right.astype(F32)[0:8], -1.0)
    return left, right


def taps_of(index_tiles, table, entries):
    hot = [
        (lax.broadcasted_iota(jnp.int32, (entries, LANES), 0) == tile.astype(jnp.int32)).astype(F32).astype(BF)
        for tile in index_tiles
    ]
    return dot(hot[0] if len(hot) == 1 else jnp.concatenate(hot, axis=1), table, TT)


def skew(taps, f, part):
    tile = taps[:, f * LANES:(f + 1) * LANES]
    low = lane_of(tile.shape) < MID
    tile = jnp.where(low, 0.0, tile) if part else jnp.where(low, tile, 0.0)
    return pltpu.roll(tile, part * MID, 1, stride=1, stride_axis=0)


def source_kernel(
    sa_ref, sb_ref, sidx_ref, taps_ref, bins_ref, weight_ref,
    near_ref, mid_ref, far_ref, pair_ref, table_ref, sx_ref, wt_ref,
):
    rows, cols = bins_ref.shape
    freqs = near_ref.shape[0]
    tiles = cols // LANES
    for f in range(freqs):
        for part in range(2):
            at = f * LANES + part * MID
            table_ref[at:at + MID, :] = jnp.zeros((MID, table_ref.shape[1]), BF)
            table_ref[at:at + TAPS, :] = taps_ref[part, :, f, :].astype(BF)
    table = table_ref[...]
    entries = table.shape[1]
    wt_ref[...] = jnp.zeros(wt_ref.shape, F32)
    wt_ref[0:DEPTHS, 0:weight_ref.shape[1]] = weight_ref[...]
    for t in range(tiles):
        bins = bins_ref[:, t * LANES:(t + 1) * LANES]
        for z in range(DEPTHS):
            row = jnp.broadcast_to(wt_ref[z:z + 1, :], (rows, LANES))
            pair_ref[z, t] = jnp.take_along_axis(row, bins, axis=1)
    left, right = index_sides(sa_ref, sb_ref, 2 * freqs * HALO, "src")
    sx_ref[...] = jnp.zeros(sx_ref.shape, F32)
    sx_ref[0:DEPTHS, 0:rows] = sidx_ref[...].astype(F32)
    reach = HALO - HALF
    index = join([(left, 0, reach - rows), (sx_ref[...], reach, reach), (right, reach + rows, reach + rows)])
    out = lax.broadcasted_iota(jnp.int32, (LANES, LANES), 0)
    lane = lane_of((LANES, LANES))
    ops = []
    for z in range(DEPTHS):
        taps = taps_of([roll(index, -z * HALF)[z:z + 1]], table, entries)
        found = []
        for part in range(2 * freqs):
            skewed = skew(taps, part // 2, part % 2)
            found.append((jnp.where(lane >= out, skewed, 0.0), jnp.where(lane < out, skewed, 0.0)))
        ops.append(found)
    narrow = lane_of((rows, LANES))
    for f in range(freqs):
        s0 = [[tile.astype(BF) for tile in ops[0][2 * f + part]] for part in range(2)]
        s1 = [ops[1][2 * f + part][0].astype(BF) for part in range(2)]
        s2 = [ops[2][2 * f + part][0][:rows].astype(BF) for part in range(2)]
        got = dot(jnp.concatenate(s2, axis=0), jnp.concatenate(s1, axis=1))
        re = (got[:rows, :LANES] - got[rows:, LANES:]).astype(BF)
        im = (got[:rows, LANES:] + got[rows:, :LANES]).astype(BF)
        stack = jnp.concatenate([re, s1[0][HALF:HALF + rows], im, s1[1][HALF:HALF + rows]], axis=0)
        by_re = dot(stack, jnp.concatenate(s0[0], axis=1))
        by_im = dot(stack, jnp.concatenate(s0[1], axis=1))
        pr = by_re[:2 * rows] - by_im[2 * rows:]
        pi = by_im[:2 * rows] + by_re[2 * rows:]
        size = rows + 2 * HALF
        own = slice(reach, reach + rows)
        parts = [
            join([(ops[0][2 * f + part][0][own], 0, -reach), (ops[0][2 * f + part][1][own], LANES - reach, -reach)])
            for part in range(2)
        ]
        parts = [jnp.where(narrow < size, part, 0.0) for part in parts]
        minus = -parts[1]
        near_ref[f, :, 0:LANES] = jnp.where(narrow < size, parts[0], roll(minus, size)).astype(BF)
        near_ref[f, :, LANES:] = jnp.where(narrow < 2 * size - LANES, roll(minus, size), 0.0).astype(BF)
        mids = [
            join([(g[rows:, :LANES], 0, -HALF), (g[rows:, LANES:], LANES - HALF, -HALF)]) for g in (pr, pi)
        ]
        mid_ref[f, :, 0:LANES] = mids[0].astype(BF)
        mid_ref[f, :, LANES:] = (-mids[1]).astype(BF)
        re, im = pr[:rows].astype(BF), pi[:rows].astype(BF)
        far_ref[f, 0] = jnp.concatenate([re, im], axis=0)
        far_ref[f, 1] = jnp.concatenate([-im, re], axis=0)


def windows(own, left, right, blocks):
    tiles, found = len(own), []
    for b in range(blocks):
        first = b * OUT - HALO
        j, s = divmod(first, LANES)
        pieces = []
        if b == 0:
            pieces = [(left[0], 0, left[1]), (own[0], HALO, HALO)]
        else:
            pieces.append((own[j], 0, -s))
            if s and j + 1 < tiles:
                pieces.append((own[j + 1], LANES - s, -s))
            end = tiles * LANES - first
            if end < LANES:
                pieces.append((right[0], end, end + right[1]))
        found.append(join(pieces))
    return found


def receiver_steps(first, w_ref, freqs, rows, keep):
    source = first
    blocks = len(first[0])
    for z in range(DEPTHS):
        after = [[None] * blocks for _ in range(2 * freqs)]
        for b in range(blocks):
            for f in range(freqs):
                both = jnp.concatenate([source[f][b], source[freqs + f][b]], axis=1)
                w = jnp.concatenate([w_ref[z, b, f, 0], w_ref[z, b, f, 1]], axis=1)
                got = dot(both, w, NT)
                for p, lanes in ((f, got[:, :OUT]), (freqs + f, got[:, LANES:LANES + OUT])):
                    after[p][b] = jnp.concatenate([lanes, jnp.zeros((rows, LANES - OUT), F32)], axis=1).astype(BF)
        if z < DEPTHS - 1:
            lane = lane_of((rows, LANES))
            source = [
                [
                    jnp.where(lane < OUT, plane[b], roll(plane[b + 1], OUT)) if b + 1 < blocks else plane[b]
                    for b in range(blocks)
                ]
                for plane in after
            ]
        else:
            source = after
        for p in range(2 * freqs):
            for b in range(blocks):
                keep(z, p, b, source[p][b])


def halo_sides(ra_ref, rb_ref, at, part):
    left, right = from_sides(ra_ref[at, :], rb_ref[at, :], "rec")
    left = jnp.where(has_left("rec"), left, jnp.zeros_like(left))
    right = jnp.where(has_right("rec"), right, jnp.zeros_like(right))
    return (left, HALO + part * MID), (right, -part * MID)


def own_kernel(x_ref, ra_ref, rb_ref, ridx_ref, table_ref, w_ref, a_ref, widx_ref):
    planes, rows, cols = x_ref.shape
    tiles = cols // LANES
    freqs = planes // 2
    blocks = w_ref.shape[1]
    table = table_ref[...]
    entries = table.shape[1]
    left, right = index_sides(ra_ref, rb_ref, freqs * rows, "rec")
    widx_ref[...] = jnp.zeros(widx_ref.shape, F32)
    widx_ref[0:DEPTHS, :] = ridx_ref[...].astype(F32)
    own = [widx_ref[:, t * LANES:(t + 1) * LANES] for t in range(tiles)]
    none = jnp.full((8, LANES), -1.0, F32)
    for z in range(DEPTHS):
        before = HALF * (DEPTHS - 1 - z)
        index = []
        for t in range(tiles + 1):
            pieces = []
            if before:
                pieces.append(((left, own[0])[min(t, 1)] if t < 2 else own[t - 1], 0, before))
            if t < tiles:
                pieces.append((own[t], before, before))
            else:
                if before:
                    pieces.append((right, before, before))
                pieces.append((none, 2 * before, 0))
            index.append(join(pieces)[z:z + 1])
        taps = taps_of(index, table, entries)
        for b in range(blocks):
            valid = min(OUT, cols + 2 * before - b * OUT)
            at = slice(b * OUT, b * OUT + valid)
            for f in range(freqs):
                re, im = (skew(taps[at], f, part) for part in range(2))
                minus, re, im = (-im).astype(BF), re.astype(BF), im.astype(BF)
                for half, (top, low) in enumerate(((re, im), (minus, re))):
                    w_ref[z, b, f, half, 0:valid, :] = top
                    w_ref[z, b, f, half, valid:LANES, :] = jnp.zeros((LANES - valid, LANES), BF)
                    w_ref[z, b, f, half, LANES:LANES + valid, :] = low
                    if valid < OUT:
                        w_ref[z, b, f, half, LANES + valid:, :] = jnp.zeros((OUT - valid, LANES), BF)
    first = []
    for p in range(planes):
        part, f = divmod(p, freqs)
        sides = halo_sides(ra_ref, rb_ref, slice(f * rows, (f + 1) * rows), part)
        first.append(windows([x_ref[p, :, t:t + LANES] for t in range(0, cols, LANES)], *sides, blocks))

    def keep(z, p, b, value):
        a_ref[z, p, b] = value

    receiver_steps(first, w_ref, freqs, rows, keep)


def image_kernel(
    ma_ref, mb_ref, sa_ref, sb_ref, ra_ref, rb_ref, w_ref, own_ref, near_ref, mid_ref, far_ref, pair_ref,
    send_ref, keep_ref, deep_ref, a_ref, part_ref,
):
    _, planes, blocks, rows, _ = own_ref.shape
    freqs = planes // 2
    tiles = pair_ref.shape[1]
    full = rows + 2 * HALO
    first = []
    for p in range(planes):
        part, f = divmod(p, freqs)
        at = slice(p * HALO, (p + 1) * HALO)
        parts = [(sa_ref[at, :], sb_ref[at, :])] + [(ma_ref[p, t], mb_ref[p, t]) for t in range(tiles - 1)]
        main = []
        for a, b in parts:
            left, right = from_sides(a, b, "src")
            left = jnp.where(has_left("src"), left, jnp.zeros_like(left))
            right = jnp.where(has_right("src"), right, jnp.zeros_like(right))
            main.append(jnp.concatenate([left, right], axis=0))
        ends, mixed = main[:2]
        lane = lane_of(ends.shape)
        main = [jnp.where(lane < MID, ends, mixed)] + main[2:] + [jnp.where(lane < MID, mixed, ends)]
        sides = []
        for cells, amount in halo_sides(ra_ref, rb_ref, slice(2 * f * HALO, 2 * (f + 1) * HALO), part):
            top = jnp.where(has_left("src"), cells[:HALO], jnp.zeros_like(cells[:HALO]))
            low = jnp.where(has_right("src"), cells[HALO:], jnp.zeros_like(cells[HALO:]))
            sides.append((jnp.concatenate([top, low], axis=0), amount))
        first.append(windows(main, *sides, blocks))

    def place(z, p, b):
        return deep_ref.at[p, b] if z == DEPTHS - 1 else a_ref.at[z, p, b]

    def keep(z, p, b, value):
        to = place(z, p, b)
        to[0:HALO] = value[:HALO]
        to[HALO:HALO + rows] = own_ref[z, p, b]
        to[HALO + rows:] = value[HALO:]

    receiver_steps(first, w_ref, freqs, 2 * HALO, keep)

    def field(z, p, b, reach):
        at = slice(HALO - reach, HALO + rows + reach)
        return jnp.concatenate([place(z, p, b)[at], place(z, p, b + 1)[at]], axis=1)

    images = []
    for z, ref in ((0, near_ref), (1, mid_ref)):
        reach = HALF * (z + 1)
        size = rows + 2 * reach
        out = []
        for b in range(0, blocks, 2):
            total = None
            for f in range(freqs):
                both = jnp.concatenate([field(z, f, b, reach), field(z, freqs + f, b, reach)], axis=0)
                term = dot(ref[f, :, 0:2 * size], both)
                total = term if total is None else total + term
            out += [total[:, :LANES], total[:, LANES:]]
        images.append([gather(out, t * LANES + HALF * (DEPTHS - 1 - z), LANES) for t in range(tiles)])
    real = [None] * blocks
    for b in range(0, blocks, 2):
        for f in range(freqs):
            got = dot(far_ref[f, 0][:rows, :full], field(2, f, b, HALO))
            got += dot(far_ref[f, 1][:rows, :full], field(2, freqs + f, b, HALO))
            got = got.astype(BF).astype(F32)
            for k in range(2):
                term = got[:, k * LANES:(k + 1) * LANES]
                real[b + k] = term if real[b + k] is None else real[b + k] + term
    real = [gather(real, t * LANES) for t in range(tiles)]
    for t in range(tiles):
        value = pair_ref[DEPTHS - 1, t] * real[t]
        for z in range(DEPTHS - 1):
            value += pair_ref[z, t] * images[z][t]
        part_ref[:, t * LANES:(t + 1) * LANES] = value
    count = lax.axis_size("freq")
    share = rows // count
    me = lax.axis_index("freq")
    keep_ref[...] = part_ref[pl.ds(pl.multiple_of(me * share, 8), share), :]
    for j in range(1, count):
        there = partner(me, j, count)
        send_ref[j - 1] = part_ref[pl.ds(pl.multiple_of(there * share, 8), share), :].astype(BF)


def final_kernel(deep_ref, far_ref, final_ref):
    planes, blocks, full, _ = deep_ref.shape
    _, rows, cols = final_ref.shape
    freqs = planes // 2
    for f in range(freqs):
        out = []
        for b in range(0, blocks, 2):
            parts = [jnp.concatenate([deep_ref[p, b], deep_ref[p, b + 1]], axis=1) for p in (f, freqs + f)]
            got = dot(far_ref[f, 0][:, :full], parts[0]) + dot(far_ref[f, 1][:, :full], parts[1])
            got = got.astype(BF)
            out += [got[:, :LANES], got[:, LANES:]]
        for t in range(0, cols, LANES):
            both = gather(out, t)
            final_ref[f, :, t:t + LANES] = both[:rows]
            final_ref[freqs + f, :, t:t + LANES] = both[rows:]


def partner(me, j, count):
    if count & (count - 1) == 0:
        return me ^ j
    return (me + j) % count


def local_call(kernel, outs, scratch=(), flops=0, moved=0, vmem=16, **others):
    return pl.pallas_call(
        kernel,
        out_shape=[jax.ShapeDtypeStruct(s, d) for s, d in outs],
        scratch_shapes=[pltpu.VMEM(*s) if isinstance(s, tuple) else s for s in scratch],
        **others,
        compiler_params=pltpu.CompilerParams(vmem_limit_bytes=vmem << 20),
        cost_estimate=pl.CostEstimate(flops=flops, bytes_accessed=moved, transcendentals=0),
    )


def migrate(wave, tap_table, src_index, rec_index, offset_bin, bin_weight):
    freqs, rows, cols = wave.shape[1:]
    planes = 2 * freqs
    tiles = cols // LANES
    entries = tap_table.shape[1]
    count = lax.axis_size("freq")
    share = rows // count
    full = rows + 2 * HALO
    blocks = -(-(cols + 2 * (HALO - HALF)) // OUT)

    main = ((planes, tiles - 1, HALO, LANES), BF)
    small = ((planes * HALO + IDX_ROWS, LANES), BF)
    inputs = (wave.reshape(planes, rows, cols), src_index, rec_index, jnp.transpose(tap_table, (0, 3, 2, 1)), offset_bin, bin_weight)
    inputs = tuple(pltpu.with_memory_space_constraint(a, pltpu.HBM) for a in inputs)
    ma, mb, sa, sb, x, src_index, rec_index, tap_table, offset_bin, bin_weight = local_call(
        load_kernel,
        [main, main, small, small] + [(a.shape, a.dtype) for a in inputs],
        [pltpu.SemaphoreType.DMA((len(inputs),))],
        moved=1 << 20,
        in_specs=[pl.BlockSpec(memory_space=pltpu.HBM)] * len(inputs),
    )(*inputs)
    sa, sb = swaps(sa, sb, "src")
    ma, mb = swaps(ma, mb, "src")
    near = ((freqs * rows + IDX_ROWS, LANES), BF)
    ra, rb = local_call(near_kernel, [near, near], moved=1 << 16)(x, rec_index)
    ra, rb = swaps(ra, rb, "rec")
    edge = ((freqs * 2 * HALO, LANES), BF)
    ea, eb = local_call(edge_kernel, [edge, edge], moved=1 << 16)(sa, sb)
    ea, eb = swaps(ea, eb, "rec")

    near, mid, far, pair, table = local_call(
        source_kernel,
        [
            ((freqs, rows, 2 * LANES), BF),
            ((freqs, rows, 2 * LANES), BF),
            ((freqs, 2, 2 * rows, 2 * LANES), BF),
            ((DEPTHS, tiles, rows, LANES), F32),
            ((freqs * LANES, entries), BF),
        ],
        [((8, LANES), F32), ((8, LANES), F32)],
        flops=1 << 28,
        moved=2 << 20,
    )(sa, sb, src_index, tap_table, offset_bin, bin_weight)
    w, own = local_call(
        own_kernel,
        [
            ((DEPTHS, blocks, freqs, 2, WROWS, LANES), BF),
            ((DEPTHS, planes, blocks, rows, LANES), BF),
        ],
        [((8, cols), F32)],
        flops=1 << 31,
        moved=5 << 20,
    )(x, ra, rb, rec_index, table)
    send, keep, deep = local_call(
        image_kernel,
        [
            ((max(count - 1, 1), share, cols), BF),
            ((share, cols), F32),
            ((planes, blocks, full, LANES), BF),
        ],
        [((DEPTHS - 1, planes, blocks, full, LANES), BF), ((rows, cols), F32)],
        flops=1 << 31,
        moved=8 << 20,
        vmem=24,
    )(ma, mb, sa, sb, ea, eb, w, own, near, mid, far, pair)
    total = keep
    for j in range(1, count):
        got = lax.ppermute(send[j - 1], "freq", [(i, partner(i, j, count)) for i in range(count)])
        total = total + got.astype(F32)
    (final,) = local_call(final_kernel, [((planes, rows, cols), BF)], flops=1 << 28, moved=1 << 20)(deep, far)
    scale = 1.0 / math.sqrt(freqs * count * DEPTHS)
    return final.reshape(wave.shape), total * scale


def solution(mesh):
    placed = (
        P(None, "freq", "src", "rec"),
        P(None, None, "freq", None),
        P(None, "src"),
        P(None, "rec"),
        P("src", "rec"),
        P(),
    )
    return jax.shard_map(
        migrate,
        mesh=mesh,
        in_specs=placed,
        out_specs=(P(None, "freq", "src", "rec"), P(("src", "freq"), "rec")),
        check_vma=False,
    )
```
